128 devices in a mesh: lat: 32 (over y, z, core), lon: 4 (over x).
Axes of the slice: x: 4, y: 4, z: 4, core: 2. Of those that a mesh axis runs over, the one named last changes fastest.
Arguments:
- adjoint_state: float32 [4, 75, 256, 1024], P(None, None, 'lat', 'lon'), may hold values from -6 to 6
- mixing_base: float32 [74, 256, 1024], P(None, 'lat', 'lon'), may hold values from 0.05 to 5
- atm_flux: float32 [4, 512, 128], P(None, 'lat'), may hold values from -6 to 6
- send_count: int32 [32, 128], P('lat', 'lon'), may hold values from 0 to 2, as said below
- send_segment: int32 [32, 256], P('lat', 'lon'), may hold values from 0 to 15, as said below
- cover_index: int32 [4, 256, 1024], P(None, 'lat', 'lon'), may hold values from 0 to 8191, as said below
- cover_weight: float32 [4, 256, 1024], P(None, 'lat', 'lon'), may hold values from 0.1 to 1
- land_mask: int32 [256, 1024], P('lat', 'lon'), may hold values 0 or 1
Outputs:
- state_adjoint: float32 [4, 75, 256, 1024], P(None, None, 'lat', 'lon')
- flux_adjoint: float32 [4, 512, 128], P(None, 'lat')
The draws below stay inside these ranges and needn't reach their ends.
Inputs may be any that keep to these rules, and one draw needn't show every extreme that they name: `send_count`: for every longitude column one ocean latitude index receives 2 segments from every owner, and every ocean device receives at least one segment from the owner of its own latitude index. `send_segment`: for each owner and longitude column, the first entries list the segments for destination 0, then destination 1 and so on, as many as send_count gives; entries past their total are unused. `cover_index`: equals src * 2 * 128 + slot * 128 + lane, where slot is below the count that owner src sends to the cell's device in the cell's longitude column.
All inputs are finite; a program needn't handle non-finite values. No bound on the sum of `land_mask` on one device may be relied on, other than what follows from the above.
Results may differ from the reference program's by a relative error of at most 0.0003.
Values sent between devices are 32-bit elements; how exact they have to be, the bound alone decides.
A program may use at most 64 MiB of HBM per device.

```python
import math
import jax
import jax.numpy as jnp

NZ = 75
RY = 8
RX = 256
ASEG_DEV = 16
CAP = 2
K = 4
NY = 256
NX = 1024
ASEG = 512
N_LAT = 32
N_LON = 4


def route_table(key):
    first, second = jax.random.split(jax.random.fold_in(key, 7))
    counts = jax.random.randint(first, (N_LAT, N_LON, N_LAT), 0, CAP + 1)
    full = jax.random.randint(second, (N_LON,), 0, N_LAT)
    target = jnp.arange(N_LAT, dtype=jnp.int32)
    counts = jnp.where(target[None, None, :] == full[None, :, None], CAP, counts)
    owner = target[:, None, None] == target[None, None, :]
    counts = jnp.where(owner, jnp.maximum(counts, 1), counts)
    return counts.astype(jnp.int32)


def draw_send_count(key, part):
    return route_table(key).reshape(N_LAT, N_LON * N_LAT)


def draw_send_segment(key, part):
    return jax.random.randint(jax.random.fold_in(key, 11), (N_LAT, N_LON * N_LAT * CAP), 0, ASEG_DEV).astype(jnp.int32)


def draw_cover_index(key, part):
    counts = route_table(key)
    live_slot = jnp.arange(CAP, dtype=jnp.int32)[None, None, None, :] < jnp.transpose(counts, (2, 1, 0))[..., None]
    live_flat = live_slot.reshape(N_LAT, N_LON, N_LAT * CAP).astype(jnp.int32)
    number = jnp.sum(live_flat, axis=-1)
    order = jnp.argsort(1 - live_flat, axis=-1, stable=True).astype(jnp.int32)
    row_owner = jnp.arange(NY, dtype=jnp.int32) // RY
    col_owner = jnp.arange(NX, dtype=jnp.int32) // RX
    limit = number[row_owner[:, None], col_owner[None, :]]
    first, second = jax.random.split(jax.random.fold_in(key, 13))
    pick = jax.random.randint(first, (K, NY, NX), 0, limit[None, :, :])
    slot = order[row_owner[None, :, None], col_owner[None, None, :], pick]
    lane = jax.random.randint(second, (K, NY, NX), 0, 128)
    return (slot * 128 + lane).astype(jnp.int32)


def place_ends(entries, key, smallest, largest):
    index_at = [jax.random.randint(jax.random.fold_in(key, axis), (), 0, length) for axis, length in enumerate(entries.shape)]
    widest = entries.shape.index(max(entries.shape))
    neighbour = index_at[:widest] + [(index_at[widest] + 1) % entries.shape[widest]] + index_at[widest + 1:]
    return entries.at[tuple(index_at)].set(smallest).at[tuple(neighbour)].set(largest)


def block_levels(stream_key, dims, cuts, low, largest):
    level = 1.0
    for dim, shards_of in cuts:
        heights = jax.random.uniform(jax.random.fold_in(jax.random.fold_in(stream_key, 6), dim), (shards_of,), jnp.float32, low / len(cuts), largest / len(cuts))
        level = level * jnp.repeat(jnp.exp(heights), dims[dim] // shards_of).reshape((-1,) + (1,) * (len(dims) - 1 - dim))
    return level


def bell_draw(rng, extent, spread, most, pieces=(), kind=jnp.bfloat16):
    entries = spread * jax.random.normal(rng, extent, jnp.float32)
    if pieces:
        entries = entries * block_levels(rng, extent, pieces, -0.22, 0.18)
    return jnp.clip(entries, -most, most).astype(kind)


def setup_inputs(seed: int = 0) -> dict:
    streams_of = jax.random.split(jax.random.key(seed), 9)
    return {
        "adjoint_state": bell_draw(streams_of[0], (4, NZ, NY, NX), 1.0, 6.0, ((2, 32), (3, 4)), jnp.float32),
        "mixing_base": jnp.clip(jnp.exp(math.log(5.0) - 4.6051702 * jax.random.uniform(streams_of[1], (NZ - 1, NY, NX), jnp.float32) ** block_levels(streams_of[1], (NZ - 1, NY, NX), ((1, 32), (2, 4)), -0.2, 0.2)), 0.05, 5.0),
        "atm_flux": bell_draw(streams_of[2], (4, ASEG, 128), 1.0, 6.0, ((1, 32),), jnp.float32),
        "send_count": draw_send_count(jax.random.fold_in(streams_of[8], 71), 0),
        "send_segment": draw_send_segment(jax.random.fold_in(streams_of[8], 71), 0),
        "cover_index": draw_cover_index(jax.random.fold_in(streams_of[8], 71), 0),
        "cover_weight": jnp.clip(0.1 + 0.9 * jax.random.uniform(streams_of[6], (K, NY, NX), jnp.float32) ** block_levels(streams_of[6], (K, NY, NX), ((1, 32), (2, 4)), -0.2, 0.2), 0.1, 1.0),
        "land_mask": place_ends((jax.random.randint(streams_of[7], (NY, NX), 0, 5) < 4).astype(jnp.int32), jax.random.fold_in(streams_of[7], 1), 0, 1),
    }


SMOOTHING = 0.02
WIND_GAIN = 1.0
DEPTH_SCALE = 12.0
FIELD_MIX = (1.0, 1.0, 2.0, 2.0)


def laplace(values, marks):
    centre = values[..., 1:-1, 1:-1]
    north = marks[:-2, 1:-1] * (values[..., :-2, 1:-1] - centre)
    south = marks[2:, 1:-1] * (values[..., 2:, 1:-1] - centre)
    west = marks[1:-1, :-2] * (values[..., 1:-1, :-2] - centre)
    east = marks[1:-1, 2:] * (values[..., 1:-1, 2:] - centre)
    return marks[1:-1, 1:-1] * (((north + south) + west) + east)


def tridiagonal(source, mixing):
    gains = jnp.array(FIELD_MIX, dtype=jnp.float32)[:, None, None]
    coupling = [gains * plane for plane in mixing]
    levels = source.shape[1]
    ratios = []
    partial_value = []
    for level in range(levels):
        diagonal = jnp.ones_like(source[:, level])
        if level > 0:
            diagonal = diagonal + coupling[level - 1]
        if level < levels - 1:
            diagonal = diagonal + coupling[level]
        if level > 0:
            pivot = diagonal - coupling[level - 1] * ratios[level - 1]
            value = (source[:, level] + coupling[level - 1] * partial_value[level - 1]) / pivot
        else:
            pivot = diagonal
            value = source[:, level] / pivot
        partial_value.append(value)
        if level < levels - 1:
            ratios.append(coupling[level] / pivot)
    result = [partial_value[-1]]
    for level in range(levels - 2, -1, -1):
        result.append(partial_value[level] + ratios[level] * result[-1])
    return jnp.stack(result[::-1], axis=1)


def extend(values):
    widths = [(0, 0)] * (values.ndim - 2) + [(1, 1), (0, 0)]
    padded = jnp.pad(values, widths)
    return jnp.concatenate([padded[..., -1:], padded, padded[..., :1]], axis=-1)


def reference(adjoint_state, mixing_base, atm_flux, send_count, send_segment, cover_index, cover_weight, land_mask):
    counts = send_count.reshape(N_LAT, N_LON, N_LAT).astype(jnp.int32)
    starts = (jnp.cumsum(counts, axis=-1) - counts).astype(jnp.int32)
    column = jnp.arange(CAP, dtype=jnp.int32)
    places = jnp.minimum(starts[..., None] + column, N_LAT * CAP - 1).astype(jnp.int32)
    lists = send_segment.reshape(N_LAT, N_LON, N_LAT * CAP)
    chosen = jnp.take_along_axis(lists, places.reshape(N_LAT, N_LON, N_LAT * CAP), axis=-1)
    owner_base = (jnp.arange(N_LAT, dtype=jnp.int32) * ASEG_DEV)[:, None, None]
    source = (chosen + owner_base).reshape(N_LAT, N_LON, N_LAT, CAP)
    source = jnp.transpose(source, (1, 2, 0, 3)).reshape(N_LON, N_LAT, N_LAT * CAP).astype(jnp.int32)
    row_owner = (jnp.arange(NY, dtype=jnp.int32) // RY)[:, None]
    col_owner = (jnp.arange(NX, dtype=jnp.int32) // RX)[None, :]
    place = (128 * source[col_owner, row_owner, cover_index // 128] + cover_index % 128).astype(jnp.int32)
    flat_atm = atm_flux.reshape(4, -1)
    forcing = cover_weight[0] * flat_atm[:, place[0]]
    for item in range(1, K):
        forcing = forcing + cover_weight[item] * flat_atm[:, place[item]]
    surface = WIND_GAIN * (forcing[2] * forcing[2] + forcing[3] * forcing[3]) + jax.nn.softplus(forcing[1] - forcing[0])
    mixing = [mixing_base[level] + surface * math.exp(-level / DEPTH_SCALE) for level in range(NZ - 1)]
    land = land_mask.astype(jnp.float32)
    marks = extend(land)

    def smooth_once(values):
        inner = laplace(extend(values), marks)
        return values - SMOOTHING * laplace(extend(inner), marks)

    smoothed = smooth_once(smooth_once(adjoint_state))
    state_adjoint = tridiagonal(smoothed, mixing)
    flux_back = land * state_adjoint[:, 0]
    back = jnp.zeros((4, N_LAT * ASEG_DEV * 128), dtype=jnp.float32)
    for item in range(K):
        back = back.at[:, place[item]].add(cover_weight[item] * flux_back)
    return state_adjoint, back.reshape(4, N_LAT * ASEG_DEV, 128)
```

```python
import math

import jax
import jax.numpy as jnp
import numpy as np
from jax import lax
from jax.experimental import pallas as pl
from jax.experimental.pallas import tpu as pltpu
from jax.sharding import PartitionSpec as P

SMOOTHING = 0.02
WIND_GAIN = 1.0
DEPTH_SCALE = 12.0
FIELD_MIX = (1.0, 1.0, 2.0, 2.0)


def with_halo(block, sides, width):
    for axis, dim in sides:
        count = lax.axis_size(axis)
        forward = [(i, i + 1) for i in range(count - 1)]
        forward.append((count - 1, 0))
        backward = [(target, source) for source, target in forward]
        low = lax.ppermute(
            lax.slice_in_dim(block, block.shape[dim] - width, None, axis=dim), axis, forward
        )
        high = lax.ppermute(lax.slice_in_dim(block, 0, width, axis=dim), axis, backward)
        block = jnp.concatenate([low, block, high], axis=dim)
    return block


def laplace(values, marks):
    centre = values[..., 1:-1, 1:-1]
    north = marks[:-2, 1:-1] * (values[..., :-2, 1:-1] - centre)
    south = marks[2:, 1:-1] * (values[..., 2:, 1:-1] - centre)
    west = marks[1:-1, :-2] * (values[..., 1:-1, :-2] - centre)
    east = marks[1:-1, 2:] * (values[..., 1:-1, 2:] - centre)
    return marks[1:-1, 1:-1] * (north + south + west + east)


def tridiagonal_kernel(decay_ref, src_ref, base_ref, surf_ref, land_ref, out_ref, back_ref, ratio_ref):
    fields, levels = src_ref.shape[0], src_ref.shape[1]
    gains = sorted(set(FIELD_MIX))
    groups = [[f for f in range(fields) if FIELD_MIX[f] == g] for g in gains]
    surf = surf_ref[...]
    zero = jnp.zeros_like(surf)

    def step(level, below_mix, above_mix, ratios, parts):
        new_ratios, new_parts = [], list(parts)
        for gi, gain in enumerate(gains):
            below = gain * below_mix
            above = gain * above_mix
            pivot = ((1.0 + below) + above) - below * ratios[gi]
            if level is not None:
                ratio = above / pivot
                ratio_ref[gi, level] = ratio
                new_ratios.append(ratio)
            for f in groups[gi]:
                value = (src_ref[f, level if level is not None else levels - 1] + below * parts[f]) / pivot
                out_ref[f, level if level is not None else levels - 1] = value
                new_parts[f] = value
        return tuple(new_ratios), tuple(new_parts)

    def forward(level, carry):
        below_mix, ratios, parts = carry
        mix = base_ref[level] + surf * decay_ref[level]
        ratios, parts = step(level, below_mix, mix, ratios, parts)
        return (mix, ratios, parts)

    carry = (zero, tuple(zero for _ in gains), tuple(zero for _ in range(fields)))
    last_mix, ratios, parts = lax.fori_loop(0, levels - 1, forward, carry)
    step(None, last_mix, zero, ratios, parts)

    def backward(i, later):
        level = levels - 2 - i
        result = []
        for gi in range(len(gains)):
            ratio = ratio_ref[gi, level]
            for f in groups[gi]:
                value = out_ref[f, level] + ratio * later[f]
                out_ref[f, level] = value
                result.append((f, value))
        result.sort(key=lambda item: item[0])
        return tuple(v for _, v in result)

    final = tuple(out_ref[f, levels - 1] for f in range(fields))
    lax.fori_loop(0, levels - 1, backward, final)
    land = land_ref[...]
    for f in range(fields):
        back_ref[f] = land * out_ref[f, 0]


def tridiagonal(source, mixing_base, surface, land):
    fields, levels = source.shape[0], source.shape[1]
    decay_table = np.array(
        [math.exp(-level / DEPTH_SCALE) for level in range(levels)], dtype=np.float32
    )
    vmem = pltpu.MemorySpace.VMEM
    return pl.pallas_call(
        tridiagonal_kernel,
        out_shape=(
            jax.ShapeDtypeStruct(source.shape, jnp.float32),
            jax.ShapeDtypeStruct((fields,) + source.shape[2:], jnp.float32),
        ),
        in_specs=[pl.BlockSpec(memory_space=pltpu.MemorySpace.SMEM)]
        + [pl.BlockSpec(memory_space=vmem)] * 4,
        out_specs=(pl.BlockSpec(memory_space=vmem), pl.BlockSpec(memory_space=vmem)),
        scratch_shapes=[pltpu.VMEM((len(set(FIELD_MIX)), levels) + source.shape[2:], jnp.float32)],
    )(jnp.asarray(decay_table), source, mixing_base, surface, land)


def lat_edges(marks, width):
    lat_count = lax.axis_size("lat")
    where_lat = lax.axis_index("lat")
    rows = lax.broadcasted_iota(jnp.int32, marks.shape, 0)
    keep_top = jnp.logical_or(where_lat > 0, rows >= width)
    keep_bottom = jnp.logical_or(where_lat < lat_count - 1, rows < marks.shape[0] - width)
    return jnp.where(jnp.logical_and(keep_top, keep_bottom), marks, 0.0)


def single_rim(values):
    return with_halo(values, (("lat", 2), ("lon", 3)), 1)


def shards(
    adjoint_state,
    mixing_base,
    atm_flux,
    send_count,
    send_segment,
    cover_index,
    cover_weight,
    land_mask,
):
    lat_count = lax.axis_size("lat")
    owned = atm_flux.shape[1]
    counts = send_count[0]
    capacity = send_segment.shape[1] // lat_count
    starts = jnp.cumsum(counts) - counts
    column = jnp.arange(capacity, dtype=jnp.int32)
    places = jnp.minimum(starts[:, None] + column[None, :], send_segment.shape[1] - 1)
    chosen = send_segment[0][places]
    live_slot = column[None, :] < counts[:, None]
    whole = lax.all_gather(atm_flux, "lat", axis=1, tiled=True)
    global_ids = lax.axis_index("lat") * owned + chosen
    arrived = lax.all_to_all(global_ids, "lat", split_axis=0, concat_axis=0, tiled=True)
    received = whole[:, arrived, :]
    flat_recv = received.reshape(4, -1)
    picked = flat_recv[:, cover_index]
    forcing = cover_weight[0] * picked[:, 0]
    for item in range(1, cover_index.shape[0]):
        forcing = forcing + cover_weight[item] * picked[:, item]
    surface = WIND_GAIN * (forcing[2] * forcing[2] + forcing[3] * forcing[3]) + jax.nn.softplus(
        forcing[1] - forcing[0]
    )
    width = 1
    land = land_mask.astype(jnp.float32)
    coast_rim = with_halo(land_mask, (("lat", 0), ("lon", 1)), width)
    marks = lat_edges(coast_rim.astype(jnp.float32), width)
    smoothed = adjoint_state
    for turn in range(2):
        inner = laplace(single_rim(smoothed), marks)
        smoothed = smoothed - SMOOTHING * laplace(single_rim(inner), marks)
    state_adjoint, flux_back = tridiagonal(smoothed, mixing_base, surface, land)
    weighted = cover_weight[None] * flux_back[:, None]
    buffer = jnp.zeros_like(flat_recv).at[:, cover_index].add(weighted)
    returned = lax.all_to_all(
        buffer.reshape(received.shape), "lat", split_axis=1, concat_axis=1, tiled=True
    )
    kept = jnp.where(live_slot[None, :, :, None], returned, 0.0).reshape(4, -1, 128)
    owner_sum = jnp.zeros_like(atm_flux).at[:, chosen.reshape(-1), :].add(kept)
    flux_adjoint = lax.psum(owner_sum, "lon")
    return (state_adjoint, flux_adjoint)


def solution(mesh):
    in_specs = (
        P(None, None, "lat", "lon"),
        P(None, "lat", "lon"),
        P(None, "lat", None),
        P("lat", "lon"),
        P("lat", "lon"),
        P(None, "lat", "lon"),
        P(None, "lat", "lon"),
        P("lat", "lon"),
    )
    out_specs = (P(None, None, "lat", "lon"), P(None, "lat", None))
    return jax.shard_map(shards, mesh=mesh, in_specs=in_specs, out_specs=out_specs, check_vma=False)
```

```python
import math

import jax
import jax.numpy as jnp
import numpy as np
from jax import lax
from jax.experimental import pallas as pl
from jax.experimental.pallas import tpu as pltpu
from jax.sharding import PartitionSpec as P

SMOOTHING = 0.02
WIND_GAIN = 1.0
DEPTH_SCALE = 12.0
FIELD_MIX = (1.0, 1.0, 2.0, 2.0)


HALO = 4


def from_neighbours(block, axis, dim, width):
    count = lax.axis_size(axis)
    to_prev = [(i, (i - 1) % count) for i in range(count)]
    to_next = [(i, (i + 1) % count) for i in range(count)]
    size = block.shape[dim]
    from_next = lax.ppermute(lax.slice_in_dim(block, 0, width, axis=dim), axis, to_prev)
    from_prev = lax.ppermute(lax.slice_in_dim(block, size - width, size, axis=dim), axis, to_next)
    return from_next, from_prev


def extended_planes(values, land_mask, width):
    fields, levels, rows, cols = values.shape
    planes = values.reshape(fields * levels, rows, cols)
    coast = land_mask.astype(jnp.float32)[None]
    stack = jnp.concatenate([planes, coast], axis=0)
    south, north = from_neighbours(stack, "lat", 1, width)
    tall = jnp.concatenate([stack, south, north], axis=1)
    east, west = from_neighbours(tall, "lon", 2, width)
    wide = -(-(cols + 2 * width) // 128) * 128
    gap = jnp.zeros(tall.shape[:2] + (wide - cols - 2 * width,), jnp.float32)
    ext = jnp.concatenate([tall, east, gap, west], axis=2)
    lat_count = lax.axis_size("lat")
    where_lat = lax.axis_index("lat")
    row = lax.broadcasted_iota(jnp.int32, ext.shape[1:], 0)
    outside = jnp.logical_or(
        jnp.logical_and(where_lat == 0, row >= rows + width),
        jnp.logical_and(where_lat == lat_count - 1, jnp.logical_and(row >= rows, row < rows + width)),
    )
    mask = jnp.where(outside, 0.0, ext[-1])
    return ext, mask


def with_halo(block, sides, width):
    for axis, dim in sides:
        count = lax.axis_size(axis)
        forward = [(i, i + 1) for i in range(count - 1)]
        forward.append((count - 1, 0))
        backward = [(target, source) for source, target in forward]
        low = lax.ppermute(
            lax.slice_in_dim(block, block.shape[dim] - width, None, axis=dim), axis, forward
        )
        high = lax.ppermute(lax.slice_in_dim(block, 0, width, axis=dim), axis, backward)
        block = jnp.concatenate([low, block, high], axis=dim)
    return block


def laplace(values, marks):
    centre = values[..., 1:-1, 1:-1]
    north = marks[:-2, 1:-1] * (values[..., :-2, 1:-1] - centre)
    south = marks[2:, 1:-1] * (values[..., 2:, 1:-1] - centre)
    west = marks[1:-1, :-2] * (values[..., 1:-1, :-2] - centre)
    east = marks[1:-1, 2:] * (values[..., 1:-1, 2:] - centre)
    return marks[1:-1, 1:-1] * (north + south + west + east)


def tridiagonal_kernel(
    decay_ref, ext_ref, mask_ref, base_ref, surf_ref, land_ref, out_ref, back_ref, ratio_ref, marks_ref
):
    fields, levels = out_ref.shape[0], out_ref.shape[1]
    rows, cols = out_ref.shape[2], out_ref.shape[3]
    tall, wide = mask_ref.shape
    marks = mask_ref[...]
    marks_ref[0] = marks
    marks_ref[1] = pltpu.roll(marks, 1, 0)
    marks_ref[2] = pltpu.roll(marks, tall - 1, 0)
    marks_ref[3] = pltpu.roll(marks, 1, 1)
    marks_ref[4] = pltpu.roll(marks, wide - 1, 1)

    def laplace_ext(values):
        north = marks_ref[1] * (pltpu.roll(values, 1, 0) - values)
        south = marks_ref[2] * (pltpu.roll(values, tall - 1, 0) - values)
        west = marks_ref[3] * (pltpu.roll(values, 1, 1) - values)
        east = marks_ref[4] * (pltpu.roll(values, wide - 1, 1) - values)
        return marks_ref[0] * (((north + south) + west) + east)

    def smoothed(f, level):
        values = ext_ref[f * levels + level]
        for turn in range(2):
            inner = laplace_ext(values)
            values = values - SMOOTHING * laplace_ext(inner)
        return values[:rows, :cols]

    gains = sorted(set(FIELD_MIX))
    groups = [[f for f in range(fields) if FIELD_MIX[f] == g] for g in gains]
    surf = surf_ref[...]
    zero = jnp.zeros_like(surf)

    def step(level, below_mix, above_mix, ratios, parts):
        new_ratios, new_parts = [], list(parts)
        for gi, gain in enumerate(gains):
            below = gain * below_mix
            above = gain * above_mix
            pivot = ((1.0 + below) + above) - below * ratios[gi]
            if level is not None:
                ratio = above / pivot
                ratio_ref[gi, level] = ratio
                new_ratios.append(ratio)
            for f in groups[gi]:
                value = (smoothed(f, level if level is not None else levels - 1) + below * parts[f]) / pivot
                out_ref[f, level if level is not None else levels - 1] = value
                new_parts[f] = value
        return tuple(new_ratios), tuple(new_parts)

    def forward(level, carry):
        below_mix, ratios, parts = carry
        mix = base_ref[level] + surf * decay_ref[level]
        ratios, parts = step(level, below_mix, mix, ratios, parts)
        return (mix, ratios, parts)

    carry = (zero, tuple(zero for _ in gains), tuple(zero for _ in range(fields)))
    last_mix, ratios, parts = lax.fori_loop(0, levels - 1, forward, carry)
    step(None, last_mix, zero, ratios, parts)

    def backward(i, later):
        level = levels - 2 - i
        result = []
        for gi in range(len(gains)):
            ratio = ratio_ref[gi, level]
            for f in groups[gi]:
                value = out_ref[f, level] + ratio * later[f]
                out_ref[f, level] = value
                result.append((f, value))
        result.sort(key=lambda item: item[0])
        return tuple(v for _, v in result)

    final = tuple(out_ref[f, levels - 1] for f in range(fields))
    lax.fori_loop(0, levels - 1, backward, final)
    land = land_ref[...]
    for f in range(fields):
        back_ref[f] = land * out_ref[f, 0]


def tridiagonal(ext, mask, shape, mixing_base, surface, land):
    fields, levels = shape[0], shape[1]
    decay_table = np.array(
        [math.exp(-level / DEPTH_SCALE) for level in range(levels)], dtype=np.float32
    )
    vmem = pltpu.MemorySpace.VMEM
    return pl.pallas_call(
        tridiagonal_kernel,
        out_shape=(
            jax.ShapeDtypeStruct(shape, jnp.float32),
            jax.ShapeDtypeStruct((fields,) + shape[2:], jnp.float32),
        ),
        in_specs=[pl.BlockSpec(memory_space=pltpu.MemorySpace.SMEM)]
        + [pl.BlockSpec(memory_space=vmem)] * 5,
        out_specs=(pl.BlockSpec(memory_space=vmem), pl.BlockSpec(memory_space=vmem)),
        scratch_shapes=[
            pltpu.VMEM((len(set(FIELD_MIX)), levels) + shape[2:], jnp.float32),
            pltpu.VMEM((5,) + mask.shape, jnp.float32),
        ],
    )(jnp.asarray(decay_table), ext, mask, mixing_base, surface, land)


def lat_edges(marks, width):
    lat_count = lax.axis_size("lat")
    where_lat = lax.axis_index("lat")
    rows = lax.broadcasted_iota(jnp.int32, marks.shape, 0)
    keep_top = jnp.logical_or(where_lat > 0, rows >= width)
    keep_bottom = jnp.logical_or(where_lat < lat_count - 1, rows < marks.shape[0] - width)
    return jnp.where(jnp.logical_and(keep_top, keep_bottom), marks, 0.0)


def single_rim(values):
    return with_halo(values, (("lat", 2), ("lon", 3)), 1)


def shards(
    adjoint_state,
    mixing_base,
    atm_flux,
    send_count,
    send_segment,
    cover_index,
    cover_weight,
    land_mask,
):
    lat_count = lax.axis_size("lat")
    owned = atm_flux.shape[1]
    counts = send_count[0]
    capacity = send_segment.shape[1] // lat_count
    starts = jnp.cumsum(counts) - counts
    column = jnp.arange(capacity, dtype=jnp.int32)
    places = jnp.minimum(starts[:, None] + column[None, :], send_segment.shape[1] - 1)
    chosen = send_segment[0][places]
    live_slot = column[None, :] < counts[:, None]
    whole = lax.all_gather(atm_flux, "lat", axis=1, tiled=True)
    global_ids = lax.axis_index("lat") * owned + chosen
    arrived = lax.all_to_all(global_ids, "lat", split_axis=0, concat_axis=0, tiled=True)
    received = whole[:, arrived, :]
    flat_recv = received.reshape(4, -1)
    picked = flat_recv[:, cover_index]
    forcing = cover_weight[0] * picked[:, 0]
    for item in range(1, cover_index.shape[0]):
        forcing = forcing + cover_weight[item] * picked[:, item]
    surface = WIND_GAIN * (forcing[2] * forcing[2] + forcing[3] * forcing[3]) + jax.nn.softplus(
        forcing[1] - forcing[0]
    )
    land = land_mask.astype(jnp.float32)
    ext, mask = extended_planes(adjoint_state, land_mask, HALO)
    state_adjoint, flux_back = tridiagonal(ext, mask, adjoint_state.shape, mixing_base, surface, land)
    weighted = cover_weight[None] * flux_back[:, None]
    buffer = jnp.zeros_like(flat_recv).at[:, cover_index].add(weighted)
    returned = lax.all_to_all(
        buffer.reshape(received.shape), "lat", split_axis=1, concat_axis=1, tiled=True
    )
    kept = jnp.where(live_slot[None, :, :, None], returned, 0.0).reshape(4, -1, 128)
    owner_sum = jnp.zeros_like(atm_flux).at[:, chosen.reshape(-1), :].add(kept)
    flux_adjoint = lax.psum(owner_sum, "lon")
    return (state_adjoint, flux_adjoint)


def solution(mesh):
    in_specs = (
        P(None, None, "lat", "lon"),
        P(None, "lat", "lon"),
        P(None, "lat", None),
        P("lat", "lon"),
        P("lat", "lon"),
        P(None, "lat", "lon"),
        P(None, "lat", "lon"),
        P("lat", "lon"),
    )
    out_specs = (P(None, None, "lat", "lon"), P(None, "lat", None))
    return jax.shard_map(shards, mesh=mesh, in_specs=in_specs, out_specs=out_specs, check_vma=False)
```

```python
import math

import jax
import jax.numpy as jnp
import numpy as np
from jax import lax
from jax.experimental import pallas as pl
from jax.experimental.pallas import tpu as pltpu
from jax.sharding import PartitionSpec as P

SMOOTHING = 0.02
WIND_GAIN = 1.0
DEPTH_SCALE = 12.0
FIELD_MIX = (1.0, 1.0, 2.0, 2.0)


HALO = 4


def from_neighbours(block, axis, dim, width):
    count = lax.axis_size(axis)
    to_prev = [(i, (i - 1) % count) for i in range(count)]
    to_next = [(i, (i + 1) % count) for i in range(count)]
    size = block.shape[dim]
    from_next = lax.ppermute(lax.slice_in_dim(block, 0, width, axis=dim), axis, to_prev)
    from_prev = lax.ppermute(lax.slice_in_dim(block, size - width, size, axis=dim), axis, to_next)
    return from_next, from_prev


def extended_planes(values, land_mask, width):
    fields, levels, rows, cols = values.shape
    planes = values.reshape(fields * levels, rows, cols)
    coast = land_mask.astype(jnp.float32)[None]
    stack = jnp.concatenate([planes, coast], axis=0)
    south, north = from_neighbours(stack, "lat", 1, width)
    tall = jnp.concatenate([stack, south, north], axis=1)
    east, west = from_neighbours(tall, "lon", 2, width)
    wide = -(-(cols + 2 * width) // 128) * 128
    gap = jnp.zeros(tall.shape[:2] + (wide - cols - 2 * width,), jnp.float32)
    ext = jnp.concatenate([tall, east, gap, west], axis=2)
    lat_count = lax.axis_size("lat")
    where_lat = lax.axis_index("lat")
    row = lax.broadcasted_iota(jnp.int32, ext.shape[1:], 0)
    outside = jnp.logical_or(
        jnp.logical_and(where_lat == 0, row >= rows + width),
        jnp.logical_and(where_lat == lat_count - 1, jnp.logical_and(row >= rows, row < rows + width)),
    )
    mask = jnp.where(outside, 0.0, ext[-1])
    return ext, mask


def with_halo(block, sides, width):
    for axis, dim in sides:
        count = lax.axis_size(axis)
        forward = [(i, i + 1) for i in range(count - 1)]
        forward.append((count - 1, 0))
        backward = [(target, source) for source, target in forward]
        low = lax.ppermute(
            lax.slice_in_dim(block, block.shape[dim] - width, None, axis=dim), axis, forward
        )
        high = lax.ppermute(lax.slice_in_dim(block, 0, width, axis=dim), axis, backward)
        block = jnp.concatenate([low, block, high], axis=dim)
    return block


def laplace(values, marks):
    centre = values[..., 1:-1, 1:-1]
    north = marks[:-2, 1:-1] * (values[..., :-2, 1:-1] - centre)
    south = marks[2:, 1:-1] * (values[..., 2:, 1:-1] - centre)
    west = marks[1:-1, :-2] * (values[..., 1:-1, :-2] - centre)
    east = marks[1:-1, 2:] * (values[..., 1:-1, 2:] - centre)
    return marks[1:-1, 1:-1] * (north + south + west + east)


def tridiagonal_kernel(
    decay_ref, ext_ref, mask_ref, base_ref, surf_ref, land_ref, out_ref, back_ref, ratio_ref, marks_ref
):
    fields, levels = out_ref.shape[0], out_ref.shape[1]
    rows, cols = out_ref.shape[2], out_ref.shape[3]
    tall, wide = mask_ref.shape
    marks = mask_ref[...]
    marks_ref[0] = marks
    marks_ref[1] = pltpu.roll(marks, 1, 0)
    marks_ref[2] = pltpu.roll(marks, tall - 1, 0)
    marks_ref[3] = pltpu.roll(marks, 1, 1)
    marks_ref[4] = pltpu.roll(marks, wide - 1, 1)

    def laplace_ext(values):
        north = marks_ref[1] * (pltpu.roll(values, 1, 0) - values)
        south = marks_ref[2] * (pltpu.roll(values, tall - 1, 0) - values)
        west = marks_ref[3] * (pltpu.roll(values, 1, 1) - values)
        east = marks_ref[4] * (pltpu.roll(values, wide - 1, 1) - values)
        return marks_ref[0] * (((north + south) + west) + east)

    def smoothed(f, level):
        values = ext_ref[f * levels + level]
        for turn in range(2):
            inner = laplace_ext(values)
            values = values - SMOOTHING * laplace_ext(inner)
        return values[:rows, :cols]

    gains = sorted(set(FIELD_MIX))
    groups = [[f for f in range(fields) if FIELD_MIX[f] == g] for g in gains]
    surf = surf_ref[...]
    zero = jnp.zeros_like(surf)

    def step(level, below_mix, above_mix, ratios, parts):
        new_ratios, new_parts = [], list(parts)
        for gi, gain in enumerate(gains):
            below = gain * below_mix
            above = gain * above_mix
            pivot = ((1.0 + below) + above) - below * ratios[gi]
            if level is not None:
                ratio = above / pivot
                ratio_ref[gi, level] = ratio
                new_ratios.append(ratio)
            for f in groups[gi]:
                value = (smoothed(f, level if level is not None else levels - 1) + below * parts[f]) / pivot
                out_ref[f, level if level is not None else levels - 1] = value
                new_parts[f] = value
        return tuple(new_ratios), tuple(new_parts)

    def forward(level, carry):
        below_mix, ratios, parts = carry
        mix = base_ref[level] + surf * decay_ref[level]
        ratios, parts = step(level, below_mix, mix, ratios, parts)
        return (mix, ratios, parts)

    carry = (zero, tuple(zero for _ in gains), tuple(zero for _ in range(fields)))
    last_mix, ratios, parts = lax.fori_loop(0, levels - 1, forward, carry)
    step(None, last_mix, zero, ratios, parts)

    def backward(i, later):
        level = levels - 2 - i
        result = []
        for gi in range(len(gains)):
            ratio = ratio_ref[gi, level]
            for f in groups[gi]:
                value = out_ref[f, level] + ratio * later[f]
                out_ref[f, level] = value
                result.append((f, value))
        result.sort(key=lambda item: item[0])
        return tuple(v for _, v in result)

    final = tuple(out_ref[f, levels - 1] for f in range(fields))
    lax.fori_loop(0, levels - 1, backward, final)
    land = land_ref[...]
    for f in range(fields):
        back_ref[f] = land * out_ref[f, 0]


def tridiagonal(ext, mask, shape, mixing_base, surface, land):
    fields, levels = shape[0], shape[1]
    decay_table = np.array(
        [math.exp(-level / DEPTH_SCALE) for level in range(levels)], dtype=np.float32
    )
    vmem = pltpu.MemorySpace.VMEM
    return pl.pallas_call(
        tridiagonal_kernel,
        out_shape=(
            jax.ShapeDtypeStruct(shape, jnp.float32),
            jax.ShapeDtypeStruct((fields,) + shape[2:], jnp.float32),
        ),
        in_specs=[pl.BlockSpec(memory_space=pltpu.MemorySpace.SMEM)]
        + [pl.BlockSpec(memory_space=vmem)] * 5,
        out_specs=(pl.BlockSpec(memory_space=vmem), pl.BlockSpec(memory_space=vmem)),
        scratch_shapes=[
            pltpu.VMEM((len(set(FIELD_MIX)), levels) + shape[2:], jnp.float32),
            pltpu.VMEM((5,) + mask.shape, jnp.float32),
        ],
    )(jnp.asarray(decay_table), ext, mask, mixing_base, surface, land)


def split_three(values):
    high = values.astype(jnp.bfloat16)
    rest = values - high.astype(jnp.float32)
    middle = rest.astype(jnp.bfloat16)
    low = (rest - middle.astype(jnp.float32)).astype(jnp.bfloat16)
    return high, middle, low


def matmul_exact(parts, other, contract):
    numbers = (((1,), (contract,)), ((), ()))
    total = None
    for part in parts:
        product = lax.dot_general(part, other, numbers, preferred_element_type=jnp.float32)
        total = product if total is None else total + product
    return total


def gather_kernel(recv_ref, index_ref, weight_ref, out_ref):
    stacked, lanes = recv_ref.shape
    fields, rows, cols = out_ref.shape
    segments = stacked // fields
    items = index_ref.shape[0] // rows
    parts = split_three(recv_ref[...])
    lane_iota = lax.broadcasted_iota(jnp.int32, (lanes, cols), 0)
    segment_iota = lax.broadcasted_iota(jnp.int32, (fields, segments, cols), 1)

    def row_step(y, carry):
        total = None
        for item in range(items):
            index = index_ref[pl.ds(item * rows + y, 1), :]
            onehot = (lane_iota == index % lanes).astype(jnp.bfloat16)
            chosen = matmul_exact(parts, onehot, 0).reshape(fields, segments, cols)
            hit = segment_iota == (index // lanes)[None]
            picked = jnp.sum(jnp.where(hit, chosen, 0.0), axis=1)
            term = weight_ref[pl.ds(item * rows + y, 1), :] * picked
            total = term if total is None else total + term
        out_ref[:, pl.ds(y, 1), :] = total[:, None, :]
        return carry

    lax.fori_loop(0, rows, row_step, 0)


def scatter_kernel(back_ref, index_ref, weight_ref, out_ref):
    fields, rows, cols = back_ref.shape
    stacked, lanes = out_ref.shape
    segments = stacked // fields
    items = index_ref.shape[0] // rows
    lane_iota = lax.broadcasted_iota(jnp.int32, (lanes, cols), 0)
    segment_iota = lax.broadcasted_iota(jnp.int32, (fields, segments, cols), 1)

    def row_step(y, total):
        back = back_ref[:, pl.ds(y, 1), :]
        for item in range(items):
            index = index_ref[pl.ds(item * rows + y, 1), :]
            onehot = (lane_iota == index % lanes).astype(jnp.bfloat16)
            weighted = weight_ref[pl.ds(item * rows + y, 1), :][None] * back
            hit = segment_iota == (index // lanes)[None]
            spread = jnp.where(hit, weighted, 0.0).reshape(stacked, cols)
            total = total + matmul_exact(split_three(spread), onehot, 1)
        return total

    out_ref[...] = lax.fori_loop(0, rows, row_step, jnp.zeros((stacked, lanes), jnp.float32))


def remap_call(kernel, out_shape, *operands):
    vmem = pltpu.MemorySpace.VMEM
    return pl.pallas_call(
        kernel,
        out_shape=jax.ShapeDtypeStruct(out_shape, jnp.float32),
        in_specs=[pl.BlockSpec(memory_space=vmem)] * len(operands),
        out_specs=pl.BlockSpec(memory_space=vmem),
    )(*operands)


def lat_edges(marks, width):
    lat_count = lax.axis_size("lat")
    where_lat = lax.axis_index("lat")
    rows = lax.broadcasted_iota(jnp.int32, marks.shape, 0)
    keep_top = jnp.logical_or(where_lat > 0, rows >= width)
    keep_bottom = jnp.logical_or(where_lat < lat_count - 1, rows < marks.shape[0] - width)
    return jnp.where(jnp.logical_and(keep_top, keep_bottom), marks, 0.0)


def single_rim(values):
    return with_halo(values, (("lat", 2), ("lon", 3)), 1)


def shards(
    adjoint_state,
    mixing_base,
    atm_flux,
    send_count,
    send_segment,
    cover_index,
    cover_weight,
    land_mask,
):
    lat_count = lax.axis_size("lat")
    owned = atm_flux.shape[1]
    counts = send_count[0]
    capacity = send_segment.shape[1] // lat_count
    starts = jnp.cumsum(counts) - counts
    column = jnp.arange(capacity, dtype=jnp.int32)
    places = jnp.minimum(starts[:, None] + column[None, :], send_segment.shape[1] - 1)
    chosen = send_segment[0][places]
    live_slot = column[None, :] < counts[:, None]
    whole = lax.all_gather(atm_flux, "lat", axis=1, tiled=True)
    global_ids = lax.axis_index("lat") * owned + chosen
    arrived = lax.all_to_all(global_ids, "lat", split_axis=0, concat_axis=0, tiled=True)
    received = whole[:, arrived, :]
    items, rows, cols = cover_index.shape
    fields = received.shape[0]
    flat_recv = received.reshape(-1, received.shape[-1])
    index_rows = cover_index.reshape(items * rows, cols)
    weight_rows = cover_weight.reshape(items * rows, cols)
    forcing = remap_call(gather_kernel, (fields, rows, cols), flat_recv, index_rows, weight_rows)
    surface = WIND_GAIN * (forcing[2] * forcing[2] + forcing[3] * forcing[3]) + jax.nn.softplus(
        forcing[1] - forcing[0]
    )
    land = land_mask.astype(jnp.float32)
    ext, mask = extended_planes(adjoint_state, land_mask, HALO)
    state_adjoint, flux_back = tridiagonal(ext, mask, adjoint_state.shape, mixing_base, surface, land)
    buffer = remap_call(scatter_kernel, flat_recv.shape, flux_back, index_rows, weight_rows)
    returned = lax.all_to_all(
        buffer.reshape(received.shape), "lat", split_axis=1, concat_axis=1, tiled=True
    )
    kept = jnp.where(live_slot[None, :, :, None], returned, 0.0).reshape(4, -1, 128)
    owner_sum = jnp.zeros_like(atm_flux).at[:, chosen.reshape(-1), :].add(kept)
    flux_adjoint = lax.psum(owner_sum, "lon")
    return (state_adjoint, flux_adjoint)


def solution(mesh):
    in_specs = (
        P(None, None, "lat", "lon"),
        P(None, "lat", "lon"),
        P(None, "lat", None),
        P("lat", "lon"),
        P("lat", "lon"),
        P(None, "lat", "lon"),
        P(None, "lat", "lon"),
        P("lat", "lon"),
    )
    out_specs = (P(None, None, "lat", "lon"), P(None, "lat", None))
    return jax.shard_map(shards, mesh=mesh, in_specs=in_specs, out_specs=out_specs, check_vma=False)
```

```python
import math

import jax
import jax.numpy as jnp
import numpy as np
from jax import lax
from jax.experimental import pallas as pl
from jax.experimental.pallas import tpu as pltpu
from jax.sharding import PartitionSpec as P

SMOOTHING = 0.02
WIND_GAIN = 1.0
DEPTH_SCALE = 12.0
FIELD_MIX = (1.0, 1.0, 2.0, 2.0)


HALO = 4


def from_neighbours(block, axis, dim, width):
    count = lax.axis_size(axis)
    to_prev = [(i, (i - 1) % count) for i in range(count)]
    to_next = [(i, (i + 1) % count) for i in range(count)]
    size = block.shape[dim]
    from_next = lax.ppermute(lax.slice_in_dim(block, 0, width, axis=dim), axis, to_prev)
    from_prev = lax.ppermute(lax.slice_in_dim(block, size - width, size, axis=dim), axis, to_next)
    return from_next, from_prev


def extended_planes(values, land_mask, width):
    fields, levels, rows, cols = values.shape
    planes = values.reshape(fields * levels, rows, cols)
    coast = land_mask.astype(jnp.float32)[None]
    stack = jnp.concatenate([planes, coast], axis=0)
    south, north = from_neighbours(stack, "lat", 1, width)
    tall = jnp.concatenate([stack, south, north], axis=1)
    east, west = from_neighbours(tall, "lon", 2, width)
    wide = -(-(cols + 2 * width) // 128) * 128
    gap = jnp.zeros(tall.shape[:2] + (wide - cols - 2 * width,), jnp.float32)
    ext = jnp.concatenate([tall, east, gap, west], axis=2)
    lat_count = lax.axis_size("lat")
    where_lat = lax.axis_index("lat")
    row = lax.broadcasted_iota(jnp.int32, ext.shape[1:], 0)
    outside = jnp.logical_or(
        jnp.logical_and(where_lat == 0, row >= rows + width),
        jnp.logical_and(where_lat == lat_count - 1, jnp.logical_and(row >= rows, row < rows + width)),
    )
    mask = jnp.where(outside, 0.0, ext[-1])
    return ext, mask


def with_halo(block, sides, width):
    for axis, dim in sides:
        count = lax.axis_size(axis)
        forward = [(i, i + 1) for i in range(count - 1)]
        forward.append((count - 1, 0))
        backward = [(target, source) for source, target in forward]
        low = lax.ppermute(
            lax.slice_in_dim(block, block.shape[dim] - width, None, axis=dim), axis, forward
        )
        high = lax.ppermute(lax.slice_in_dim(block, 0, width, axis=dim), axis, backward)
        block = jnp.concatenate([low, block, high], axis=dim)
    return block


def laplace(values, marks):
    centre = values[..., 1:-1, 1:-1]
    north = marks[:-2, 1:-1] * (values[..., :-2, 1:-1] - centre)
    south = marks[2:, 1:-1] * (values[..., 2:, 1:-1] - centre)
    west = marks[1:-1, :-2] * (values[..., 1:-1, :-2] - centre)
    east = marks[1:-1, 2:] * (values[..., 1:-1, 2:] - centre)
    return marks[1:-1, 1:-1] * (north + south + west + east)


def tridiagonal_kernel(
    decay_ref, ext_ref, mask_ref, base_ref, surf_ref, land_ref, out_ref, back_ref, ratio_ref, marks_ref
):
    fields, levels = out_ref.shape[0], out_ref.shape[1]
    rows, cols = out_ref.shape[2], out_ref.shape[3]
    tall, wide = mask_ref.shape
    marks = mask_ref[...]
    marks_ref[0] = marks
    marks_ref[1] = pltpu.roll(marks, 1, 0)
    marks_ref[2] = pltpu.roll(marks, tall - 1, 0)
    marks_ref[3] = pltpu.roll(marks, 1, 1)
    marks_ref[4] = pltpu.roll(marks, wide - 1, 1)

    def laplace_ext(values):
        north = marks_ref[1] * (pltpu.roll(values, 1, 0) - values)
        south = marks_ref[2] * (pltpu.roll(values, tall - 1, 0) - values)
        west = marks_ref[3] * (pltpu.roll(values, 1, 1) - values)
        east = marks_ref[4] * (pltpu.roll(values, wide - 1, 1) - values)
        return marks_ref[0] * (((north + south) + west) + east)

    def smoothed(f, level):
        values = ext_ref[f * levels + level]
        for turn in range(2):
            inner = laplace_ext(values)
            values = values - SMOOTHING * laplace_ext(inner)
        return values[:rows, :cols]

    gains = sorted(set(FIELD_MIX))
    groups = [[f for f in range(fields) if FIELD_MIX[f] == g] for g in gains]
    surf = surf_ref[...]
    zero = jnp.zeros_like(surf)

    def step(level, below_mix, above_mix, ratios, parts):
        new_ratios, new_parts = [], list(parts)
        for gi, gain in enumerate(gains):
            below = gain * below_mix
            above = gain * above_mix
            pivot = ((1.0 + below) + above) - below * ratios[gi]
            if level is not None:
                ratio = above / pivot
                ratio_ref[gi, level] = ratio
                new_ratios.append(ratio)
            for f in groups[gi]:
                value = (smoothed(f, level if level is not None else levels - 1) + below * parts[f]) / pivot
                out_ref[f, level if level is not None else levels - 1] = value
                new_parts[f] = value
        return tuple(new_ratios), tuple(new_parts)

    def forward(level, carry):
        below_mix, ratios, parts = carry
        mix = base_ref[level] + surf * decay_ref[level]
        ratios, parts = step(level, below_mix, mix, ratios, parts)
        return (mix, ratios, parts)

    carry = (zero, tuple(zero for _ in gains), tuple(zero for _ in range(fields)))
    last_mix, ratios, parts = lax.fori_loop(0, levels - 1, forward, carry)
    step(None, last_mix, zero, ratios, parts)

    def backward(i, later):
        level = levels - 2 - i
        result = []
        for gi in range(len(gains)):
            ratio = ratio_ref[gi, level]
            for f in groups[gi]:
                value = out_ref[f, level] + ratio * later[f]
                out_ref[f, level] = value
                result.append((f, value))
        result.sort(key=lambda item: item[0])
        return tuple(v for _, v in result)

    final = tuple(out_ref[f, levels - 1] for f in range(fields))
    lax.fori_loop(0, levels - 1, backward, final)
    land = land_ref[...]
    for f in range(fields):
        back_ref[f] = land * out_ref[f, 0]


def tridiagonal(ext, mask, shape, mixing_base, surface, land):
    fields, levels = shape[0], shape[1]
    decay_table = np.array(
        [math.exp(-level / DEPTH_SCALE) for level in range(levels)], dtype=np.float32
    )
    vmem = pltpu.MemorySpace.VMEM
    return pl.pallas_call(
        tridiagonal_kernel,
        out_shape=(
            jax.ShapeDtypeStruct(shape, jnp.float32),
            jax.ShapeDtypeStruct((fields,) + shape[2:], jnp.float32),
        ),
        in_specs=[pl.BlockSpec(memory_space=pltpu.MemorySpace.SMEM)]
        + [pl.BlockSpec(memory_space=vmem)] * 5,
        out_specs=(pl.BlockSpec(memory_space=vmem), pl.BlockSpec(memory_space=vmem)),
        scratch_shapes=[
            pltpu.VMEM((len(set(FIELD_MIX)), levels) + shape[2:], jnp.float32),
            pltpu.VMEM((5,) + mask.shape, jnp.float32),
        ],
    )(jnp.asarray(decay_table), ext, mask, mixing_base, surface, land)


def split_three(values):
    high = values.astype(jnp.bfloat16)
    rest = values - high.astype(jnp.float32)
    middle = rest.astype(jnp.bfloat16)
    low = (rest - middle.astype(jnp.float32)).astype(jnp.bfloat16)
    return high, middle, low


def matmul_exact(parts, other, contract):
    numbers = (((1,), (contract,)), ((), ()))
    total = None
    for part in parts:
        product = lax.dot_general(part, other, numbers, preferred_element_type=jnp.float32)
        total = product if total is None else total + product
    return total


def gather_kernel(recv_ref, index_ref, weight_ref, out_ref):
    stacked, lanes = recv_ref.shape
    fields, rows, cols = out_ref.shape
    segments = stacked // fields
    items = index_ref.shape[0] // rows
    parts = split_three(recv_ref[...])
    lane_iota = lax.broadcasted_iota(jnp.int32, (lanes, cols), 0)
    segment_iota = lax.broadcasted_iota(jnp.int32, (fields, segments, cols), 1)

    def row_step(y, carry):
        total = None
        for item in range(items):
            index = index_ref[pl.ds(item * rows + y, 1), :]
            onehot = (lane_iota == index % lanes).astype(jnp.bfloat16)
            chosen = matmul_exact(parts, onehot, 0).reshape(fields, segments, cols)
            hit = segment_iota == (index // lanes)[None]
            picked = jnp.sum(jnp.where(hit, chosen, 0.0), axis=1)
            term = weight_ref[pl.ds(item * rows + y, 1), :] * picked
            total = term if total is None else total + term
        out_ref[:, pl.ds(y, 1), :] = total[:, None, :]
        return carry

    lax.fori_loop(0, rows, row_step, 0)


def scatter_kernel(back_ref, index_ref, weight_ref, out_ref):
    fields, rows, cols = back_ref.shape
    stacked, lanes = out_ref.shape
    segments = stacked // fields
    items = index_ref.shape[0] // rows
    lane_iota = lax.broadcasted_iota(jnp.int32, (lanes, cols), 0)
    segment_iota = lax.broadcasted_iota(jnp.int32, (fields, segments, cols), 1)

    def row_step(y, total):
        back = back_ref[:, pl.ds(y, 1), :]
        for item in range(items):
            index = index_ref[pl.ds(item * rows + y, 1), :]
            onehot = (lane_iota == index % lanes).astype(jnp.bfloat16)
            weighted = weight_ref[pl.ds(item * rows + y, 1), :][None] * back
            hit = segment_iota == (index // lanes)[None]
            spread = jnp.where(hit, weighted, 0.0).reshape(stacked, cols)
            total = total + matmul_exact(split_three(spread), onehot, 1)
        return total

    out_ref[...] = lax.fori_loop(0, rows, row_step, jnp.zeros((stacked, lanes), jnp.float32))


def remap_call(kernel, out_shape, *operands):
    vmem = pltpu.MemorySpace.VMEM
    return pl.pallas_call(
        kernel,
        out_shape=jax.ShapeDtypeStruct(out_shape, jnp.float32),
        in_specs=[pl.BlockSpec(memory_space=vmem)] * len(operands),
        out_specs=pl.BlockSpec(memory_space=vmem),
    )(*operands)


def sum_over(values, axis):
    count = lax.axis_size(axis)
    if count & (count - 1):
        return lax.psum(values, axis)
    step = 1
    while step < count:
        pairs = [(i, i ^ step) for i in range(count)]
        values = values + lax.ppermute(values, axis, pairs)
        step *= 2
    return values


def lat_edges(marks, width):
    lat_count = lax.axis_size("lat")
    where_lat = lax.axis_index("lat")
    rows = lax.broadcasted_iota(jnp.int32, marks.shape, 0)
    keep_top = jnp.logical_or(where_lat > 0, rows >= width)
    keep_bottom = jnp.logical_or(where_lat < lat_count - 1, rows < marks.shape[0] - width)
    return jnp.where(jnp.logical_and(keep_top, keep_bottom), marks, 0.0)


def single_rim(values):
    return with_halo(values, (("lat", 2), ("lon", 3)), 1)


def shards(
    adjoint_state,
    mixing_base,
    atm_flux,
    send_count,
    send_segment,
    cover_index,
    cover_weight,
    land_mask,
):
    lat_count = lax.axis_size("lat")
    owned = atm_flux.shape[1]
    counts = send_count[0]
    capacity = send_segment.shape[1] // lat_count
    starts = jnp.cumsum(counts) - counts
    column = jnp.arange(capacity, dtype=jnp.int32)
    places = jnp.minimum(starts[:, None] + column[None, :], send_segment.shape[1] - 1)
    chosen = send_segment[0][places]
    live_slot = column[None, :] < counts[:, None]
    outgoing = atm_flux[:, chosen, :]
    received = lax.all_to_all(outgoing, "lat", split_axis=1, concat_axis=1, tiled=True)
    items, rows, cols = cover_index.shape
    fields = received.shape[0]
    flat_recv = received.reshape(-1, received.shape[-1])
    index_rows = cover_index.reshape(items * rows, cols)
    weight_rows = cover_weight.reshape(items * rows, cols)
    forcing = remap_call(gather_kernel, (fields, rows, cols), flat_recv, index_rows, weight_rows)
    surface = WIND_GAIN * (forcing[2] * forcing[2] + forcing[3] * forcing[3]) + jax.nn.softplus(
        forcing[1] - forcing[0]
    )
    land = land_mask.astype(jnp.float32)
    ext, mask = extended_planes(adjoint_state, land_mask, HALO)
    state_adjoint, flux_back = tridiagonal(ext, mask, adjoint_state.shape, mixing_base, surface, land)
    buffer = remap_call(scatter_kernel, flat_recv.shape, flux_back, index_rows, weight_rows)
    returned = lax.all_to_all(
        buffer.reshape(received.shape), "lat", split_axis=1, concat_axis=1, tiled=True
    )
    kept = jnp.where(live_slot[None, :, :, None], returned, 0.0).reshape(4, -1, 128)
    owner_sum = jnp.zeros_like(atm_flux).at[:, chosen.reshape(-1), :].add(kept)
    flux_adjoint = sum_over(owner_sum, "lon")
    return (state_adjoint, flux_adjoint)


def solution(mesh):
    in_specs = (
        P(None, None, "lat", "lon"),
        P(None, "lat", "lon"),
        P(None, "lat", None),
        P("lat", "lon"),
        P("lat", "lon"),
        P(None, "lat", "lon"),
        P(None, "lat", "lon"),
        P("lat", "lon"),
    )
    out_specs = (P(None, None, "lat", "lon"), P(None, "lat", None))
    return jax.shard_map(shards, mesh=mesh, in_specs=in_specs, out_specs=out_specs, check_vma=False)
```

```python
import math

import jax
import jax.numpy as jnp
import numpy as np
from jax import lax
from jax.experimental import pallas as pl
from jax.experimental.pallas import tpu as pltpu
from jax.sharding import PartitionSpec as P

SMOOTHING = 0.02
WIND_GAIN = 1.0
DEPTH_SCALE = 12.0
FIELD_MIX = (1.0, 1.0, 2.0, 2.0)


HALO = 4


def from_neighbours(block, axis, dim, width):
    count = lax.axis_size(axis)
    to_prev = [(i, (i - 1) % count) for i in range(count)]
    to_next = [(i, (i + 1) % count) for i in range(count)]
    size = block.shape[dim]
    from_next = lax.ppermute(lax.slice_in_dim(block, 0, width, axis=dim), axis, to_prev)
    from_prev = lax.ppermute(lax.slice_in_dim(block, size - width, size, axis=dim), axis, to_next)
    return from_next, from_prev


def extended_planes(values, land_mask, width):
    fields, levels, rows, cols = values.shape
    planes = values.reshape(fields * levels, rows, cols)
    coast = land_mask.astype(jnp.float32)[None]
    stack = jnp.concatenate([planes, coast], axis=0)
    south, north = from_neighbours(stack, "lat", 1, width)
    tall = jnp.concatenate([stack, south, north], axis=1)
    east, west = from_neighbours(tall, "lon", 2, width)
    wide = -(-(cols + 2 * width) // 128) * 128
    gap = jnp.zeros(tall.shape[:2] + (wide - cols - 2 * width,), jnp.float32)
    ext = jnp.concatenate([tall, east, gap, west], axis=2)
    lat_count = lax.axis_size("lat")
    where_lat = lax.axis_index("lat")
    row = lax.broadcasted_iota(jnp.int32, ext.shape[1:], 0)
    outside = jnp.logical_or(
        jnp.logical_and(where_lat == 0, row >= rows + width),
        jnp.logical_and(where_lat == lat_count - 1, jnp.logical_and(row >= rows, row < rows + width)),
    )
    mask = jnp.where(outside, 0.0, ext[-1])
    return ext, mask


def with_halo(block, sides, width):
    for axis, dim in sides:
        count = lax.axis_size(axis)
        forward = [(i, i + 1) for i in range(count - 1)]
        forward.append((count - 1, 0))
        backward = [(target, source) for source, target in forward]
        low = lax.ppermute(
            lax.slice_in_dim(block, block.shape[dim] - width, None, axis=dim), axis, forward
        )
        high = lax.ppermute(lax.slice_in_dim(block, 0, width, axis=dim), axis, backward)
        block = jnp.concatenate([low, block, high], axis=dim)
    return block


def laplace(values, marks):
    centre = values[..., 1:-1, 1:-1]
    north = marks[:-2, 1:-1] * (values[..., :-2, 1:-1] - centre)
    south = marks[2:, 1:-1] * (values[..., 2:, 1:-1] - centre)
    west = marks[1:-1, :-2] * (values[..., 1:-1, :-2] - centre)
    east = marks[1:-1, 2:] * (values[..., 1:-1, 2:] - centre)
    return marks[1:-1, 1:-1] * (north + south + west + east)


def tridiagonal_kernel(
    decay_ref, ext_ref, mask_ref, base_ref, surf_ref, land_ref, out_ref, back_ref, ratio_ref, marks_ref
):
    fields, levels = out_ref.shape[0], out_ref.shape[1]
    rows, cols = out_ref.shape[2], out_ref.shape[3]
    tall, wide = mask_ref.shape
    marks = mask_ref[...]
    marks_ref[0] = marks
    marks_ref[1] = pltpu.roll(marks, 1, 0)
    marks_ref[2] = pltpu.roll(marks, tall - 1, 0)
    marks_ref[3] = pltpu.roll(marks, 1, 1)
    marks_ref[4] = pltpu.roll(marks, wide - 1, 1)

    def laplace_ext(values):
        north = marks_ref[1] * (pltpu.roll(values, 1, 0) - values)
        south = marks_ref[2] * (pltpu.roll(values, tall - 1, 0) - values)
        west = marks_ref[3] * (pltpu.roll(values, 1, 1) - values)
        east = marks_ref[4] * (pltpu.roll(values, wide - 1, 1) - values)
        return marks_ref[0] * (((north + south) + west) + east)

    def smoothed(f, level):
        values = ext_ref[f * levels + level]
        for turn in range(2):
            inner = laplace_ext(values)
            values = values - SMOOTHING * laplace_ext(inner)
        return values[:rows, :cols]

    gains = sorted(set(FIELD_MIX))
    groups = [[f for f in range(fields) if FIELD_MIX[f] == g] for g in gains]
    surf = surf_ref[...]
    zero = jnp.zeros_like(surf)

    def step(level, below_mix, above_mix, ratios, parts):
        new_ratios, new_parts = [], list(parts)
        for gi, gain in enumerate(gains):
            below = gain * below_mix
            above = gain * above_mix
            pivot = ((1.0 + below) + above) - below * ratios[gi]
            if level is not None:
                ratio = above / pivot
                ratio_ref[gi, level] = ratio
                new_ratios.append(ratio)
            for f in groups[gi]:
                value = (smoothed(f, level if level is not None else levels - 1) + below * parts[f]) / pivot
                out_ref[f, level if level is not None else levels - 1] = value
                new_parts[f] = value
        return tuple(new_ratios), tuple(new_parts)

    def forward(level, carry):
        below_mix, ratios, parts = carry
        mix = base_ref[level] + surf * decay_ref[level]
        ratios, parts = step(level, below_mix, mix, ratios, parts)
        return (mix, ratios, parts)

    carry = (zero, tuple(zero for _ in gains), tuple(zero for _ in range(fields)))
    last_mix, ratios, parts = lax.fori_loop(0, levels - 1, forward, carry)
    step(None, last_mix, zero, ratios, parts)

    def backward(i, later):
        level = levels - 2 - i
        result = []
        for gi in range(len(gains)):
            ratio = ratio_ref[gi, level]
            for f in groups[gi]:
                value = out_ref[f, level] + ratio * later[f]
                out_ref[f, level] = value
                result.append((f, value))
        result.sort(key=lambda item: item[0])
        return tuple(v for _, v in result)

    final = tuple(out_ref[f, levels - 1] for f in range(fields))
    lax.fori_loop(0, levels - 1, backward, final)
    land = land_ref[...]
    for f in range(fields):
        back_ref[f] = land * out_ref[f, 0]


def tridiagonal(ext, mask, shape, mixing_base, surface, land):
    fields, levels = shape[0], shape[1]
    decay_table = np.array(
        [math.exp(-level / DEPTH_SCALE) for level in range(levels)], dtype=np.float32
    )
    vmem = pltpu.MemorySpace.VMEM
    return pl.pallas_call(
        tridiagonal_kernel,
        out_shape=(
            jax.ShapeDtypeStruct(shape, jnp.float32),
            jax.ShapeDtypeStruct((fields,) + shape[2:], jnp.float32),
        ),
        in_specs=[pl.BlockSpec(memory_space=pltpu.MemorySpace.SMEM)]
        + [pl.BlockSpec(memory_space=vmem)] * 5,
        out_specs=(pl.BlockSpec(memory_space=vmem), pl.BlockSpec(memory_space=vmem)),
        scratch_shapes=[
            pltpu.VMEM((len(set(FIELD_MIX)), levels) + shape[2:], jnp.float32),
            pltpu.VMEM((5,) + mask.shape, jnp.float32),
        ],
    )(jnp.asarray(decay_table), ext, mask, mixing_base, surface, land)


def split_three(values):
    high = values.astype(jnp.bfloat16)
    rest = values - high.astype(jnp.float32)
    middle = rest.astype(jnp.bfloat16)
    low = (rest - middle.astype(jnp.float32)).astype(jnp.bfloat16)
    return high, middle, low


def matmul_exact(parts, other, contract):
    numbers = (((1,), (contract,)), ((), ()))
    total = None
    for part in parts:
        product = lax.dot_general(part, other, numbers, preferred_element_type=jnp.float32)
        total = product if total is None else total + product
    return total


def gather_kernel(recv_ref, index_ref, weight_ref, after_ref, out_ref):
    stacked, lanes = recv_ref.shape
    fields, rows, cols = out_ref.shape
    segments = stacked // fields
    items = index_ref.shape[0] // rows
    parts = split_three(recv_ref[...])
    lane_iota = lax.broadcasted_iota(jnp.int32, (lanes, cols), 0)
    segment_iota = lax.broadcasted_iota(jnp.int32, (fields, segments, cols), 1)

    def row_step(y, carry):
        total = None
        for item in range(items):
            index = index_ref[pl.ds(item * rows + y, 1), :]
            onehot = (lane_iota == index % lanes).astype(jnp.bfloat16)
            chosen = matmul_exact(parts, onehot, 0).reshape(fields, segments, cols)
            hit = segment_iota == (index // lanes)[None]
            picked = jnp.sum(jnp.where(hit, chosen, 0.0), axis=1)
            term = weight_ref[pl.ds(item * rows + y, 1), :] * picked
            total = term if total is None else total + term
        out_ref[:, pl.ds(y, 1), :] = total[:, None, :]
        return carry

    lax.fori_loop(0, rows, row_step, 0)


def scatter_kernel(back_ref, index_ref, weight_ref, out_ref):
    fields, rows, cols = back_ref.shape
    stacked, lanes = out_ref.shape
    segments = stacked // fields
    items = index_ref.shape[0] // rows
    lane_iota = lax.broadcasted_iota(jnp.int32, (lanes, cols), 0)
    segment_iota = lax.broadcasted_iota(jnp.int32, (fields, segments, cols), 1)

    def row_step(y, total):
        back = back_ref[:, pl.ds(y, 1), :]
        for item in range(items):
            index = index_ref[pl.ds(item * rows + y, 1), :]
            onehot = (lane_iota == index % lanes).astype(jnp.bfloat16)
            weighted = weight_ref[pl.ds(item * rows + y, 1), :][None] * back
            hit = segment_iota == (index // lanes)[None]
            spread = jnp.where(hit, weighted, 0.0).reshape(stacked, cols)
            total = total + matmul_exact(split_three(spread), onehot, 1)
        return total

    out_ref[...] = lax.fori_loop(0, rows, row_step, jnp.zeros((stacked, lanes), jnp.float32))


def remap_call(kernel, out_shape, *operands, after=()):
    vmem = pltpu.MemorySpace.VMEM
    return pl.pallas_call(
        kernel,
        out_shape=jax.ShapeDtypeStruct(out_shape, jnp.float32),
        in_specs=[pl.BlockSpec(memory_space=vmem)] * len(operands)
        + [pl.BlockSpec(memory_space=pl.ANY)] * len(after),
        out_specs=pl.BlockSpec(memory_space=vmem),
    )(*operands, *after)


def sum_over(values, axis):
    count = lax.axis_size(axis)
    if count & (count - 1):
        return lax.psum(values, axis)
    step = 1
    while step < count:
        pairs = [(i, i ^ step) for i in range(count)]
        values = values + lax.ppermute(values, axis, pairs)
        step *= 2
    return values


def lat_edges(marks, width):
    lat_count = lax.axis_size("lat")
    where_lat = lax.axis_index("lat")
    rows = lax.broadcasted_iota(jnp.int32, marks.shape, 0)
    keep_top = jnp.logical_or(where_lat > 0, rows >= width)
    keep_bottom = jnp.logical_or(where_lat < lat_count - 1, rows < marks.shape[0] - width)
    return jnp.where(jnp.logical_and(keep_top, keep_bottom), marks, 0.0)


def single_rim(values):
    return with_halo(values, (("lat", 2), ("lon", 3)), 1)


def shards(
    adjoint_state,
    mixing_base,
    atm_flux,
    send_count,
    send_segment,
    cover_index,
    cover_weight,
    land_mask,
):
    lat_count = lax.axis_size("lat")
    owned = atm_flux.shape[1]
    counts = send_count[0]
    capacity = send_segment.shape[1] // lat_count
    starts = jnp.cumsum(counts) - counts
    column = jnp.arange(capacity, dtype=jnp.int32)
    places = jnp.minimum(starts[:, None] + column[None, :], send_segment.shape[1] - 1)
    chosen = send_segment[0][places]
    live_slot = column[None, :] < counts[:, None]
    outgoing = atm_flux[:, chosen, :]
    received = lax.all_to_all(outgoing, "lat", split_axis=1, concat_axis=1, tiled=True)
    items, rows, cols = cover_index.shape
    fields = received.shape[0]
    flat_recv = received.reshape(-1, received.shape[-1])
    index_rows = cover_index.reshape(items * rows, cols)
    weight_rows = cover_weight.reshape(items * rows, cols)
    land = land_mask.astype(jnp.float32)
    ext, mask = extended_planes(adjoint_state, land_mask, HALO)
    forcing = remap_call(
        gather_kernel, (fields, rows, cols), flat_recv, index_rows, weight_rows, after=(ext,)
    )
    surface = WIND_GAIN * (forcing[2] * forcing[2] + forcing[3] * forcing[3]) + jax.nn.softplus(
        forcing[1] - forcing[0]
    )
    state_adjoint, flux_back = tridiagonal(ext, mask, adjoint_state.shape, mixing_base, surface, land)
    buffer = remap_call(scatter_kernel, flat_recv.shape, flux_back, index_rows, weight_rows)
    returned = lax.all_to_all(
        buffer.reshape(received.shape), "lat", split_axis=1, concat_axis=1, tiled=True
    )
    kept = jnp.where(live_slot[None, :, :, None], returned, 0.0).reshape(4, -1, 128)
    owner_sum = jnp.zeros_like(atm_flux).at[:, chosen.reshape(-1), :].add(kept)
    flux_adjoint = sum_over(owner_sum, "lon")
    return (state_adjoint, flux_adjoint)


def solution(mesh):
    in_specs = (
        P(None, None, "lat", "lon"),
        P(None, "lat", "lon"),
        P(None, "lat", None),
        P("lat", "lon"),
        P("lat", "lon"),
        P(None, "lat", "lon"),
        P(None, "lat", "lon"),
        P("lat", "lon"),
    )
    out_specs = (P(None, None, "lat", "lon"), P(None, "lat", None))
    return jax.shard_map(shards, mesh=mesh, in_specs=in_specs, out_specs=out_specs, check_vma=False)
```

```python
import math

import jax
import jax.numpy as jnp
import numpy as np
from jax import lax
from jax.experimental import pallas as pl
from jax.experimental.pallas import tpu as pltpu
from jax.sharding import PartitionSpec as P

SMOOTHING = 0.02
WIND_GAIN = 1.0
DEPTH_SCALE = 12.0
FIELD_MIX = (1.0, 1.0, 2.0, 2.0)


HALO = 4


def from_neighbours(block, axis, dim, width):
    count = lax.axis_size(axis)
    to_prev = [(i, (i - 1) % count) for i in range(count)]
    to_next = [(i, (i + 1) % count) for i in range(count)]
    size = block.shape[dim]
    from_next = lax.ppermute(lax.slice_in_dim(block, 0, width, axis=dim), axis, to_prev)
    from_prev = lax.ppermute(lax.slice_in_dim(block, size - width, size, axis=dim), axis, to_next)
    return from_next, from_prev


def extended_planes(values, land_mask, width):
    fields, levels, rows, cols = values.shape
    planes = values.reshape(fields * levels, rows, cols)
    coast = land_mask.astype(jnp.float32)[None]
    stack = jnp.concatenate([planes, coast], axis=0)
    south, north = from_neighbours(stack, "lat", 1, width)
    east, west = from_neighbours(stack, "lon", 2, width)
    sides = jnp.concatenate([east, west], axis=2)
    corner_south, corner_north = from_neighbours(sides, "lat", 1, width)
    wide = -(-(cols + 2 * width) // 128) * 128

    def band(middle, edges):
        gap = jnp.zeros(middle.shape[:2] + (wide - cols - 2 * width,), jnp.float32)
        return jnp.concatenate([middle, edges[:, :, :width], gap, edges[:, :, width:]], axis=2)

    ext = jnp.concatenate(
        [band(stack, sides), band(south, corner_south), band(north, corner_north)], axis=1
    )
    lat_count = lax.axis_size("lat")
    where_lat = lax.axis_index("lat")
    row = lax.broadcasted_iota(jnp.int32, ext.shape[1:], 0)
    outside = jnp.logical_or(
        jnp.logical_and(where_lat == 0, row >= rows + width),
        jnp.logical_and(where_lat == lat_count - 1, jnp.logical_and(row >= rows, row < rows + width)),
    )
    mask = jnp.where(outside, 0.0, ext[-1])
    return ext, mask


def with_halo(block, sides, width):
    for axis, dim in sides:
        count = lax.axis_size(axis)
        forward = [(i, i + 1) for i in range(count - 1)]
        forward.append((count - 1, 0))
        backward = [(target, source) for source, target in forward]
        low = lax.ppermute(
            lax.slice_in_dim(block, block.shape[dim] - width, None, axis=dim), axis, forward
        )
        high = lax.ppermute(lax.slice_in_dim(block, 0, width, axis=dim), axis, backward)
        block = jnp.concatenate([low, block, high], axis=dim)
    return block


def laplace(values, marks):
    centre = values[..., 1:-1, 1:-1]
    north = marks[:-2, 1:-1] * (values[..., :-2, 1:-1] - centre)
    south = marks[2:, 1:-1] * (values[..., 2:, 1:-1] - centre)
    west = marks[1:-1, :-2] * (values[..., 1:-1, :-2] - centre)
    east = marks[1:-1, 2:] * (values[..., 1:-1, 2:] - centre)
    return marks[1:-1, 1:-1] * (north + south + west + east)


def tridiagonal_kernel(
    decay_ref, ext_ref, mask_ref, base_ref, surf_ref, land_ref, out_ref, back_ref, ratio_ref, marks_ref
):
    fields, levels = out_ref.shape[0], out_ref.shape[1]
    rows, cols = out_ref.shape[2], out_ref.shape[3]
    tall, wide = mask_ref.shape
    marks = mask_ref[...]
    marks_ref[0] = marks * pltpu.roll(marks, 1, 0)
    marks_ref[1] = marks * pltpu.roll(marks, tall - 1, 0)
    marks_ref[2] = marks * pltpu.roll(marks, 1, 1)
    marks_ref[3] = marks * pltpu.roll(marks, wide - 1, 1)

    def laplace_ext(values):
        north = marks_ref[0] * (pltpu.roll(values, 1, 0) - values)
        south = marks_ref[1] * (pltpu.roll(values, tall - 1, 0) - values)
        west = marks_ref[2] * (pltpu.roll(values, 1, 1) - values)
        east = marks_ref[3] * (pltpu.roll(values, wide - 1, 1) - values)
        return ((north + south) + west) + east

    def smoothed(f, level):
        values = ext_ref[f * levels + level]
        for turn in range(2):
            inner = laplace_ext(values)
            values = values - SMOOTHING * laplace_ext(inner)
        return values[:rows, :cols]

    gains = sorted(set(FIELD_MIX))
    groups = [[f for f in range(fields) if FIELD_MIX[f] == g] for g in gains]
    surf = surf_ref[...]
    zero = jnp.zeros_like(surf)

    def step(level, below_mix, above_mix, ratios, parts):
        new_ratios, new_parts = [], list(parts)
        for gi, gain in enumerate(gains):
            below = gain * below_mix
            above = gain * above_mix
            pivot = ((1.0 + below) + above) - below * ratios[gi]
            if level is not None:
                ratio = above / pivot
                ratio_ref[gi, level] = ratio
                new_ratios.append(ratio)
            for f in groups[gi]:
                value = (smoothed(f, level if level is not None else levels - 1) + below * parts[f]) / pivot
                out_ref[f, level if level is not None else levels - 1] = value
                new_parts[f] = value
        return tuple(new_ratios), tuple(new_parts)

    def forward(level, carry):
        below_mix, ratios, parts = carry
        mix = base_ref[level] + surf * decay_ref[level]
        ratios, parts = step(level, below_mix, mix, ratios, parts)
        return (mix, ratios, parts)

    carry = (zero, tuple(zero for _ in gains), tuple(zero for _ in range(fields)))
    last_mix, ratios, parts = lax.fori_loop(0, levels - 1, forward, carry)
    step(None, last_mix, zero, ratios, parts)

    def backward(i, later):
        level = levels - 2 - i
        result = []
        for gi in range(len(gains)):
            ratio = ratio_ref[gi, level]
            for f in groups[gi]:
                value = out_ref[f, level] + ratio * later[f]
                out_ref[f, level] = value
                result.append((f, value))
        result.sort(key=lambda item: item[0])
        return tuple(v for _, v in result)

    final = tuple(out_ref[f, levels - 1] for f in range(fields))
    lax.fori_loop(0, levels - 1, backward, final)
    land = land_ref[...]
    for f in range(fields):
        back_ref[f] = land * out_ref[f, 0]


def tridiagonal(ext, mask, shape, mixing_base, surface, land):
    fields, levels = shape[0], shape[1]
    decay_table = np.array(
        [math.exp(-level / DEPTH_SCALE) for level in range(levels)], dtype=np.float32
    )
    vmem = pltpu.MemorySpace.VMEM
    return pl.pallas_call(
        tridiagonal_kernel,
        out_shape=(
            jax.ShapeDtypeStruct(shape, jnp.float32),
            jax.ShapeDtypeStruct((fields,) + shape[2:], jnp.float32),
        ),
        in_specs=[pl.BlockSpec(memory_space=pltpu.MemorySpace.SMEM)]
        + [pl.BlockSpec(memory_space=vmem)] * 5,
        out_specs=(pl.BlockSpec(memory_space=vmem), pl.BlockSpec(memory_space=vmem)),
        scratch_shapes=[
            pltpu.VMEM((len(set(FIELD_MIX)), levels) + shape[2:], jnp.float32),
            pltpu.VMEM((4,) + mask.shape, jnp.float32),
        ],
    )(jnp.asarray(decay_table), ext, mask, mixing_base, surface, land)


def split_three(values):
    high = values.astype(jnp.bfloat16)
    rest = values - high.astype(jnp.float32)
    middle = rest.astype(jnp.bfloat16)
    low = (rest - middle.astype(jnp.float32)).astype(jnp.bfloat16)
    return high, middle, low


def matmul_exact(parts, other, contract):
    numbers = (((1,), (contract,)), ((), ()))
    total = None
    for part in parts:
        product = lax.dot_general(part, other, numbers, preferred_element_type=jnp.float32)
        total = product if total is None else total + product
    return total


def gather_kernel(recv_ref, index_ref, weight_ref, after_ref, out_ref):
    stacked, lanes = recv_ref.shape
    fields, rows, cols = out_ref.shape
    segments = stacked // fields
    items = index_ref.shape[0] // rows
    parts = split_three(recv_ref[...])
    lane_iota = lax.broadcasted_iota(jnp.int32, (lanes, cols), 0)
    segment_iota = lax.broadcasted_iota(jnp.int32, (fields, segments, cols), 1)

    def row_step(y, carry):
        total = None
        for item in range(items):
            index = index_ref[pl.ds(item * rows + y, 1), :]
            onehot = (lane_iota == index % lanes).astype(jnp.bfloat16)
            chosen = matmul_exact(parts, onehot, 0).reshape(fields, segments, cols)
            hit = segment_iota == (index // lanes)[None]
            picked = jnp.sum(jnp.where(hit, chosen, 0.0), axis=1)
            term = weight_ref[pl.ds(item * rows + y, 1), :] * picked
            total = term if total is None else total + term
        out_ref[:, pl.ds(y, 1), :] = total[:, None, :]
        return carry

    lax.fori_loop(0, rows, row_step, 0)


def scatter_kernel(back_ref, index_ref, weight_ref, out_ref):
    fields, rows, cols = back_ref.shape
    stacked, lanes = out_ref.shape
    segments = stacked // fields
    items = index_ref.shape[0] // rows
    lane_iota = lax.broadcasted_iota(jnp.int32, (lanes, cols), 0)
    segment_iota = lax.broadcasted_iota(jnp.int32, (fields, segments, cols), 1)

    def row_step(y, total):
        back = back_ref[:, pl.ds(y, 1), :]
        for item in range(items):
            index = index_ref[pl.ds(item * rows + y, 1), :]
            onehot = (lane_iota == index % lanes).astype(jnp.bfloat16)
            weighted = weight_ref[pl.ds(item * rows + y, 1), :][None] * back
            hit = segment_iota == (index // lanes)[None]
            spread = jnp.where(hit, weighted, 0.0).reshape(stacked, cols)
            total = total + matmul_exact(split_three(spread), onehot, 1)
        return total

    out_ref[...] = lax.fori_loop(0, rows, row_step, jnp.zeros((stacked, lanes), jnp.float32))


def remap_call(kernel, out_shape, *operands, after=()):
    vmem = pltpu.MemorySpace.VMEM
    return pl.pallas_call(
        kernel,
        out_shape=jax.ShapeDtypeStruct(out_shape, jnp.float32),
        in_specs=[pl.BlockSpec(memory_space=vmem)] * len(operands)
        + [pl.BlockSpec(memory_space=pl.ANY)] * len(after),
        out_specs=pl.BlockSpec(memory_space=vmem),
    )(*operands, *after)


def sum_over(values, axis):
    count = lax.axis_size(axis)
    if count & (count - 1):
        return lax.psum(values, axis)
    step = 1
    while step < count:
        pairs = [(i, i ^ step) for i in range(count)]
        values = values + lax.ppermute(values, axis, pairs)
        step *= 2
    return values


def lat_edges(marks, width):
    lat_count = lax.axis_size("lat")
    where_lat = lax.axis_index("lat")
    rows = lax.broadcasted_iota(jnp.int32, marks.shape, 0)
    keep_top = jnp.logical_or(where_lat > 0, rows >= width)
    keep_bottom = jnp.logical_or(where_lat < lat_count - 1, rows < marks.shape[0] - width)
    return jnp.where(jnp.logical_and(keep_top, keep_bottom), marks, 0.0)


def single_rim(values):
    return with_halo(values, (("lat", 2), ("lon", 3)), 1)


def shards(
    adjoint_state,
    mixing_base,
    atm_flux,
    send_count,
    send_segment,
    cover_index,
    cover_weight,
    land_mask,
):
    lat_count = lax.axis_size("lat")
    owned = atm_flux.shape[1]
    counts = send_count[0]
    capacity = send_segment.shape[1] // lat_count
    starts = jnp.cumsum(counts) - counts
    column = jnp.arange(capacity, dtype=jnp.int32)
    places = jnp.minimum(starts[:, None] + column[None, :], send_segment.shape[1] - 1)
    chosen = send_segment[0][places]
    live_slot = column[None, :] < counts[:, None]
    outgoing = atm_flux[:, chosen, :]
    received = lax.all_to_all(outgoing, "lat", split_axis=1, concat_axis=1, tiled=True)
    items, rows, cols = cover_index.shape
    fields = received.shape[0]
    flat_recv = received.reshape(-1, received.shape[-1])
    index_rows = cover_index.reshape(items * rows, cols)
    weight_rows = cover_weight.reshape(items * rows, cols)
    land = land_mask.astype(jnp.float32)
    ext, mask = extended_planes(adjoint_state, land_mask, HALO)
    forcing = remap_call(
        gather_kernel, (fields, rows, cols), flat_recv, index_rows, weight_rows, after=(ext,)
    )
    surface = WIND_GAIN * (forcing[2] * forcing[2] + forcing[3] * forcing[3]) + jax.nn.softplus(
        forcing[1] - forcing[0]
    )
    state_adjoint, flux_back = tridiagonal(ext, mask, adjoint_state.shape, mixing_base, surface, land)
    buffer = remap_call(scatter_kernel, flat_recv.shape, flux_back, index_rows, weight_rows)
    returned = lax.all_to_all(
        buffer.reshape(received.shape), "lat", split_axis=1, concat_axis=1, tiled=True
    )
    kept = jnp.where(live_slot[None, :, :, None], returned, 0.0).reshape(4, -1, 128)
    owner_sum = jnp.zeros_like(atm_flux).at[:, chosen.reshape(-1), :].add(kept)
    flux_adjoint = sum_over(owner_sum, "lon")
    return (state_adjoint, flux_adjoint)


def solution(mesh):
    in_specs = (
        P(None, None, "lat", "lon"),
        P(None, "lat", "lon"),
        P(None, "lat", None),
        P("lat", "lon"),
        P("lat", "lon"),
        P(None, "lat", "lon"),
        P(None, "lat", "lon"),
        P("lat", "lon"),
    )
    out_specs = (P(None, None, "lat", "lon"), P(None, "lat", None))
    return jax.shard_map(shards, mesh=mesh, in_specs=in_specs, out_specs=out_specs, check_vma=False)
```

```python
import math

import jax
import jax.numpy as jnp
import numpy as np
from jax import lax
from jax.experimental import pallas as pl
from jax.experimental.pallas import tpu as pltpu
from jax.sharding import PartitionSpec as P

SMOOTHING = 0.02
WIND_GAIN = 1.0
DEPTH_SCALE = 12.0
FIELD_MIX = (1.0, 1.0, 2.0, 2.0)


HALO = 4


def from_neighbours(block, axis, dim, width):
    count = lax.axis_size(axis)
    to_prev = [(i, (i - 1) % count) for i in range(count)]
    to_next = [(i, (i + 1) % count) for i in range(count)]
    size = block.shape[dim]
    from_next = lax.ppermute(lax.slice_in_dim(block, 0, width, axis=dim), axis, to_prev)
    from_prev = lax.ppermute(lax.slice_in_dim(block, size - width, size, axis=dim), axis, to_next)
    return from_next, from_prev


def extended_planes(values, land_mask, width):
    fields, levels, rows, cols = values.shape
    planes = values.reshape(fields * levels, rows, cols)
    coast = land_mask.astype(jnp.float32)[None]
    stack = jnp.concatenate([planes, coast], axis=0)
    south, north = from_neighbours(stack, "lat", 1, width)
    east, west = from_neighbours(stack, "lon", 2, width)
    sides = jnp.concatenate([east, west], axis=2)
    corner_south, corner_north = from_neighbours(sides, "lat", 1, width)
    wide = -(-(2 * width) // 128) * 128
    edges = jnp.concatenate([sides, corner_south, corner_north], axis=1)
    gap = jnp.zeros(edges.shape[:2] + (wide - 2 * width,), jnp.float32)
    edge_tile = jnp.concatenate([edges[:, :, :width], gap, edges[:, :, width:]], axis=2)
    halo_rows = jnp.concatenate([south, north], axis=1)
    coast_plane = jnp.concatenate(
        [jnp.concatenate([stack[-1], halo_rows[-1]], axis=0), edge_tile[-1]], axis=1
    )
    lat_count = lax.axis_size("lat")
    where_lat = lax.axis_index("lat")
    row = lax.broadcasted_iota(jnp.int32, coast_plane.shape, 0)
    outside = jnp.logical_or(
        jnp.logical_and(where_lat == 0, row >= rows + width),
        jnp.logical_and(where_lat == lat_count - 1, jnp.logical_and(row >= rows, row < rows + width)),
    )
    mask = jnp.where(outside, 0.0, coast_plane)
    return planes, halo_rows, edge_tile, mask


def with_halo(block, sides, width):
    for axis, dim in sides:
        count = lax.axis_size(axis)
        forward = [(i, i + 1) for i in range(count - 1)]
        forward.append((count - 1, 0))
        backward = [(target, source) for source, target in forward]
        low = lax.ppermute(
            lax.slice_in_dim(block, block.shape[dim] - width, None, axis=dim), axis, forward
        )
        high = lax.ppermute(lax.slice_in_dim(block, 0, width, axis=dim), axis, backward)
        block = jnp.concatenate([low, block, high], axis=dim)
    return block


def laplace(values, marks):
    centre = values[..., 1:-1, 1:-1]
    north = marks[:-2, 1:-1] * (values[..., :-2, 1:-1] - centre)
    south = marks[2:, 1:-1] * (values[..., 2:, 1:-1] - centre)
    west = marks[1:-1, :-2] * (values[..., 1:-1, :-2] - centre)
    east = marks[1:-1, 2:] * (values[..., 1:-1, 2:] - centre)
    return marks[1:-1, 1:-1] * (north + south + west + east)


def tridiagonal_kernel(
    decay_ref, inner_ref, rows_ref, edge_ref, mask_ref, base_ref, surf_ref, land_ref,
    out_ref, back_ref, ratio_ref, marks_ref,
):
    fields, levels = out_ref.shape[0], out_ref.shape[1]
    rows, cols = out_ref.shape[2], out_ref.shape[3]
    tall, wide = mask_ref.shape
    marks = mask_ref[...]
    marks_ref[0] = marks * pltpu.roll(marks, 1, 0)
    marks_ref[1] = marks * pltpu.roll(marks, tall - 1, 0)
    marks_ref[2] = marks * pltpu.roll(marks, 1, 1)
    marks_ref[3] = marks * pltpu.roll(marks, wide - 1, 1)

    def laplace_ext(values):
        north = marks_ref[0] * (pltpu.roll(values, 1, 0) - values)
        south = marks_ref[1] * (pltpu.roll(values, tall - 1, 0) - values)
        west = marks_ref[2] * (pltpu.roll(values, 1, 1) - values)
        east = marks_ref[3] * (pltpu.roll(values, wide - 1, 1) - values)
        return ((north + south) + west) + east

    def smoothed(f, level):
        plane = f * levels + level
        values = jnp.concatenate([inner_ref[plane], rows_ref[plane]], axis=0)
        values = jnp.concatenate([values, edge_ref[plane]], axis=1)
        for turn in range(2):
            inner = laplace_ext(values)
            values = values - SMOOTHING * laplace_ext(inner)
        return values[:rows, :cols]

    gains = sorted(set(FIELD_MIX))
    groups = [[f for f in range(fields) if FIELD_MIX[f] == g] for g in gains]
    surf = surf_ref[...]
    zero = jnp.zeros_like(surf)

    def step(level, below_mix, above_mix, ratios, parts):
        new_ratios, new_parts = [], list(parts)
        for gi, gain in enumerate(gains):
            below = gain * below_mix
            above = gain * above_mix
            pivot = ((1.0 + below) + above) - below * ratios[gi]
            if level is not None:
                ratio = above / pivot
                ratio_ref[gi, level] = ratio
                new_ratios.append(ratio)
            for f in groups[gi]:
                value = (smoothed(f, level if level is not None else levels - 1) + below * parts[f]) / pivot
                out_ref[f, level if level is not None else levels - 1] = value
                new_parts[f] = value
        return tuple(new_ratios), tuple(new_parts)

    def forward(level, carry):
        below_mix, ratios, parts = carry
        mix = base_ref[level] + surf * decay_ref[level]
        ratios, parts = step(level, below_mix, mix, ratios, parts)
        return (mix, ratios, parts)

    carry = (zero, tuple(zero for _ in gains), tuple(zero for _ in range(fields)))
    last_mix, ratios, parts = lax.fori_loop(0, levels - 1, forward, carry)
    step(None, last_mix, zero, ratios, parts)

    def backward(i, later):
        level = levels - 2 - i
        result = []
        for gi in range(len(gains)):
            ratio = ratio_ref[gi, level]
            for f in groups[gi]:
                value = out_ref[f, level] + ratio * later[f]
                out_ref[f, level] = value
                result.append((f, value))
        result.sort(key=lambda item: item[0])
        return tuple(v for _, v in result)

    final = tuple(out_ref[f, levels - 1] for f in range(fields))
    lax.fori_loop(0, levels - 1, backward, final)
    land = land_ref[...]
    for f in range(fields):
        back_ref[f] = land * out_ref[f, 0]


def tridiagonal(pieces, mask, shape, mixing_base, surface, land):
    fields, levels = shape[0], shape[1]
    decay_table = np.array(
        [math.exp(-level / DEPTH_SCALE) for level in range(levels)], dtype=np.float32
    )
    vmem = pltpu.MemorySpace.VMEM
    return pl.pallas_call(
        tridiagonal_kernel,
        out_shape=(
            jax.ShapeDtypeStruct(shape, jnp.float32),
            jax.ShapeDtypeStruct((fields,) + shape[2:], jnp.float32),
        ),
        in_specs=[pl.BlockSpec(memory_space=pltpu.MemorySpace.SMEM)]
        + [pl.BlockSpec(memory_space=vmem)] * (len(pieces) + 4),
        out_specs=(pl.BlockSpec(memory_space=vmem), pl.BlockSpec(memory_space=vmem)),
        scratch_shapes=[
            pltpu.VMEM((len(set(FIELD_MIX)), levels) + shape[2:], jnp.float32),
            pltpu.VMEM((4,) + mask.shape, jnp.float32),
        ],
    )(jnp.asarray(decay_table), *pieces, mask, mixing_base, surface, land)


def split_three(values):
    high = values.astype(jnp.bfloat16)
    rest = values - high.astype(jnp.float32)
    middle = rest.astype(jnp.bfloat16)
    low = (rest - middle.astype(jnp.float32)).astype(jnp.bfloat16)
    return high, middle, low


def matmul_exact(parts, other, contract):
    numbers = (((1,), (contract,)), ((), ()))
    total = None
    for part in parts:
        product = lax.dot_general(part, other, numbers, preferred_element_type=jnp.float32)
        total = product if total is None else total + product
    return total


def gather_kernel(recv_ref, index_ref, weight_ref, *after_and_out):
    out_ref = after_and_out[-1]
    stacked, lanes = recv_ref.shape
    fields, rows, cols = out_ref.shape
    segments = stacked // fields
    items = index_ref.shape[0] // rows
    parts = split_three(recv_ref[...])
    lane_iota = lax.broadcasted_iota(jnp.int32, (lanes, cols), 0)
    segment_iota = lax.broadcasted_iota(jnp.int32, (fields, segments, cols), 1)

    def row_step(y, carry):
        total = None
        for item in range(items):
            index = index_ref[pl.ds(item * rows + y, 1), :]
            onehot = (lane_iota == index % lanes).astype(jnp.bfloat16)
            chosen = matmul_exact(parts, onehot, 0).reshape(fields, segments, cols)
            hit = segment_iota == (index // lanes)[None]
            picked = jnp.sum(jnp.where(hit, chosen, 0.0), axis=1)
            term = weight_ref[pl.ds(item * rows + y, 1), :] * picked
            total = term if total is None else total + term
        out_ref[:, pl.ds(y, 1), :] = total[:, None, :]
        return carry

    lax.fori_loop(0, rows, row_step, 0)


def scatter_kernel(back_ref, index_ref, weight_ref, out_ref):
    fields, rows, cols = back_ref.shape
    stacked, lanes = out_ref.shape
    segments = stacked // fields
    items = index_ref.shape[0] // rows
    lane_iota = lax.broadcasted_iota(jnp.int32, (lanes, cols), 0)
    segment_iota = lax.broadcasted_iota(jnp.int32, (fields, segments, cols), 1)

    def row_step(y, total):
        back = back_ref[:, pl.ds(y, 1), :]
        for item in range(items):
            index = index_ref[pl.ds(item * rows + y, 1), :]
            onehot = (lane_iota == index % lanes).astype(jnp.bfloat16)
            weighted = weight_ref[pl.ds(item * rows + y, 1), :][None] * back
            hit = segment_iota == (index // lanes)[None]
            spread = jnp.where(hit, weighted, 0.0).reshape(stacked, cols)
            total = total + matmul_exact(split_three(spread), onehot, 1)
        return total

    out_ref[...] = lax.fori_loop(0, rows, row_step, jnp.zeros((stacked, lanes), jnp.float32))


def remap_call(kernel, out_shape, *operands, after=()):
    vmem = pltpu.MemorySpace.VMEM
    return pl.pallas_call(
        kernel,
        out_shape=jax.ShapeDtypeStruct(out_shape, jnp.float32),
        in_specs=[pl.BlockSpec(memory_space=vmem)] * len(operands)
        + [pl.BlockSpec(memory_space=pl.ANY)] * len(after),
        out_specs=pl.BlockSpec(memory_space=vmem),
    )(*operands, *after)


def sum_over(values, axis):
    count = lax.axis_size(axis)
    if count & (count - 1):
        return lax.psum(values, axis)
    step = 1
    while step < count:
        pairs = [(i, i ^ step) for i in range(count)]
        values = values + lax.ppermute(values, axis, pairs)
        step *= 2
    return values


def lat_edges(marks, width):
    lat_count = lax.axis_size("lat")
    where_lat = lax.axis_index("lat")
    rows = lax.broadcasted_iota(jnp.int32, marks.shape, 0)
    keep_top = jnp.logical_or(where_lat > 0, rows >= width)
    keep_bottom = jnp.logical_or(where_lat < lat_count - 1, rows < marks.shape[0] - width)
    return jnp.where(jnp.logical_and(keep_top, keep_bottom), marks, 0.0)


def single_rim(values):
    return with_halo(values, (("lat", 2), ("lon", 3)), 1)


def shards(
    adjoint_state,
    mixing_base,
    atm_flux,
    send_count,
    send_segment,
    cover_index,
    cover_weight,
    land_mask,
):
    lat_count = lax.axis_size("lat")
    owned = atm_flux.shape[1]
    counts = send_count[0]
    capacity = send_segment.shape[1] // lat_count
    starts = jnp.cumsum(counts) - counts
    column = jnp.arange(capacity, dtype=jnp.int32)
    places = jnp.minimum(starts[:, None] + column[None, :], send_segment.shape[1] - 1)
    chosen = send_segment[0][places]
    live_slot = column[None, :] < counts[:, None]
    outgoing = atm_flux[:, chosen, :]
    received = lax.all_to_all(outgoing, "lat", split_axis=1, concat_axis=1, tiled=True)
    items, rows, cols = cover_index.shape
    fields = received.shape[0]
    flat_recv = received.reshape(-1, received.shape[-1])
    index_rows = cover_index.reshape(items * rows, cols)
    weight_rows = cover_weight.reshape(items * rows, cols)
    land = land_mask.astype(jnp.float32)
    *pieces, mask = extended_planes(adjoint_state, land_mask, HALO)
    forcing = remap_call(
        gather_kernel, (fields, rows, cols), flat_recv, index_rows, weight_rows, after=tuple(pieces[1:])
    )
    surface = WIND_GAIN * (forcing[2] * forcing[2] + forcing[3] * forcing[3]) + jax.nn.softplus(
        forcing[1] - forcing[0]
    )
    state_adjoint, flux_back = tridiagonal(pieces, mask, adjoint_state.shape, mixing_base, surface, land)
    buffer = remap_call(scatter_kernel, flat_recv.shape, flux_back, index_rows, weight_rows)
    returned = lax.all_to_all(
        buffer.reshape(received.shape), "lat", split_axis=1, concat_axis=1, tiled=True
    )
    kept = jnp.where(live_slot[None, :, :, None], returned, 0.0).reshape(4, -1, 128)
    owner_sum = jnp.zeros_like(atm_flux).at[:, chosen.reshape(-1), :].add(kept)
    flux_adjoint = sum_over(owner_sum, "lon")
    return (state_adjoint, flux_adjoint)


def solution(mesh):
    in_specs = (
        P(None, None, "lat", "lon"),
        P(None, "lat", "lon"),
        P(None, "lat", None),
        P("lat", "lon"),
        P("lat", "lon"),
        P(None, "lat", "lon"),
        P(None, "lat", "lon"),
        P("lat", "lon"),
    )
    out_specs = (P(None, None, "lat", "lon"), P(None, "lat", None))
    return jax.shard_map(shards, mesh=mesh, in_specs=in_specs, out_specs=out_specs, check_vma=False)
```

```python
import math

import jax
import jax.numpy as jnp
import numpy as np
from jax import lax
from jax.experimental import pallas as pl
from jax.experimental.pallas import tpu as pltpu
from jax.sharding import PartitionSpec as P

SMOOTHING = 0.02
WIND_GAIN = 1.0
DEPTH_SCALE = 12.0
FIELD_MIX = (1.0, 1.0, 2.0, 2.0)


HALO = 4


def from_neighbours(block, axis, dim, width):
    count = lax.axis_size(axis)
    to_prev = [(i, (i - 1) % count) for i in range(count)]
    to_next = [(i, (i + 1) % count) for i in range(count)]
    size = block.shape[dim]
    from_next = lax.ppermute(lax.slice_in_dim(block, 0, width, axis=dim), axis, to_prev)
    from_prev = lax.ppermute(lax.slice_in_dim(block, size - width, size, axis=dim), axis, to_next)
    return from_next, from_prev


def extended_planes(values, land_mask, width):
    fields, levels, rows, cols = values.shape
    planes = values.reshape(fields * levels, rows, cols)
    coast = land_mask.astype(jnp.float32)[None]
    stack = jnp.concatenate([planes, coast], axis=0)
    south, north = from_neighbours(stack, "lat", 1, width)
    east, west = from_neighbours(stack, "lon", 2, width)
    sides = jnp.concatenate([east, west], axis=2)
    corner_south, corner_north = from_neighbours(sides, "lat", 1, width)
    wide = -(-(2 * width) // 128) * 128
    edges = jnp.concatenate([sides, corner_south, corner_north], axis=1)
    gap = jnp.zeros(edges.shape[:2] + (wide - 2 * width,), jnp.float32)
    edge_tile = jnp.concatenate([edges[:, :, :width], gap, edges[:, :, width:]], axis=2)
    halo_rows = jnp.concatenate([south, north], axis=1)
    coast_plane = jnp.concatenate(
        [jnp.concatenate([stack[-1], halo_rows[-1]], axis=0), edge_tile[-1]], axis=1
    )
    lat_count = lax.axis_size("lat")
    where_lat = lax.axis_index("lat")
    row = lax.broadcasted_iota(jnp.int32, coast_plane.shape, 0)
    outside = jnp.logical_or(
        jnp.logical_and(where_lat == 0, row >= rows + width),
        jnp.logical_and(where_lat == lat_count - 1, jnp.logical_and(row >= rows, row < rows + width)),
    )
    mask = jnp.where(outside, 0.0, coast_plane)
    return planes, halo_rows, edge_tile, mask


def with_halo(block, sides, width):
    for axis, dim in sides:
        count = lax.axis_size(axis)
        forward = [(i, i + 1) for i in range(count - 1)]
        forward.append((count - 1, 0))
        backward = [(target, source) for source, target in forward]
        low = lax.ppermute(
            lax.slice_in_dim(block, block.shape[dim] - width, None, axis=dim), axis, forward
        )
        high = lax.ppermute(lax.slice_in_dim(block, 0, width, axis=dim), axis, backward)
        block = jnp.concatenate([low, block, high], axis=dim)
    return block


def laplace(values, marks):
    centre = values[..., 1:-1, 1:-1]
    north = marks[:-2, 1:-1] * (values[..., :-2, 1:-1] - centre)
    south = marks[2:, 1:-1] * (values[..., 2:, 1:-1] - centre)
    west = marks[1:-1, :-2] * (values[..., 1:-1, :-2] - centre)
    east = marks[1:-1, 2:] * (values[..., 1:-1, 2:] - centre)
    return marks[1:-1, 1:-1] * (north + south + west + east)


def tridiagonal_kernel(
    decay_ref, inner_ref, rows_ref, edge_ref, mask_ref, base_ref, surf_ref, land_ref,
    out_ref, back_ref, ratio_ref, marks_ref,
):
    fields, levels = out_ref.shape[0], out_ref.shape[1]
    rows, cols = out_ref.shape[2], out_ref.shape[3]
    tall, wide = mask_ref.shape
    marks = mask_ref[...]
    marks_ref[0] = marks * pltpu.roll(marks, 1, 0)
    marks_ref[1] = marks * pltpu.roll(marks, tall - 1, 0)
    marks_ref[2] = marks * pltpu.roll(marks, 1, 1)
    marks_ref[3] = marks * pltpu.roll(marks, wide - 1, 1)
    marks_ref[4] = (marks_ref[0] + marks_ref[1]) + (marks_ref[2] + marks_ref[3])

    def laplace_ext(values, inner=False):
        shifted = [
            pltpu.roll(values, 1, 0),
            pltpu.roll(values, tall - 1, 0),
            pltpu.roll(values, 1, 1),
            pltpu.roll(values, wide - 1, 1),
        ]
        if inner:
            shifted = [part[:rows, :cols] for part in shifted]
            values = values[:rows, :cols]
            weight = [marks_ref[i, :rows, :cols] for i in range(5)]
        else:
            weight = [marks_ref[i] for i in range(5)]
        vertical = weight[0] * shifted[0] + weight[1] * shifted[1]
        across = weight[2] * shifted[2] + weight[3] * shifted[3]
        return (vertical + across) - weight[4] * values

    def smoothed(f, level):
        plane = f * levels + level
        values = jnp.concatenate([inner_ref[plane], rows_ref[plane]], axis=0)
        values = jnp.concatenate([values, edge_ref[plane]], axis=1)
        inner = laplace_ext(values)
        values = values - SMOOTHING * laplace_ext(inner)
        inner = laplace_ext(values)
        return values[:rows, :cols] - SMOOTHING * laplace_ext(inner, inner=True)

    gains = sorted(set(FIELD_MIX))
    groups = [[f for f in range(fields) if FIELD_MIX[f] == g] for g in gains]
    surf = surf_ref[...]
    zero = jnp.zeros_like(surf)

    def step(level, below_mix, above_mix, ratios, parts):
        new_ratios, new_parts = [], list(parts)
        for gi, gain in enumerate(gains):
            below = gain * below_mix
            above = gain * above_mix
            pivot = ((1.0 + below) + above) - below * ratios[gi]
            if level is not None:
                ratio = above / pivot
                ratio_ref[gi, level] = ratio
                new_ratios.append(ratio)
            for f in groups[gi]:
                value = (smoothed(f, level if level is not None else levels - 1) + below * parts[f]) / pivot
                out_ref[f, level if level is not None else levels - 1] = value
                new_parts[f] = value
        return tuple(new_ratios), tuple(new_parts)

    def forward(level, carry):
        below_mix, ratios, parts = carry
        mix = base_ref[level] + surf * decay_ref[level]
        ratios, parts = step(level, below_mix, mix, ratios, parts)
        return (mix, ratios, parts)

    carry = (zero, tuple(zero for _ in gains), tuple(zero for _ in range(fields)))
    last_mix, ratios, parts = lax.fori_loop(0, levels - 1, forward, carry)
    step(None, last_mix, zero, ratios, parts)

    def backward(i, later):
        level = levels - 2 - i
        result = []
        for gi in range(len(gains)):
            ratio = ratio_ref[gi, level]
            for f in groups[gi]:
                value = out_ref[f, level] + ratio * later[f]
                out_ref[f, level] = value
                result.append((f, value))
        result.sort(key=lambda item: item[0])
        return tuple(v for _, v in result)

    final = tuple(out_ref[f, levels - 1] for f in range(fields))
    lax.fori_loop(0, levels - 1, backward, final)
    land = land_ref[...]
    for f in range(fields):
        back_ref[f] = land * out_ref[f, 0]


def tridiagonal(pieces, mask, shape, mixing_base, surface, land):
    fields, levels = shape[0], shape[1]
    decay_table = np.array(
        [math.exp(-level / DEPTH_SCALE) for level in range(levels)], dtype=np.float32
    )
    vmem = pltpu.MemorySpace.VMEM
    return pl.pallas_call(
        tridiagonal_kernel,
        out_shape=(
            jax.ShapeDtypeStruct(shape, jnp.float32),
            jax.ShapeDtypeStruct((fields,) + shape[2:], jnp.float32),
        ),
        in_specs=[pl.BlockSpec(memory_space=pltpu.MemorySpace.SMEM)]
        + [pl.BlockSpec(memory_space=vmem)] * (len(pieces) + 4),
        out_specs=(pl.BlockSpec(memory_space=vmem), pl.BlockSpec(memory_space=vmem)),
        scratch_shapes=[
            pltpu.VMEM((len(set(FIELD_MIX)), levels) + shape[2:], jnp.float32),
            pltpu.VMEM((5,) + mask.shape, jnp.float32),
        ],
    )(jnp.asarray(decay_table), *pieces, mask, mixing_base, surface, land)


def split_three(values):
    high = values.astype(jnp.bfloat16)
    rest = values - high.astype(jnp.float32)
    middle = rest.astype(jnp.bfloat16)
    low = (rest - middle.astype(jnp.float32)).astype(jnp.bfloat16)
    return high, middle, low


def matmul_exact(parts, other, contract):
    numbers = (((1,), (contract,)), ((), ()))
    total = None
    for part in parts:
        product = lax.dot_general(part, other, numbers, preferred_element_type=jnp.float32)
        total = product if total is None else total + product
    return total


def gather_kernel(recv_ref, index_ref, weight_ref, *after_and_out):
    out_ref = after_and_out[-1]
    stacked, lanes = recv_ref.shape
    fields, rows, cols = out_ref.shape
    segments = stacked // fields
    items = index_ref.shape[0] // rows
    parts = split_three(recv_ref[...])
    lane_iota = lax.broadcasted_iota(jnp.int32, (lanes, cols), 0)
    segment_iota = lax.broadcasted_iota(jnp.int32, (fields, segments, cols), 1)

    def row_step(y, carry):
        total = None
        for item in range(items):
            index = index_ref[pl.ds(item * rows + y, 1), :]
            onehot = (lane_iota == index % lanes).astype(jnp.bfloat16)
            chosen = matmul_exact(parts, onehot, 0).reshape(fields, segments, cols)
            hit = segment_iota == (index // lanes)[None]
            picked = jnp.sum(jnp.where(hit, chosen, 0.0), axis=1)
            term = weight_ref[pl.ds(item * rows + y, 1), :] * picked
            total = term if total is None else total + term
        out_ref[:, pl.ds(y, 1), :] = total[:, None, :]
        return carry

    lax.fori_loop(0, rows, row_step, 0)


def scatter_kernel(back_ref, index_ref, weight_ref, out_ref):
    fields, rows, cols = back_ref.shape
    stacked, lanes = out_ref.shape
    segments = stacked // fields
    items = index_ref.shape[0] // rows
    lane_iota = lax.broadcasted_iota(jnp.int32, (lanes, cols), 0)
    segment_iota = lax.broadcasted_iota(jnp.int32, (fields, segments, cols), 1)

    def row_step(y, total):
        back = back_ref[:, pl.ds(y, 1), :]
        for item in range(items):
            index = index_ref[pl.ds(item * rows + y, 1), :]
            onehot = (lane_iota == index % lanes).astype(jnp.bfloat16)
            weighted = weight_ref[pl.ds(item * rows + y, 1), :][None] * back
            hit = segment_iota == (index // lanes)[None]
            spread = jnp.where(hit, weighted, 0.0).reshape(stacked, cols)
            total = total + matmul_exact(split_three(spread), onehot, 1)
        return total

    out_ref[...] = lax.fori_loop(0, rows, row_step, jnp.zeros((stacked, lanes), jnp.float32))


def remap_call(kernel, out_shape, *operands, after=()):
    vmem = pltpu.MemorySpace.VMEM
    return pl.pallas_call(
        kernel,
        out_shape=jax.ShapeDtypeStruct(out_shape, jnp.float32),
        in_specs=[pl.BlockSpec(memory_space=vmem)] * len(operands)
        + [pl.BlockSpec(memory_space=pl.ANY)] * len(after),
        out_specs=pl.BlockSpec(memory_space=vmem),
    )(*operands, *after)


def sum_over(values, axis):
    count = lax.axis_size(axis)
    if count & (count - 1):
        return lax.psum(values, axis)
    step = 1
    while step < count:
        pairs = [(i, i ^ step) for i in range(count)]
        values = values + lax.ppermute(values, axis, pairs)
        step *= 2
    return values


def lat_edges(marks, width):
    lat_count = lax.axis_size("lat")
    where_lat = lax.axis_index("lat")
    rows = lax.broadcasted_iota(jnp.int32, marks.shape, 0)
    keep_top = jnp.logical_or(where_lat > 0, rows >= width)
    keep_bottom = jnp.logical_or(where_lat < lat_count - 1, rows < marks.shape[0] - width)
    return jnp.where(jnp.logical_and(keep_top, keep_bottom), marks, 0.0)


def single_rim(values):
    return with_halo(values, (("lat", 2), ("lon", 3)), 1)


def shards(
    adjoint_state,
    mixing_base,
    atm_flux,
    send_count,
    send_segment,
    cover_index,
    cover_weight,
    land_mask,
):
    lat_count = lax.axis_size("lat")
    owned = atm_flux.shape[1]
    counts = send_count[0]
    capacity = send_segment.shape[1] // lat_count
    starts = jnp.cumsum(counts) - counts
    column = jnp.arange(capacity, dtype=jnp.int32)
    places = jnp.minimum(starts[:, None] + column[None, :], send_segment.shape[1] - 1)
    chosen = send_segment[0][places]
    live_slot = column[None, :] < counts[:, None]
    outgoing = atm_flux[:, chosen, :]
    received = lax.all_to_all(outgoing, "lat", split_axis=1, concat_axis=1, tiled=True)
    items, rows, cols = cover_index.shape
    fields = received.shape[0]
    flat_recv = received.reshape(-1, received.shape[-1])
    index_rows = cover_index.reshape(items * rows, cols)
    weight_rows = cover_weight.reshape(items * rows, cols)
    land = land_mask.astype(jnp.float32)
    *pieces, mask = extended_planes(adjoint_state, land_mask, HALO)
    forcing = remap_call(
        gather_kernel, (fields, rows, cols), flat_recv, index_rows, weight_rows, after=tuple(pieces[1:])
    )
    surface = WIND_GAIN * (forcing[2] * forcing[2] + forcing[3] * forcing[3]) + jax.nn.softplus(
        forcing[1] - forcing[0]
    )
    state_adjoint, flux_back = tridiagonal(pieces, mask, adjoint_state.shape, mixing_base, surface, land)
    buffer = remap_call(scatter_kernel, flat_recv.shape, flux_back, index_rows, weight_rows)
    returned = lax.all_to_all(
        buffer.reshape(received.shape), "lat", split_axis=1, concat_axis=1, tiled=True
    )
    kept = jnp.where(live_slot[None, :, :, None], returned, 0.0).reshape(4, -1, 128)
    owner_sum = jnp.zeros_like(atm_flux).at[:, chosen.reshape(-1), :].add(kept)
    flux_adjoint = sum_over(owner_sum, "lon")
    return (state_adjoint, flux_adjoint)


def solution(mesh):
    in_specs = (
        P(None, None, "lat", "lon"),
        P(None, "lat", "lon"),
        P(None, "lat", None),
        P("lat", "lon"),
        P("lat", "lon"),
        P(None, "lat", "lon"),
        P(None, "lat", "lon"),
        P("lat", "lon"),
    )
    out_specs = (P(None, None, "lat", "lon"), P(None, "lat", None))
    return jax.shard_map(shards, mesh=mesh, in_specs=in_specs, out_specs=out_specs, check_vma=False)
```

```python
import math

import jax
import jax.numpy as jnp
import numpy as np
from jax import lax
from jax.experimental import pallas as pl
from jax.experimental.pallas import tpu as pltpu
from jax.sharding import PartitionSpec as P

SMOOTHING = 0.02
WIND_GAIN = 1.0
DEPTH_SCALE = 12.0
FIELD_MIX = (1.0, 1.0, 2.0, 2.0)


HALO = 4


def from_neighbours(block, axis, dim, width):
    count = lax.axis_size(axis)
    to_prev = [(i, (i - 1) % count) for i in range(count)]
    to_next = [(i, (i + 1) % count) for i in range(count)]
    size = block.shape[dim]
    from_next = lax.ppermute(lax.slice_in_dim(block, 0, width, axis=dim), axis, to_prev)
    from_prev = lax.ppermute(lax.slice_in_dim(block, size - width, size, axis=dim), axis, to_next)
    return from_next, from_prev


def extended_planes(values, land_mask, width):
    fields, levels, rows, cols = values.shape
    planes = values.reshape(fields * levels, rows, cols)
    coast = land_mask.astype(jnp.float32)[None]
    stack = jnp.concatenate([planes, coast], axis=0)
    south, north = from_neighbours(stack, "lat", 1, width)
    east, west = from_neighbours(stack, "lon", 2, width)
    sides = jnp.concatenate([east, west], axis=2)
    corner_south, corner_north = from_neighbours(sides, "lat", 1, width)
    wide = -(-(2 * width) // 128) * 128
    edges = jnp.concatenate([sides, corner_south, corner_north], axis=1)
    gap = jnp.zeros(edges.shape[:2] + (wide - 2 * width,), jnp.float32)
    edge_tile = jnp.concatenate([edges[:, :, :width], gap, edges[:, :, width:]], axis=2)
    halo_rows = jnp.concatenate([south, north], axis=1)
    coast_plane = jnp.concatenate(
        [jnp.concatenate([stack[-1], halo_rows[-1]], axis=0), edge_tile[-1]], axis=1
    )
    lat_count = lax.axis_size("lat")
    where_lat = lax.axis_index("lat")
    row = lax.broadcasted_iota(jnp.int32, coast_plane.shape, 0)
    outside = jnp.logical_or(
        jnp.logical_and(where_lat == 0, row >= rows + width),
        jnp.logical_and(where_lat == lat_count - 1, jnp.logical_and(row >= rows, row < rows + width)),
    )
    mask = jnp.where(outside, 0.0, coast_plane)
    return planes, halo_rows, edge_tile, mask


def with_halo(block, sides, width):
    for axis, dim in sides:
        count = lax.axis_size(axis)
        forward = [(i, i + 1) for i in range(count - 1)]
        forward.append((count - 1, 0))
        backward = [(target, source) for source, target in forward]
        low = lax.ppermute(
            lax.slice_in_dim(block, block.shape[dim] - width, None, axis=dim), axis, forward
        )
        high = lax.ppermute(lax.slice_in_dim(block, 0, width, axis=dim), axis, backward)
        block = jnp.concatenate([low, block, high], axis=dim)
    return block


def laplace(values, marks):
    centre = values[..., 1:-1, 1:-1]
    north = marks[:-2, 1:-1] * (values[..., :-2, 1:-1] - centre)
    south = marks[2:, 1:-1] * (values[..., 2:, 1:-1] - centre)
    west = marks[1:-1, :-2] * (values[..., 1:-1, :-2] - centre)
    east = marks[1:-1, 2:] * (values[..., 1:-1, 2:] - centre)
    return marks[1:-1, 1:-1] * (north + south + west + east)


def tridiagonal_kernel(
    decay_ref, inner_ref, rows_ref, edge_ref, mask_ref, base_ref, surf_ref, land_ref,
    out_ref, back_ref, ratio_ref, marks_ref,
):
    fields, levels = out_ref.shape[0], out_ref.shape[1]
    rows, cols = out_ref.shape[2], out_ref.shape[3]
    tall, wide = mask_ref.shape
    marks = mask_ref[...]
    marks_ref[0] = marks * pltpu.roll(marks, 1, 0)
    marks_ref[1] = marks * pltpu.roll(marks, tall - 1, 0)
    marks_ref[2] = marks * pltpu.roll(marks, 1, 1)
    marks_ref[3] = marks * pltpu.roll(marks, wide - 1, 1)
    marks_ref[4] = (marks_ref[0] + marks_ref[1]) + (marks_ref[2] + marks_ref[3])

    def laplace_ext(values, inner=False):
        shifted = [
            pltpu.roll(values, 1, 0),
            pltpu.roll(values, tall - 1, 0),
            pltpu.roll(values, 1, 1),
            pltpu.roll(values, wide - 1, 1),
        ]
        if inner:
            shifted = [part[:rows, :cols] for part in shifted]
            values = values[:rows, :cols]
            weight = [marks_ref[i, :rows, :cols] for i in range(5)]
        else:
            weight = [marks_ref[i] for i in range(5)]
        vertical = weight[0] * shifted[0] + weight[1] * shifted[1]
        across = weight[2] * shifted[2] + weight[3] * shifted[3]
        return (vertical + across) - weight[4] * values

    def smoothed(f, level):
        plane = f * levels + level
        values = jnp.concatenate([inner_ref[plane], rows_ref[plane]], axis=0)
        values = jnp.concatenate([values, edge_ref[plane]], axis=1)
        inner = laplace_ext(values)
        values = values - SMOOTHING * laplace_ext(inner)
        inner = laplace_ext(values)
        return values[:rows, :cols] - SMOOTHING * laplace_ext(inner, inner=True)

    gains = sorted(set(FIELD_MIX))
    groups = [[f for f in range(fields) if FIELD_MIX[f] == g] for g in gains]
    surf = surf_ref[...]
    zero = jnp.zeros_like(surf)

    def step(level, below_mix, above_mix, ratios, parts):
        new_ratios, new_parts = [], list(parts)
        for gi, gain in enumerate(gains):
            below = gain * below_mix
            above = gain * above_mix
            pivot = ((1.0 + below) + above) - below * ratios[gi]
            scale = 1.0 / pivot
            if level is not None:
                ratio = above * scale
                ratio_ref[gi, level] = ratio
                new_ratios.append(ratio)
            for f in groups[gi]:
                value = (smoothed(f, level if level is not None else levels - 1) + below * parts[f]) * scale
                out_ref[f, level if level is not None else levels - 1] = value
                new_parts[f] = value
        return tuple(new_ratios), tuple(new_parts)

    def forward(level, carry):
        below_mix, ratios, parts = carry
        mix = base_ref[level] + surf * decay_ref[level]
        ratios, parts = step(level, below_mix, mix, ratios, parts)
        return (mix, ratios, parts)

    carry = (zero, tuple(zero for _ in gains), tuple(zero for _ in range(fields)))
    last_mix, ratios, parts = lax.fori_loop(0, levels - 1, forward, carry)
    step(None, last_mix, zero, ratios, parts)

    def backward(i, later):
        level = levels - 2 - i
        result = []
        for gi in range(len(gains)):
            ratio = ratio_ref[gi, level]
            for f in groups[gi]:
                value = out_ref[f, level] + ratio * later[f]
                out_ref[f, level] = value
                result.append((f, value))
        result.sort(key=lambda item: item[0])
        return tuple(v for _, v in result)

    final = tuple(out_ref[f, levels - 1] for f in range(fields))
    lax.fori_loop(0, levels - 1, backward, final)
    land = land_ref[...]
    for f in range(fields):
        back_ref[f] = land * out_ref[f, 0]


def tridiagonal(pieces, mask, shape, mixing_base, surface, land):
    fields, levels = shape[0], shape[1]
    decay_table = np.array(
        [math.exp(-level / DEPTH_SCALE) for level in range(levels)], dtype=np.float32
    )
    vmem = pltpu.MemorySpace.VMEM
    return pl.pallas_call(
        tridiagonal_kernel,
        out_shape=(
            jax.ShapeDtypeStruct(shape, jnp.float32),
            jax.ShapeDtypeStruct((fields,) + shape[2:], jnp.float32),
        ),
        in_specs=[pl.BlockSpec(memory_space=pltpu.MemorySpace.SMEM)]
        + [pl.BlockSpec(memory_space=vmem)] * (len(pieces) + 4),
        out_specs=(pl.BlockSpec(memory_space=vmem), pl.BlockSpec(memory_space=vmem)),
        scratch_shapes=[
            pltpu.VMEM((len(set(FIELD_MIX)), levels) + shape[2:], jnp.float32),
            pltpu.VMEM((5,) + mask.shape, jnp.float32),
        ],
    )(jnp.asarray(decay_table), *pieces, mask, mixing_base, surface, land)


def split_parts(values):
    high = values.astype(jnp.bfloat16)
    low = (values - high.astype(jnp.float32)).astype(jnp.bfloat16)
    return high, low


def matmul_exact(parts, other, contract):
    numbers = (((1,), (contract,)), ((), ()))
    total = None
    for part in parts:
        product = lax.dot_general(part, other, numbers, preferred_element_type=jnp.float32)
        total = product if total is None else total + product
    return total


def gather_kernel(recv_ref, index_ref, weight_ref, *after_and_out):
    out_ref = after_and_out[-1]
    stacked, lanes = recv_ref.shape
    fields, rows, cols = out_ref.shape
    segments = stacked // fields
    items = index_ref.shape[0] // rows
    parts = split_parts(recv_ref[...])
    lane_iota = lax.broadcasted_iota(jnp.int32, (lanes, cols), 0)
    segment_iota = lax.broadcasted_iota(jnp.int32, (fields, segments, cols), 1)

    def row_step(y, carry):
        total = None
        for item in range(items):
            index = index_ref[pl.ds(item * rows + y, 1), :]
            onehot = (lane_iota == index % lanes).astype(jnp.bfloat16)
            chosen = matmul_exact(parts, onehot, 0).reshape(fields, segments, cols)
            hit = segment_iota == (index // lanes)[None]
            picked = jnp.sum(jnp.where(hit, chosen, 0.0), axis=1)
            term = weight_ref[pl.ds(item * rows + y, 1), :] * picked
            total = term if total is None else total + term
        out_ref[:, pl.ds(y, 1), :] = total[:, None, :]
        return carry

    lax.fori_loop(0, rows, row_step, 0)


def scatter_kernel(back_ref, index_ref, weight_ref, out_ref):
    fields, rows, cols = back_ref.shape
    stacked, lanes = out_ref.shape
    segments = stacked // fields
    items = index_ref.shape[0] // rows
    lane_iota = lax.broadcasted_iota(jnp.int32, (lanes, cols), 0)
    segment_iota = lax.broadcasted_iota(jnp.int32, (fields, segments, cols), 1)

    def row_step(y, total):
        back = back_ref[:, pl.ds(y, 1), :]
        for item in range(items):
            index = index_ref[pl.ds(item * rows + y, 1), :]
            onehot = (lane_iota == index % lanes).astype(jnp.bfloat16)
            weighted = weight_ref[pl.ds(item * rows + y, 1), :][None] * back
            hit = segment_iota == (index // lanes)[None]
            spread = jnp.where(hit, weighted, 0.0).reshape(stacked, cols)
            total = total + matmul_exact(split_parts(spread), onehot, 1)
        return total

    out_ref[...] = lax.fori_loop(0, rows, row_step, jnp.zeros((stacked, lanes), jnp.float32))


def remap_call(kernel, out_shape, *operands, after=()):
    vmem = pltpu.MemorySpace.VMEM
    return pl.pallas_call(
        kernel,
        out_shape=jax.ShapeDtypeStruct(out_shape, jnp.float32),
        in_specs=[pl.BlockSpec(memory_space=vmem)] * len(operands)
        + [pl.BlockSpec(memory_space=pl.ANY)] * len(after),
        out_specs=pl.BlockSpec(memory_space=vmem),
    )(*operands, *after)


def sum_over(values, axis):
    count = lax.axis_size(axis)
    if count & (count - 1):
        return lax.psum(values, axis)
    step = 1
    while step < count:
        pairs = [(i, i ^ step) for i in range(count)]
        values = values + lax.ppermute(values, axis, pairs)
        step *= 2
    return values


def lat_edges(marks, width):
    lat_count = lax.axis_size("lat")
    where_lat = lax.axis_index("lat")
    rows = lax.broadcasted_iota(jnp.int32, marks.shape, 0)
    keep_top = jnp.logical_or(where_lat > 0, rows >= width)
    keep_bottom = jnp.logical_or(where_lat < lat_count - 1, rows < marks.shape[0] - width)
    return jnp.where(jnp.logical_and(keep_top, keep_bottom), marks, 0.0)


def single_rim(values):
    return with_halo(values, (("lat", 2), ("lon", 3)), 1)


def shards(
    adjoint_state,
    mixing_base,
    atm_flux,
    send_count,
    send_segment,
    cover_index,
    cover_weight,
    land_mask,
):
    lat_count = lax.axis_size("lat")
    owned = atm_flux.shape[1]
    counts = send_count[0]
    capacity = send_segment.shape[1] // lat_count
    starts = jnp.cumsum(counts) - counts
    column = jnp.arange(capacity, dtype=jnp.int32)
    places = jnp.minimum(starts[:, None] + column[None, :], send_segment.shape[1] - 1)
    chosen = send_segment[0][places]
    live_slot = column[None, :] < counts[:, None]
    outgoing = atm_flux[:, chosen, :]
    received = lax.all_to_all(outgoing, "lat", split_axis=1, concat_axis=1, tiled=True)
    items, rows, cols = cover_index.shape
    fields = received.shape[0]
    flat_recv = received.reshape(-1, received.shape[-1])
    index_rows = cover_index.reshape(items * rows, cols)
    weight_rows = cover_weight.reshape(items * rows, cols)
    land = land_mask.astype(jnp.float32)
    *pieces, mask = extended_planes(adjoint_state, land_mask, HALO)
    forcing = remap_call(
        gather_kernel, (fields, rows, cols), flat_recv, index_rows, weight_rows, after=tuple(pieces[1:])
    )
    surface = WIND_GAIN * (forcing[2] * forcing[2] + forcing[3] * forcing[3]) + jax.nn.softplus(
        forcing[1] - forcing[0]
    )
    state_adjoint, flux_back = tridiagonal(pieces, mask, adjoint_state.shape, mixing_base, surface, land)
    buffer = remap_call(scatter_kernel, flat_recv.shape, flux_back, index_rows, weight_rows)
    returned = lax.all_to_all(
        buffer.reshape(received.shape), "lat", split_axis=1, concat_axis=1, tiled=True
    )
    owned_ids = lax.broadcasted_iota(jnp.int32, (owned,) + chosen.shape, 0)
    picks = jnp.logical_and(owned_ids == chosen[None], live_slot[None]).astype(jnp.float32)
    owner_sum = jnp.einsum(
        "sdc,fdck->fsk", picks, returned, precision=lax.Precision.HIGHEST
    )
    flux_adjoint = sum_over(owner_sum, "lon")
    return (state_adjoint, flux_adjoint)


def solution(mesh):
    in_specs = (
        P(None, None, "lat", "lon"),
        P(None, "lat", "lon"),
        P(None, "lat", None),
        P("lat", "lon"),
        P("lat", "lon"),
        P(None, "lat", "lon"),
        P(None, "lat", "lon"),
        P("lat", "lon"),
    )
    out_specs = (P(None, None, "lat", "lon"), P(None, "lat", None))
    return jax.shard_map(shards, mesh=mesh, in_specs=in_specs, out_specs=out_specs, check_vma=False)
```

```python
import math

import jax
import jax.numpy as jnp
import numpy as np
from jax import lax
from jax.experimental import pallas as pl
from jax.experimental.pallas import tpu as pltpu
from jax.sharding import PartitionSpec as P

SMOOTHING = 0.02
WIND_GAIN = 1.0
DEPTH_SCALE = 12.0
FIELD_MIX = (1.0, 1.0, 2.0, 2.0)


HALO = 4


def from_neighbours(block, axis, dim, width):
    count = lax.axis_size(axis)
    to_prev = [(i, (i - 1) % count) for i in range(count)]
    to_next = [(i, (i + 1) % count) for i in range(count)]
    size = block.shape[dim]
    from_next = lax.ppermute(lax.slice_in_dim(block, 0, width, axis=dim), axis, to_prev)
    from_prev = lax.ppermute(lax.slice_in_dim(block, size - width, size, axis=dim), axis, to_next)
    return from_next, from_prev


def extended_planes(values, land_mask, width):
    fields, levels, rows, cols = values.shape
    planes = values.reshape(fields * levels, rows, cols)
    coast = land_mask.astype(jnp.float32)[None]
    stack = jnp.concatenate([planes, coast], axis=0)
    south, north = from_neighbours(stack, "lat", 1, width)
    east, west = from_neighbours(stack, "lon", 2, width)
    sides = jnp.concatenate([east, west], axis=2)
    corner_south, corner_north = from_neighbours(sides, "lat", 1, width)
    wide = -(-(2 * width) // 128) * 128
    edges = jnp.concatenate([sides, corner_south, corner_north], axis=1)
    gap = jnp.zeros(edges.shape[:2] + (wide - 2 * width,), jnp.float32)
    edge_tile = jnp.concatenate([edges[:, :, :width], gap, edges[:, :, width:]], axis=2)
    halo_rows = jnp.concatenate([south, north], axis=1)
    coast_plane = jnp.concatenate(
        [jnp.concatenate([stack[-1], halo_rows[-1]], axis=0), edge_tile[-1]], axis=1
    )
    lat_count = lax.axis_size("lat")
    where_lat = lax.axis_index("lat")
    row = lax.broadcasted_iota(jnp.int32, coast_plane.shape, 0)
    outside = jnp.logical_or(
        jnp.logical_and(where_lat == 0, row >= rows + width),
        jnp.logical_and(where_lat == lat_count - 1, jnp.logical_and(row >= rows, row < rows + width)),
    )
    mask = jnp.where(outside, 0.0, coast_plane)
    return planes, halo_rows, edge_tile, mask


def with_halo(block, sides, width):
    for axis, dim in sides:
        count = lax.axis_size(axis)
        forward = [(i, i + 1) for i in range(count - 1)]
        forward.append((count - 1, 0))
        backward = [(target, source) for source, target in forward]
        low = lax.ppermute(
            lax.slice_in_dim(block, block.shape[dim] - width, None, axis=dim), axis, forward
        )
        high = lax.ppermute(lax.slice_in_dim(block, 0, width, axis=dim), axis, backward)
        block = jnp.concatenate([low, block, high], axis=dim)
    return block


def laplace(values, marks):
    centre = values[..., 1:-1, 1:-1]
    north = marks[:-2, 1:-1] * (values[..., :-2, 1:-1] - centre)
    south = marks[2:, 1:-1] * (values[..., 2:, 1:-1] - centre)
    west = marks[1:-1, :-2] * (values[..., 1:-1, :-2] - centre)
    east = marks[1:-1, 2:] * (values[..., 1:-1, 2:] - centre)
    return marks[1:-1, 1:-1] * (north + south + west + east)


def tridiagonal_kernel(
    decay_ref, inner_ref, rows_ref, edge_ref, mask_ref, base_ref, surf_ref, land_ref,
    out_ref, back_ref, ratio_ref, marks_ref,
):
    fields, levels = out_ref.shape[0], out_ref.shape[1]
    rows, cols = out_ref.shape[2], out_ref.shape[3]
    tall, wide = mask_ref.shape
    marks = mask_ref[...]
    marks_ref[0] = marks * pltpu.roll(marks, 1, 0)
    marks_ref[1] = marks * pltpu.roll(marks, tall - 1, 0)
    marks_ref[2] = marks * pltpu.roll(marks, 1, 1)
    marks_ref[3] = marks * pltpu.roll(marks, wide - 1, 1)
    marks_ref[4] = (marks_ref[0] + marks_ref[1]) + (marks_ref[2] + marks_ref[3])

    def laplace_ext(values, inner=False):
        shifted = [
            pltpu.roll(values, 1, 0),
            pltpu.roll(values, tall - 1, 0),
            pltpu.roll(values, 1, 1),
            pltpu.roll(values, wide - 1, 1),
        ]
        if inner:
            shifted = [part[:rows, :cols] for part in shifted]
            values = values[:rows, :cols]
            weight = [marks_ref[i, :rows, :cols] for i in range(5)]
        else:
            weight = [marks_ref[i] for i in range(5)]
        vertical = weight[0] * shifted[0] + weight[1] * shifted[1]
        across = weight[2] * shifted[2] + weight[3] * shifted[3]
        return (vertical + across) - weight[4] * values

    def smoothed(f, level):
        plane = f * levels + level
        values = jnp.concatenate([inner_ref[plane], rows_ref[plane]], axis=0)
        values = jnp.concatenate([values, edge_ref[plane]], axis=1)
        inner = laplace_ext(values)
        values = values - SMOOTHING * laplace_ext(inner)
        inner = laplace_ext(values)
        return values[:rows, :cols] - SMOOTHING * laplace_ext(inner, inner=True)

    gains = sorted(set(FIELD_MIX))
    groups = [[f for f in range(fields) if FIELD_MIX[f] == g] for g in gains]
    surf = surf_ref[...]
    zero = jnp.zeros_like(surf)

    def step(level, below_mix, above_mix, ratios, parts):
        new_ratios, new_parts = [], list(parts)
        for gi, gain in enumerate(gains):
            below = gain * below_mix
            above = gain * above_mix
            pivot = ((1.0 + below) + above) - below * ratios[gi]
            scale = 1.0 / pivot
            if level is not None:
                ratio = above * scale
                ratio_ref[gi, level] = ratio
                new_ratios.append(ratio)
            for f in groups[gi]:
                value = (smoothed(f, level if level is not None else levels - 1) + below * parts[f]) * scale
                out_ref[f, level if level is not None else levels - 1] = value
                new_parts[f] = value
        return tuple(new_ratios), tuple(new_parts)

    def forward(level, carry):
        below_mix, ratios, parts = carry
        mix = base_ref[level] + surf * decay_ref[level]
        ratios, parts = step(level, below_mix, mix, ratios, parts)
        return (mix, ratios, parts)

    carry = (zero, tuple(zero for _ in gains), tuple(zero for _ in range(fields)))
    last_mix, ratios, parts = lax.fori_loop(0, levels - 1, forward, carry, unroll=2)
    step(None, last_mix, zero, ratios, parts)

    def backward(i, later):
        level = levels - 2 - i
        result = []
        for gi in range(len(gains)):
            ratio = ratio_ref[gi, level]
            for f in groups[gi]:
                value = out_ref[f, level] + ratio * later[f]
                out_ref[f, level] = value
                result.append((f, value))
        result.sort(key=lambda item: item[0])
        return tuple(v for _, v in result)

    final = tuple(out_ref[f, levels - 1] for f in range(fields))
    lax.fori_loop(0, levels - 1, backward, final, unroll=2)
    land = land_ref[...]
    for f in range(fields):
        back_ref[f] = land * out_ref[f, 0]


def tridiagonal(pieces, mask, shape, mixing_base, surface, land):
    fields, levels = shape[0], shape[1]
    decay_table = np.array(
        [math.exp(-level / DEPTH_SCALE) for level in range(levels)], dtype=np.float32
    )
    vmem = pltpu.MemorySpace.VMEM
    return pl.pallas_call(
        tridiagonal_kernel,
        out_shape=(
            jax.ShapeDtypeStruct(shape, jnp.float32),
            jax.ShapeDtypeStruct((fields,) + shape[2:], jnp.float32),
        ),
        in_specs=[pl.BlockSpec(memory_space=pltpu.MemorySpace.SMEM)]
        + [pl.BlockSpec(memory_space=vmem)] * (len(pieces) + 4),
        out_specs=(pl.BlockSpec(memory_space=vmem), pl.BlockSpec(memory_space=vmem)),
        scratch_shapes=[
            pltpu.VMEM((len(set(FIELD_MIX)), levels) + shape[2:], jnp.float32),
            pltpu.VMEM((5,) + mask.shape, jnp.float32),
        ],
    )(jnp.asarray(decay_table), *pieces, mask, mixing_base, surface, land)


def split_parts(values):
    high = values.astype(jnp.bfloat16)
    low = (values - high.astype(jnp.float32)).astype(jnp.bfloat16)
    return high, low


def matmul_exact(parts, other, contract):
    numbers = (((1,), (contract,)), ((), ()))
    total = None
    for part in parts:
        product = lax.dot_general(part, other, numbers, preferred_element_type=jnp.float32)
        total = product if total is None else total + product
    return total


def gather_kernel(recv_ref, index_ref, weight_ref, *after_and_out):
    out_ref = after_and_out[-1]
    stacked, lanes = recv_ref.shape
    fields, rows, cols = out_ref.shape
    segments = stacked // fields
    items = index_ref.shape[0] // rows
    parts = split_parts(recv_ref[...])
    lane_iota = lax.broadcasted_iota(jnp.int32, (lanes, cols), 0)
    segment_iota = lax.broadcasted_iota(jnp.int32, (fields, segments, cols), 1)

    def row_step(y, carry):
        total = None
        for item in range(items):
            index = index_ref[pl.ds(item * rows + y, 1), :]
            onehot = (lane_iota == index % lanes).astype(jnp.bfloat16)
            chosen = matmul_exact(parts, onehot, 0).reshape(fields, segments, cols)
            hit = segment_iota == (index // lanes)[None]
            picked = jnp.sum(jnp.where(hit, chosen, 0.0), axis=1)
            term = weight_ref[pl.ds(item * rows + y, 1), :] * picked
            total = term if total is None else total + term
        out_ref[:, pl.ds(y, 1), :] = total[:, None, :]
        return carry

    lax.fori_loop(0, rows, row_step, 0)


def scatter_kernel(back_ref, index_ref, weight_ref, out_ref):
    fields, rows, cols = back_ref.shape
    stacked, lanes = out_ref.shape
    segments = stacked // fields
    items = index_ref.shape[0] // rows
    lane_iota = lax.broadcasted_iota(jnp.int32, (lanes, cols), 0)
    segment_iota = lax.broadcasted_iota(jnp.int32, (fields, segments, cols), 1)

    def row_step(y, total):
        back = back_ref[:, pl.ds(y, 1), :]
        for item in range(items):
            index = index_ref[pl.ds(item * rows + y, 1), :]
            onehot = (lane_iota == index % lanes).astype(jnp.bfloat16)
            weighted = weight_ref[pl.ds(item * rows + y, 1), :][None] * back
            hit = segment_iota == (index // lanes)[None]
            spread = jnp.where(hit, weighted, 0.0).reshape(stacked, cols)
            total = total + matmul_exact(split_parts(spread), onehot, 1)
        return total

    out_ref[...] = lax.fori_loop(0, rows, row_step, jnp.zeros((stacked, lanes), jnp.float32))


def remap_call(kernel, out_shape, *operands, after=()):
    vmem = pltpu.MemorySpace.VMEM
    return pl.pallas_call(
        kernel,
        out_shape=jax.ShapeDtypeStruct(out_shape, jnp.float32),
        in_specs=[pl.BlockSpec(memory_space=vmem)] * len(operands)
        + [pl.BlockSpec(memory_space=pl.ANY)] * len(after),
        out_specs=pl.BlockSpec(memory_space=vmem),
    )(*operands, *after)


def sum_over(values, axis):
    count = lax.axis_size(axis)
    if count & (count - 1):
        return lax.psum(values, axis)
    step = 1
    while step < count:
        pairs = [(i, i ^ step) for i in range(count)]
        values = values + lax.ppermute(values, axis, pairs)
        step *= 2
    return values


def lat_edges(marks, width):
    lat_count = lax.axis_size("lat")
    where_lat = lax.axis_index("lat")
    rows = lax.broadcasted_iota(jnp.int32, marks.shape, 0)
    keep_top = jnp.logical_or(where_lat > 0, rows >= width)
    keep_bottom = jnp.logical_or(where_lat < lat_count - 1, rows < marks.shape[0] - width)
    return jnp.where(jnp.logical_and(keep_top, keep_bottom), marks, 0.0)


def single_rim(values):
    return with_halo(values, (("lat", 2), ("lon", 3)), 1)


def shards(
    adjoint_state,
    mixing_base,
    atm_flux,
    send_count,
    send_segment,
    cover_index,
    cover_weight,
    land_mask,
):
    lat_count = lax.axis_size("lat")
    owned = atm_flux.shape[1]
    counts = send_count[0]
    capacity = send_segment.shape[1] // lat_count
    starts = jnp.cumsum(counts) - counts
    column = jnp.arange(capacity, dtype=jnp.int32)
    places = jnp.minimum(starts[:, None] + column[None, :], send_segment.shape[1] - 1)
    chosen = send_segment[0][places]
    live_slot = column[None, :] < counts[:, None]
    outgoing = atm_flux[:, chosen, :]
    received = lax.all_to_all(outgoing, "lat", split_axis=1, concat_axis=1, tiled=True)
    items, rows, cols = cover_index.shape
    fields = received.shape[0]
    flat_recv = received.reshape(-1, received.shape[-1])
    index_rows = cover_index.reshape(items * rows, cols)
    weight_rows = cover_weight.reshape(items * rows, cols)
    land = land_mask.astype(jnp.float32)
    *pieces, mask = extended_planes(adjoint_state, land_mask, HALO)
    forcing = remap_call(
        gather_kernel, (fields, rows, cols), flat_recv, index_rows, weight_rows, after=tuple(pieces[1:])
    )
    surface = WIND_GAIN * (forcing[2] * forcing[2] + forcing[3] * forcing[3]) + jax.nn.softplus(
        forcing[1] - forcing[0]
    )
    state_adjoint, flux_back = tridiagonal(pieces, mask, adjoint_state.shape, mixing_base, surface, land)
    buffer = remap_call(scatter_kernel, flat_recv.shape, flux_back, index_rows, weight_rows)
    returned = lax.all_to_all(
        buffer.reshape(received.shape), "lat", split_axis=1, concat_axis=1, tiled=True
    )
    owned_ids = lax.broadcasted_iota(jnp.int32, (owned,) + chosen.shape, 0)
    picks = jnp.logical_and(owned_ids == chosen[None], live_slot[None]).astype(jnp.float32)
    owner_sum = jnp.einsum(
        "sdc,fdck->fsk", picks, returned, precision=lax.Precision.HIGHEST
    )
    flux_adjoint = sum_over(owner_sum, "lon")
    return (state_adjoint, flux_adjoint)


def solution(mesh):
    in_specs = (
        P(None, None, "lat", "lon"),
        P(None, "lat", "lon"),
        P(None, "lat", None),
        P("lat", "lon"),
        P("lat", "lon"),
        P(None, "lat", "lon"),
        P(None, "lat", "lon"),
        P("lat", "lon"),
    )
    out_specs = (P(None, None, "lat", "lon"), P(None, "lat", None))
    return jax.shard_map(shards, mesh=mesh, in_specs=in_specs, out_specs=out_specs, check_vma=False)
```

```python
import math

import jax
import jax.numpy as jnp
import numpy as np
from jax import lax
from jax.experimental import pallas as pl
from jax.experimental.pallas import tpu as pltpu
from jax.sharding import PartitionSpec as P

SMOOTHING = 0.02
WIND_GAIN = 1.0
DEPTH_SCALE = 12.0
FIELD_MIX = (1.0, 1.0, 2.0, 2.0)


HALO = 4


def from_neighbours(block, axis, dim, width):
    count = lax.axis_size(axis)
    to_prev = [(i, (i - 1) % count) for i in range(count)]
    to_next = [(i, (i + 1) % count) for i in range(count)]
    size = block.shape[dim]
    from_next = lax.ppermute(lax.slice_in_dim(block, 0, width, axis=dim), axis, to_prev)
    from_prev = lax.ppermute(lax.slice_in_dim(block, size - width, size, axis=dim), axis, to_next)
    return from_next, from_prev


def extended_planes(values, land_mask, width):
    fields, levels, rows, cols = values.shape
    planes = values.reshape(fields * levels, rows, cols)
    coast = land_mask.astype(jnp.float32)[None]
    stack = jnp.concatenate([planes, coast], axis=0)
    south, north = from_neighbours(stack, "lat", 1, width)
    east, west = from_neighbours(stack, "lon", 2, width)
    sides = jnp.concatenate([east, west], axis=2)
    corner_south, corner_north = from_neighbours(sides, "lat", 1, width)
    wide = -(-(2 * width) // 128) * 128
    edges = jnp.concatenate([sides, corner_south, corner_north], axis=1)
    gap = jnp.zeros(edges.shape[:2] + (wide - 2 * width,), jnp.float32)
    edge_tile = jnp.concatenate([edges[:, :, :width], gap, edges[:, :, width:]], axis=2)
    halo_rows = jnp.concatenate([south, north], axis=1)
    coast_plane = jnp.concatenate(
        [jnp.concatenate([stack[-1], halo_rows[-1]], axis=0), edge_tile[-1]], axis=1
    )
    lat_count = lax.axis_size("lat")
    where_lat = lax.axis_index("lat")
    row = lax.broadcasted_iota(jnp.int32, coast_plane.shape, 0)
    outside = jnp.logical_or(
        jnp.logical_and(where_lat == 0, row >= rows + width),
        jnp.logical_and(where_lat == lat_count - 1, jnp.logical_and(row >= rows, row < rows + width)),
    )
    mask = jnp.where(outside, 0.0, coast_plane)
    return planes, halo_rows, edge_tile, mask


def with_halo(block, sides, width):
    for axis, dim in sides:
        count = lax.axis_size(axis)
        forward = [(i, i + 1) for i in range(count - 1)]
        forward.append((count - 1, 0))
        backward = [(target, source) for source, target in forward]
        low = lax.ppermute(
            lax.slice_in_dim(block, block.shape[dim] - width, None, axis=dim), axis, forward
        )
        high = lax.ppermute(lax.slice_in_dim(block, 0, width, axis=dim), axis, backward)
        block = jnp.concatenate([low, block, high], axis=dim)
    return block


def laplace(values, marks):
    centre = values[..., 1:-1, 1:-1]
    north = marks[:-2, 1:-1] * (values[..., :-2, 1:-1] - centre)
    south = marks[2:, 1:-1] * (values[..., 2:, 1:-1] - centre)
    west = marks[1:-1, :-2] * (values[..., 1:-1, :-2] - centre)
    east = marks[1:-1, 2:] * (values[..., 1:-1, 2:] - centre)
    return marks[1:-1, 1:-1] * (north + south + west + east)


def tridiagonal_kernel(
    decay_ref, inner_ref, rows_ref, edge_ref, mask_ref, base_ref, surf_ref, land_ref,
    out_ref, back_ref, ratio_ref, marks_ref,
):
    fields, levels = out_ref.shape[0], out_ref.shape[1]
    rows, cols = out_ref.shape[2], out_ref.shape[3]
    tall, wide = mask_ref.shape
    marks = mask_ref[...]
    marks_ref[0] = marks * pltpu.roll(marks, 1, 0)
    marks_ref[1] = marks * pltpu.roll(marks, tall - 1, 0)
    marks_ref[2] = marks * pltpu.roll(marks, 1, 1)
    marks_ref[3] = marks * pltpu.roll(marks, wide - 1, 1)
    marks_ref[4] = (marks_ref[0] + marks_ref[1]) + (marks_ref[2] + marks_ref[3])

    def laplace_ext(values, inner=False):
        shifted = [
            pltpu.roll(values, 1, 0),
            pltpu.roll(values, tall - 1, 0),
            pltpu.roll(values, 1, 1),
            pltpu.roll(values, wide - 1, 1),
        ]
        if inner:
            shifted = [part[:rows, :cols] for part in shifted]
            values = values[:rows, :cols]
            weight = [marks_ref[i, :rows, :cols] for i in range(5)]
        else:
            weight = [marks_ref[i] for i in range(5)]
        vertical = weight[0] * shifted[0] + weight[1] * shifted[1]
        across = weight[2] * shifted[2] + weight[3] * shifted[3]
        return (vertical + across) - weight[4] * values

    def smoothed(f, level):
        plane = f * levels + level
        values = jnp.concatenate([inner_ref[plane], rows_ref[plane]], axis=0)
        values = jnp.concatenate([values, edge_ref[plane]], axis=1)
        inner = laplace_ext(values)
        values = values - SMOOTHING * laplace_ext(inner)
        inner = laplace_ext(values)
        return values[:rows, :cols] - SMOOTHING * laplace_ext(inner, inner=True)

    gains = sorted(set(FIELD_MIX))
    groups = [[f for f in range(fields) if FIELD_MIX[f] == g] for g in gains]
    surf = surf_ref[...]
    zero = jnp.zeros_like(surf)

    def step(level, below_mix, above_mix, ratios, parts):
        new_ratios, new_parts = [], list(parts)
        for gi, gain in enumerate(gains):
            below = gain * below_mix
            above = gain * above_mix
            pivot = ((1.0 + below) + above) - below * ratios[gi]
            scale = 1.0 / pivot
            if level is not None:
                ratio = above * scale
                ratio_ref[gi, level] = ratio
                new_ratios.append(ratio)
            for f in groups[gi]:
                value = (out_ref[f, level if level is not None else levels - 1] + below * parts[f]) * scale
                out_ref[f, level if level is not None else levels - 1] = value
                new_parts[f] = value
        return tuple(new_ratios), tuple(new_parts)

    def forward(level, carry):
        below_mix, ratios, parts = carry
        mix = base_ref[level] + surf * decay_ref[level]
        ratios, parts = step(level, below_mix, mix, ratios, parts)
        return (mix, ratios, parts)

    def smooth_plane(plane, carry):
        f = plane // levels
        level = plane % levels
        out_ref[f, level] = smoothed(f, level)
        return carry

    lax.fori_loop(0, fields * levels, smooth_plane, 0)
    carry = (zero, tuple(zero for _ in gains), tuple(zero for _ in range(fields)))
    last_mix, ratios, parts = lax.fori_loop(0, levels - 1, forward, carry)
    step(None, last_mix, zero, ratios, parts)

    def backward(i, later):
        level = levels - 2 - i
        result = []
        for gi in range(len(gains)):
            ratio = ratio_ref[gi, level]
            for f in groups[gi]:
                value = out_ref[f, level] + ratio * later[f]
                out_ref[f, level] = value
                result.append((f, value))
        result.sort(key=lambda item: item[0])
        return tuple(v for _, v in result)

    final = tuple(out_ref[f, levels - 1] for f in range(fields))
    lax.fori_loop(0, levels - 1, backward, final)
    land = land_ref[...]
    for f in range(fields):
        back_ref[f] = land * out_ref[f, 0]


def tridiagonal(pieces, mask, shape, mixing_base, surface, land):
    fields, levels = shape[0], shape[1]
    decay_table = np.array(
        [math.exp(-level / DEPTH_SCALE) for level in range(levels)], dtype=np.float32
    )
    vmem = pltpu.MemorySpace.VMEM
    return pl.pallas_call(
        tridiagonal_kernel,
        out_shape=(
            jax.ShapeDtypeStruct(shape, jnp.float32),
            jax.ShapeDtypeStruct((fields,) + shape[2:], jnp.float32),
        ),
        in_specs=[pl.BlockSpec(memory_space=pltpu.MemorySpace.SMEM)]
        + [pl.BlockSpec(memory_space=vmem)] * (len(pieces) + 4),
        out_specs=(pl.BlockSpec(memory_space=vmem), pl.BlockSpec(memory_space=vmem)),
        scratch_shapes=[
            pltpu.VMEM((len(set(FIELD_MIX)), levels) + shape[2:], jnp.float32),
            pltpu.VMEM((5,) + mask.shape, jnp.float32),
        ],
    )(jnp.asarray(decay_table), *pieces, mask, mixing_base, surface, land)


def split_parts(values):
    high = values.astype(jnp.bfloat16)
    low = (values - high.astype(jnp.float32)).astype(jnp.bfloat16)
    return high, low


def matmul_exact(parts, other, contract):
    numbers = (((1,), (contract,)), ((), ()))
    total = None
    for part in parts:
        product = lax.dot_general(part, other, numbers, preferred_element_type=jnp.float32)
        total = product if total is None else total + product
    return total


def gather_kernel(recv_ref, index_ref, weight_ref, *after_and_out):
    out_ref = after_and_out[-1]
    stacked, lanes = recv_ref.shape
    fields, rows, cols = out_ref.shape
    segments = stacked // fields
    items = index_ref.shape[0] // rows
    parts = split_parts(recv_ref[...])
    lane_iota = lax.broadcasted_iota(jnp.int32, (lanes, cols), 0)
    segment_iota = lax.broadcasted_iota(jnp.int32, (fields, segments, cols), 1)

    def row_step(y, carry):
        total = None
        for item in range(items):
            index = index_ref[pl.ds(item * rows + y, 1), :]
            onehot = (lane_iota == index % lanes).astype(jnp.bfloat16)
            chosen = matmul_exact(parts, onehot, 0).reshape(fields, segments, cols)
            hit = segment_iota == (index // lanes)[None]
            picked = jnp.sum(jnp.where(hit, chosen, 0.0), axis=1)
            term = weight_ref[pl.ds(item * rows + y, 1), :] * picked
            total = term if total is None else total + term
        out_ref[:, pl.ds(y, 1), :] = total[:, None, :]
        return carry

    lax.fori_loop(0, rows, row_step, 0)


def scatter_kernel(back_ref, index_ref, weight_ref, out_ref):
    fields, rows, cols = back_ref.shape
    stacked, lanes = out_ref.shape
    segments = stacked // fields
    items = index_ref.shape[0] // rows
    lane_iota = lax.broadcasted_iota(jnp.int32, (lanes, cols), 0)
    segment_iota = lax.broadcasted_iota(jnp.int32, (fields, segments, cols), 1)

    def row_step(y, total):
        back = back_ref[:, pl.ds(y, 1), :]
        for item in range(items):
            index = index_ref[pl.ds(item * rows + y, 1), :]
            onehot = (lane_iota == index % lanes).astype(jnp.bfloat16)
            weighted = weight_ref[pl.ds(item * rows + y, 1), :][None] * back
            hit = segment_iota == (index // lanes)[None]
            spread = jnp.where(hit, weighted, 0.0).reshape(stacked, cols)
            total = total + matmul_exact(split_parts(spread), onehot, 1)
        return total

    out_ref[...] = lax.fori_loop(0, rows, row_step, jnp.zeros((stacked, lanes), jnp.float32))


def remap_call(kernel, out_shape, *operands, after=()):
    vmem = pltpu.MemorySpace.VMEM
    return pl.pallas_call(
        kernel,
        out_shape=jax.ShapeDtypeStruct(out_shape, jnp.float32),
        in_specs=[pl.BlockSpec(memory_space=vmem)] * len(operands)
        + [pl.BlockSpec(memory_space=pl.ANY)] * len(after),
        out_specs=pl.BlockSpec(memory_space=vmem),
    )(*operands, *after)


def sum_over(values, axis):
    count = lax.axis_size(axis)
    if count & (count - 1):
        return lax.psum(values, axis)
    step = 1
    while step < count:
        pairs = [(i, i ^ step) for i in range(count)]
        values = values + lax.ppermute(values, axis, pairs)
        step *= 2
    return values


def lat_edges(marks, width):
    lat_count = lax.axis_size("lat")
    where_lat = lax.axis_index("lat")
    rows = lax.broadcasted_iota(jnp.int32, marks.shape, 0)
    keep_top = jnp.logical_or(where_lat > 0, rows >= width)
    keep_bottom = jnp.logical_or(where_lat < lat_count - 1, rows < marks.shape[0] - width)
    return jnp.where(jnp.logical_and(keep_top, keep_bottom), marks, 0.0)


def single_rim(values):
    return with_halo(values, (("lat", 2), ("lon", 3)), 1)


def shards(
    adjoint_state,
    mixing_base,
    atm_flux,
    send_count,
    send_segment,
    cover_index,
    cover_weight,
    land_mask,
):
    lat_count = lax.axis_size("lat")
    owned = atm_flux.shape[1]
    counts = send_count[0]
    capacity = send_segment.shape[1] // lat_count
    starts = jnp.cumsum(counts) - counts
    column = jnp.arange(capacity, dtype=jnp.int32)
    places = jnp.minimum(starts[:, None] + column[None, :], send_segment.shape[1] - 1)
    chosen = send_segment[0][places]
    live_slot = column[None, :] < counts[:, None]
    outgoing = atm_flux[:, chosen, :]
    received = lax.all_to_all(outgoing, "lat", split_axis=1, concat_axis=1, tiled=True)
    items, rows, cols = cover_index.shape
    fields = received.shape[0]
    flat_recv = received.reshape(-1, received.shape[-1])
    index_rows = cover_index.reshape(items * rows, cols)
    weight_rows = cover_weight.reshape(items * rows, cols)
    land = land_mask.astype(jnp.float32)
    *pieces, mask = extended_planes(adjoint_state, land_mask, HALO)
    forcing = remap_call(
        gather_kernel, (fields, rows, cols), flat_recv, index_rows, weight_rows, after=tuple(pieces[1:])
    )
    surface = WIND_GAIN * (forcing[2] * forcing[2] + forcing[3] * forcing[3]) + jax.nn.softplus(
        forcing[1] - forcing[0]
    )
    state_adjoint, flux_back = tridiagonal(pieces, mask, adjoint_state.shape, mixing_base, surface, land)
    buffer = remap_call(scatter_kernel, flat_recv.shape, flux_back, index_rows, weight_rows)
    returned = lax.all_to_all(
        buffer.reshape(received.shape), "lat", split_axis=1, concat_axis=1, tiled=True
    )
    owned_ids = lax.broadcasted_iota(jnp.int32, (owned,) + chosen.shape, 0)
    picks = jnp.logical_and(owned_ids == chosen[None], live_slot[None]).astype(jnp.float32)
    owner_sum = jnp.einsum(
        "sdc,fdck->fsk", picks, returned, precision=lax.Precision.HIGHEST
    )
    flux_adjoint = sum_over(owner_sum, "lon")
    return (state_adjoint, flux_adjoint)


def solution(mesh):
    in_specs = (
        P(None, None, "lat", "lon"),
        P(None, "lat", "lon"),
        P(None, "lat", None),
        P("lat", "lon"),
        P("lat", "lon"),
        P(None, "lat", "lon"),
        P(None, "lat", "lon"),
        P("lat", "lon"),
    )
    out_specs = (P(None, None, "lat", "lon"), P(None, "lat", None))
    return jax.shard_map(shards, mesh=mesh, in_specs=in_specs, out_specs=out_specs, check_vma=False)
```

```python
import math

import jax
import jax.numpy as jnp
import numpy as np
from jax import lax
from jax.experimental import pallas as pl
from jax.experimental.pallas import tpu as pltpu
from jax.sharding import PartitionSpec as P

SMOOTHING = 0.02
WIND_GAIN = 1.0
DEPTH_SCALE = 12.0
FIELD_MIX = (1.0, 1.0, 2.0, 2.0)


HALO = 4


def from_neighbours(block, axis, dim, width):
    count = lax.axis_size(axis)
    to_prev = [(i, (i - 1) % count) for i in range(count)]
    to_next = [(i, (i + 1) % count) for i in range(count)]
    size = block.shape[dim]
    from_next = lax.ppermute(lax.slice_in_dim(block, 0, width, axis=dim), axis, to_prev)
    from_prev = lax.ppermute(lax.slice_in_dim(block, size - width, size, axis=dim), axis, to_next)
    return from_next, from_prev


def extended_planes(values, land_mask, width):
    fields, levels, rows, cols = values.shape
    planes = values.reshape(fields * levels, rows, cols)
    coast = land_mask.astype(jnp.float32)[None]
    stack = jnp.concatenate([planes, coast], axis=0)
    south, north = from_neighbours(stack, "lat", 1, width)
    east, west = from_neighbours(stack, "lon", 2, width)
    sides = jnp.concatenate([east, west], axis=2)
    corner_south, corner_north = from_neighbours(sides, "lat", 1, width)
    wide = -(-(2 * width) // 128) * 128
    edges = jnp.concatenate([sides, corner_south, corner_north], axis=1)
    gap = jnp.zeros(edges.shape[:2] + (wide - 2 * width,), jnp.float32)
    edge_tile = jnp.concatenate([edges[:, :, :width], gap, edges[:, :, width:]], axis=2)
    halo_rows = jnp.concatenate([south, north], axis=1)
    coast_plane = jnp.concatenate(
        [jnp.concatenate([stack[-1], halo_rows[-1]], axis=0), edge_tile[-1]], axis=1
    )
    lat_count = lax.axis_size("lat")
    where_lat = lax.axis_index("lat")
    row = lax.broadcasted_iota(jnp.int32, coast_plane.shape, 0)
    outside = jnp.logical_or(
        jnp.logical_and(where_lat == 0, row >= rows + width),
        jnp.logical_and(where_lat == lat_count - 1, jnp.logical_and(row >= rows, row < rows + width)),
    )
    mask = jnp.where(outside, 0.0, coast_plane)
    return planes, halo_rows, edge_tile, mask


def with_halo(block, sides, width):
    for axis, dim in sides:
        count = lax.axis_size(axis)
        forward = [(i, i + 1) for i in range(count - 1)]
        forward.append((count - 1, 0))
        backward = [(target, source) for source, target in forward]
        low = lax.ppermute(
            lax.slice_in_dim(block, block.shape[dim] - width, None, axis=dim), axis, forward
        )
        high = lax.ppermute(lax.slice_in_dim(block, 0, width, axis=dim), axis, backward)
        block = jnp.concatenate([low, block, high], axis=dim)
    return block


def laplace(values, marks):
    centre = values[..., 1:-1, 1:-1]
    north = marks[:-2, 1:-1] * (values[..., :-2, 1:-1] - centre)
    south = marks[2:, 1:-1] * (values[..., 2:, 1:-1] - centre)
    west = marks[1:-1, :-2] * (values[..., 1:-1, :-2] - centre)
    east = marks[1:-1, 2:] * (values[..., 1:-1, 2:] - centre)
    return marks[1:-1, 1:-1] * (north + south + west + east)


def tridiagonal_kernel(
    decay_ref, inner_ref, rows_ref, edge_ref, mask_ref, base_ref, surf_ref, land_ref,
    out_ref, back_ref, ratio_ref, marks_ref,
):
    fields, levels = out_ref.shape[0], out_ref.shape[1]
    rows, cols = out_ref.shape[2], out_ref.shape[3]
    tall, wide = mask_ref.shape
    marks = mask_ref[...]
    marks_ref[0] = marks * pltpu.roll(marks, 1, 0)
    marks_ref[1] = marks * pltpu.roll(marks, tall - 1, 0)
    marks_ref[2] = marks * pltpu.roll(marks, 1, 1)
    marks_ref[3] = marks * pltpu.roll(marks, wide - 1, 1)
    marks_ref[4] = (marks_ref[0] + marks_ref[1]) + (marks_ref[2] + marks_ref[3])

    def laplace_ext(values, inner=False):
        shifted = [
            pltpu.roll(values, 1, 0),
            pltpu.roll(values, tall - 1, 0),
            pltpu.roll(values, 1, 1),
            pltpu.roll(values, wide - 1, 1),
        ]
        if inner:
            shifted = [part[:rows, :cols] for part in shifted]
            values = values[:rows, :cols]
            weight = [marks_ref[i, :rows, :cols] for i in range(5)]
        else:
            weight = [marks_ref[i] for i in range(5)]
        vertical = weight[0] * shifted[0] + weight[1] * shifted[1]
        across = weight[2] * shifted[2] + weight[3] * shifted[3]
        return (vertical + across) - weight[4] * values

    def smoothed(f, level):
        plane = f * levels + level
        values = jnp.concatenate([inner_ref[plane], rows_ref[plane]], axis=0)
        values = jnp.concatenate([values, edge_ref[plane]], axis=1)
        inner = laplace_ext(values)
        values = values - SMOOTHING * laplace_ext(inner)
        inner = laplace_ext(values)
        return values[:rows, :cols] - SMOOTHING * laplace_ext(inner, inner=True)

    gains = sorted(set(FIELD_MIX))
    groups = [[f for f in range(fields) if FIELD_MIX[f] == g] for g in gains]
    surf = surf_ref[...]
    zero = jnp.zeros_like(surf)

    def step(level, below_mix, above_mix, ratios, parts, sources):
        new_ratios, new_parts = [], list(parts)
        for gi, gain in enumerate(gains):
            below = gain * below_mix
            above = gain * above_mix
            pivot = ((1.0 + below) + above) - below * ratios[gi]
            scale = 1.0 / pivot
            if level is not None:
                ratio = above * scale
                ratio_ref[gi, level] = ratio
                new_ratios.append(ratio)
            for f in groups[gi]:
                value = (sources[f] + below * parts[f]) * scale
                out_ref[f, level if level is not None else levels - 1] = value
                new_parts[f] = value
        return tuple(new_ratios), tuple(new_parts)

    def forward(level, carry):
        below_mix, ratios, parts, sources = carry
        upcoming = tuple(smoothed(f, level + 1) for f in range(fields))
        mix = base_ref[level] + surf * decay_ref[level]
        ratios, parts = step(level, below_mix, mix, ratios, parts, sources)
        return (mix, ratios, parts, upcoming)

    first = tuple(smoothed(f, 0) for f in range(fields))
    carry = (zero, tuple(zero for _ in gains), tuple(zero for _ in range(fields)), first)
    last_mix, ratios, parts, sources = lax.fori_loop(0, levels - 1, forward, carry)
    step(None, last_mix, zero, ratios, parts, sources)

    def backward(i, later):
        level = levels - 2 - i
        result = []
        for gi in range(len(gains)):
            ratio = ratio_ref[gi, level]
            for f in groups[gi]:
                value = out_ref[f, level] + ratio * later[f]
                out_ref[f, level] = value
                result.append((f, value))
        result.sort(key=lambda item: item[0])
        return tuple(v for _, v in result)

    final = tuple(out_ref[f, levels - 1] for f in range(fields))
    lax.fori_loop(0, levels - 1, backward, final)
    land = land_ref[...]
    for f in range(fields):
        back_ref[f] = land * out_ref[f, 0]


def tridiagonal(pieces, mask, shape, mixing_base, surface, land):
    fields, levels = shape[0], shape[1]
    decay_table = np.array(
        [math.exp(-level / DEPTH_SCALE) for level in range(levels)], dtype=np.float32
    )
    vmem = pltpu.MemorySpace.VMEM
    return pl.pallas_call(
        tridiagonal_kernel,
        out_shape=(
            jax.ShapeDtypeStruct(shape, jnp.float32),
            jax.ShapeDtypeStruct((fields,) + shape[2:], jnp.float32),
        ),
        in_specs=[pl.BlockSpec(memory_space=pltpu.MemorySpace.SMEM)]
        + [pl.BlockSpec(memory_space=vmem)] * (len(pieces) + 4),
        out_specs=(pl.BlockSpec(memory_space=vmem), pl.BlockSpec(memory_space=vmem)),
        scratch_shapes=[
            pltpu.VMEM((len(set(FIELD_MIX)), levels) + shape[2:], jnp.float32),
            pltpu.VMEM((5,) + mask.shape, jnp.float32),
        ],
    )(jnp.asarray(decay_table), *pieces, mask, mixing_base, surface, land)


def split_parts(values):
    high = values.astype(jnp.bfloat16)
    low = (values - high.astype(jnp.float32)).astype(jnp.bfloat16)
    return high, low


def matmul_exact(parts, other, contract):
    numbers = (((1,), (contract,)), ((), ()))
    total = None
    for part in parts:
        product = lax.dot_general(part, other, numbers, preferred_element_type=jnp.float32)
        total = product if total is None else total + product
    return total


def gather_kernel(recv_ref, index_ref, weight_ref, *after_and_out):
    out_ref = after_and_out[-1]
    stacked, lanes = recv_ref.shape
    fields, rows, cols = out_ref.shape
    segments = stacked // fields
    items = index_ref.shape[0] // rows
    parts = split_parts(recv_ref[...])
    lane_iota = lax.broadcasted_iota(jnp.int32, (lanes, cols), 0)
    segment_iota = lax.broadcasted_iota(jnp.int32, (fields, segments, cols), 1)

    def row_step(y, carry):
        total = None
        for item in range(items):
            index = index_ref[pl.ds(item * rows + y, 1), :]
            onehot = (lane_iota == index % lanes).astype(jnp.bfloat16)
            chosen = matmul_exact(parts, onehot, 0).reshape(fields, segments, cols)
            hit = segment_iota == (index // lanes)[None]
            picked = jnp.sum(jnp.where(hit, chosen, 0.0), axis=1)
            term = weight_ref[pl.ds(item * rows + y, 1), :] * picked
            total = term if total is None else total + term
        out_ref[:, pl.ds(y, 1), :] = total[:, None, :]
        return carry

    lax.fori_loop(0, rows, row_step, 0)


def scatter_kernel(back_ref, index_ref, weight_ref, out_ref):
    fields, rows, cols = back_ref.shape
    stacked, lanes = out_ref.shape
    segments = stacked // fields
    items = index_ref.shape[0] // rows
    lane_iota = lax.broadcasted_iota(jnp.int32, (lanes, cols), 0)
    segment_iota = lax.broadcasted_iota(jnp.int32, (fields, segments, cols), 1)

    def row_step(y, total):
        back = back_ref[:, pl.ds(y, 1), :]
        for item in range(items):
            index = index_ref[pl.ds(item * rows + y, 1), :]
            onehot = (lane_iota == index % lanes).astype(jnp.bfloat16)
            weighted = weight_ref[pl.ds(item * rows + y, 1), :][None] * back
            hit = segment_iota == (index // lanes)[None]
            spread = jnp.where(hit, weighted, 0.0).reshape(stacked, cols)
            total = total + matmul_exact(split_parts(spread), onehot, 1)
        return total

    out_ref[...] = lax.fori_loop(0, rows, row_step, jnp.zeros((stacked, lanes), jnp.float32))


def remap_call(kernel, out_shape, *operands, after=()):
    vmem = pltpu.MemorySpace.VMEM
    return pl.pallas_call(
        kernel,
        out_shape=jax.ShapeDtypeStruct(out_shape, jnp.float32),
        in_specs=[pl.BlockSpec(memory_space=vmem)] * len(operands)
        + [pl.BlockSpec(memory_space=pl.ANY)] * len(after),
        out_specs=pl.BlockSpec(memory_space=vmem),
    )(*operands, *after)


def sum_over(values, axis):
    count = lax.axis_size(axis)
    if count & (count - 1):
        return lax.psum(values, axis)
    step = 1
    while step < count:
        pairs = [(i, i ^ step) for i in range(count)]
        values = values + lax.ppermute(values, axis, pairs)
        step *= 2
    return values


def lat_edges(marks, width):
    lat_count = lax.axis_size("lat")
    where_lat = lax.axis_index("lat")
    rows = lax.broadcasted_iota(jnp.int32, marks.shape, 0)
    keep_top = jnp.logical_or(where_lat > 0, rows >= width)
    keep_bottom = jnp.logical_or(where_lat < lat_count - 1, rows < marks.shape[0] - width)
    return jnp.where(jnp.logical_and(keep_top, keep_bottom), marks, 0.0)


def single_rim(values):
    return with_halo(values, (("lat", 2), ("lon", 3)), 1)


def shards(
    adjoint_state,
    mixing_base,
    atm_flux,
    send_count,
    send_segment,
    cover_index,
    cover_weight,
    land_mask,
):
    lat_count = lax.axis_size("lat")
    owned = atm_flux.shape[1]
    counts = send_count[0]
    capacity = send_segment.shape[1] // lat_count
    starts = jnp.cumsum(counts) - counts
    column = jnp.arange(capacity, dtype=jnp.int32)
    places = jnp.minimum(starts[:, None] + column[None, :], send_segment.shape[1] - 1)
    chosen = send_segment[0][places]
    live_slot = column[None, :] < counts[:, None]
    outgoing = atm_flux[:, chosen, :]
    received = lax.all_to_all(outgoing, "lat", split_axis=1, concat_axis=1, tiled=True)
    items, rows, cols = cover_index.shape
    fields = received.shape[0]
    flat_recv = received.reshape(-1, received.shape[-1])
    index_rows = cover_index.reshape(items * rows, cols)
    weight_rows = cover_weight.reshape(items * rows, cols)
    land = land_mask.astype(jnp.float32)
    *pieces, mask = extended_planes(adjoint_state, land_mask, HALO)
    forcing = remap_call(
        gather_kernel, (fields, rows, cols), flat_recv, index_rows, weight_rows, after=tuple(pieces[1:])
    )
    surface = WIND_GAIN * (forcing[2] * forcing[2] + forcing[3] * forcing[3]) + jax.nn.softplus(
        forcing[1] - forcing[0]
    )
    state_adjoint, flux_back = tridiagonal(pieces, mask, adjoint_state.shape, mixing_base, surface, land)
    buffer = remap_call(scatter_kernel, flat_recv.shape, flux_back, index_rows, weight_rows)
    returned = lax.all_to_all(
        buffer.reshape(received.shape), "lat", split_axis=1, concat_axis=1, tiled=True
    )
    owned_ids = lax.broadcasted_iota(jnp.int32, (owned,) + chosen.shape, 0)
    picks = jnp.logical_and(owned_ids == chosen[None], live_slot[None]).astype(jnp.float32)
    owner_sum = jnp.einsum(
        "sdc,fdck->fsk", picks, returned, precision=lax.Precision.HIGHEST
    )
    flux_adjoint = sum_over(owner_sum, "lon")
    return (state_adjoint, flux_adjoint)


def solution(mesh):
    in_specs = (
        P(None, None, "lat", "lon"),
        P(None, "lat", "lon"),
        P(None, "lat", None),
        P("lat", "lon"),
        P("lat", "lon"),
        P(None, "lat", "lon"),
        P(None, "lat", "lon"),
        P("lat", "lon"),
    )
    out_specs = (P(None, None, "lat", "lon"), P(None, "lat", None))
    return jax.shard_map(shards, mesh=mesh, in_specs=in_specs, out_specs=out_specs, check_vma=False)
```

```python
import math

import jax
import jax.numpy as jnp
import numpy as np
from jax import lax
from jax.experimental import pallas as pl
from jax.experimental.pallas import tpu as pltpu
from jax.sharding import PartitionSpec as P

SMOOTHING = 0.02
WIND_GAIN = 1.0
DEPTH_SCALE = 12.0
FIELD_MIX = (1.0, 1.0, 2.0, 2.0)


HALO = 4


def from_neighbours(block, axis, dim, width):
    count = lax.axis_size(axis)
    to_prev = [(i, (i - 1) % count) for i in range(count)]
    to_next = [(i, (i + 1) % count) for i in range(count)]
    size = block.shape[dim]
    from_next = lax.ppermute(lax.slice_in_dim(block, 0, width, axis=dim), axis, to_prev)
    from_prev = lax.ppermute(lax.slice_in_dim(block, size - width, size, axis=dim), axis, to_next)
    return from_next, from_prev


def extended_planes(values, land_mask, width):
    fields, levels, rows, cols = values.shape
    planes = values.reshape(fields * levels, rows, cols)
    coast = land_mask.astype(jnp.float32)[None]
    stack = jnp.concatenate([planes, coast], axis=0)
    south, north = from_neighbours(stack, "lat", 1, width)
    east, west = from_neighbours(stack, "lon", 2, width)
    sides = jnp.concatenate([east, west], axis=2)
    corner_south, corner_north = from_neighbours(sides, "lat", 1, width)
    wide = -(-(2 * width) // 128) * 128
    edges = jnp.concatenate([sides, corner_south, corner_north], axis=1)
    gap = jnp.zeros(edges.shape[:2] + (wide - 2 * width,), jnp.float32)
    edge_tile = jnp.concatenate([edges[:, :, :width], gap, edges[:, :, width:]], axis=2)
    halo_rows = jnp.concatenate([south, north], axis=1)
    coast_plane = jnp.concatenate(
        [jnp.concatenate([stack[-1], halo_rows[-1]], axis=0), edge_tile[-1]], axis=1
    )
    lat_count = lax.axis_size("lat")
    where_lat = lax.axis_index("lat")
    row = lax.broadcasted_iota(jnp.int32, coast_plane.shape, 0)
    outside = jnp.logical_or(
        jnp.logical_and(where_lat == 0, row >= rows + width),
        jnp.logical_and(where_lat == lat_count - 1, jnp.logical_and(row >= rows, row < rows + width)),
    )
    mask = jnp.where(outside, 0.0, coast_plane)
    return planes, halo_rows, edge_tile, mask


def with_halo(block, sides, width):
    for axis, dim in sides:
        count = lax.axis_size(axis)
        forward = [(i, i + 1) for i in range(count - 1)]
        forward.append((count - 1, 0))
        backward = [(target, source) for source, target in forward]
        low = lax.ppermute(
            lax.slice_in_dim(block, block.shape[dim] - width, None, axis=dim), axis, forward
        )
        high = lax.ppermute(lax.slice_in_dim(block, 0, width, axis=dim), axis, backward)
        block = jnp.concatenate([low, block, high], axis=dim)
    return block


def laplace(values, marks):
    centre = values[..., 1:-1, 1:-1]
    north = marks[:-2, 1:-1] * (values[..., :-2, 1:-1] - centre)
    south = marks[2:, 1:-1] * (values[..., 2:, 1:-1] - centre)
    west = marks[1:-1, :-2] * (values[..., 1:-1, :-2] - centre)
    east = marks[1:-1, 2:] * (values[..., 1:-1, 2:] - centre)
    return marks[1:-1, 1:-1] * (north + south + west + east)


def tridiagonal_kernel(
    decay_ref, inner_ref, rows_ref, edge_ref, mask_ref, base_ref, surf_ref, land_ref,
    out_ref, back_ref, ratio_ref, marks_ref,
):
    fields, levels = out_ref.shape[0], out_ref.shape[1]
    rows, cols = out_ref.shape[2], out_ref.shape[3]
    tall, wide = mask_ref.shape
    marks = mask_ref[...]
    marks_ref[0] = marks * pltpu.roll(marks, 1, 0)
    marks_ref[1] = marks * pltpu.roll(marks, tall - 1, 0)
    marks_ref[2] = marks * pltpu.roll(marks, 1, 1)
    marks_ref[3] = marks * pltpu.roll(marks, wide - 1, 1)
    marks_ref[4] = (marks_ref[0] + marks_ref[1]) + (marks_ref[2] + marks_ref[3])

    def laplace_ext(values, inner=False):
        shifted = [
            pltpu.roll(values, 1, 0),
            pltpu.roll(values, tall - 1, 0),
            pltpu.roll(values, 1, 1),
            pltpu.roll(values, wide - 1, 1),
        ]
        if inner:
            shifted = [part[:rows, :cols] for part in shifted]
            values = values[:rows, :cols]
            weight = [marks_ref[i, :rows, :cols] for i in range(5)]
        else:
            weight = [marks_ref[i] for i in range(5)]
        vertical = weight[0] * shifted[0] + weight[1] * shifted[1]
        across = weight[2] * shifted[2] + weight[3] * shifted[3]
        return (vertical + across) - weight[4] * values

    def smoothed(f, level):
        plane = f * levels + level
        values = jnp.concatenate([inner_ref[plane], rows_ref[plane]], axis=0)
        values = jnp.concatenate([values, edge_ref[plane]], axis=1)
        inner = laplace_ext(values)
        values = values - SMOOTHING * laplace_ext(inner)
        inner = laplace_ext(values)
        return values[:rows, :cols] - SMOOTHING * laplace_ext(inner, inner=True)

    gains = sorted(set(FIELD_MIX))
    groups = [[f for f in range(fields) if FIELD_MIX[f] == g] for g in gains]
    surf = surf_ref[...]
    zero = jnp.zeros_like(surf)

    def step(level, below_mix, above_mix, ratios, parts, sources):
        new_ratios, new_parts = [], list(parts)
        for gi, gain in enumerate(gains):
            below = gain * below_mix
            above = gain * above_mix
            pivot = ((1.0 + below) + above) - below * ratios[gi]
            scale = 1.0 / pivot
            if level is not None:
                ratio = above * scale
                ratio_ref[gi, level] = ratio
                new_ratios.append(ratio)
            for f in groups[gi]:
                value = (sources[f] + below * parts[f]) * scale
                out_ref[f, level if level is not None else levels - 1] = value
                new_parts[f] = value
        return tuple(new_ratios), tuple(new_parts)

    def forward(level, carry):
        below_mix, ratios, parts, sources = carry
        upcoming = tuple(smoothed(f, level + 1) for f in range(fields))
        mix = base_ref[level] + surf * decay_ref[level]
        ratios, parts = step(level, below_mix, mix, ratios, parts, sources)
        return (mix, ratios, parts, upcoming)

    first = tuple(smoothed(f, 0) for f in range(fields))
    carry = (zero, tuple(zero for _ in gains), tuple(zero for _ in range(fields)), first)
    last_mix, ratios, parts, sources = lax.fori_loop(0, levels - 1, forward, carry)
    step(None, last_mix, zero, ratios, parts, sources)

    def backward(i, later):
        level = levels - 2 - i
        result = []
        for gi in range(len(gains)):
            ratio = ratio_ref[gi, level]
            for f in groups[gi]:
                value = out_ref[f, level] + ratio * later[f]
                out_ref[f, level] = value
                result.append((f, value))
        result.sort(key=lambda item: item[0])
        return tuple(v for _, v in result)

    final = tuple(out_ref[f, levels - 1] for f in range(fields))
    lax.fori_loop(0, levels - 1, backward, final)
    land = land_ref[...]
    for f in range(fields):
        back_ref[f] = land * out_ref[f, 0]


def tridiagonal(pieces, mask, shape, mixing_base, surface, land):
    fields, levels = shape[0], shape[1]
    decay_table = np.array(
        [math.exp(-level / DEPTH_SCALE) for level in range(levels)], dtype=np.float32
    )
    vmem = pltpu.MemorySpace.VMEM
    return pl.pallas_call(
        tridiagonal_kernel,
        out_shape=(
            jax.ShapeDtypeStruct(shape, jnp.float32),
            jax.ShapeDtypeStruct((fields,) + shape[2:], jnp.float32),
        ),
        in_specs=[pl.BlockSpec(memory_space=pltpu.MemorySpace.SMEM)]
        + [pl.BlockSpec(memory_space=vmem)] * (len(pieces) + 4),
        out_specs=(pl.BlockSpec(memory_space=vmem), pl.BlockSpec(memory_space=vmem)),
        scratch_shapes=[
            pltpu.VMEM((len(set(FIELD_MIX)), levels) + shape[2:], jnp.float32),
            pltpu.VMEM((5,) + mask.shape, jnp.float32),
        ],
    )(jnp.asarray(decay_table), *pieces, mask, mixing_base, surface, land)


def split_parts(values):
    high = values.astype(jnp.bfloat16)
    low = (values - high.astype(jnp.float32)).astype(jnp.bfloat16)
    return high, low


def matmul_exact(parts, other, contract):
    numbers = (((1,), (contract,)), ((), ()))
    total = None
    for part in parts:
        product = lax.dot_general(part, other, numbers, preferred_element_type=jnp.float32)
        total = product if total is None else total + product
    return total


def gather_kernel(recv_ref, index_ref, weight_ref, *after_and_out):
    out_ref = after_and_out[-1]
    stacked, lanes = recv_ref.shape
    fields, rows, cols = out_ref.shape
    segments = stacked // fields
    items = index_ref.shape[0] // rows
    parts = split_parts(recv_ref[...])
    lane_iota = lax.broadcasted_iota(jnp.int32, (lanes, cols), 0)
    segment_iota = lax.broadcasted_iota(jnp.int32, (fields, segments, cols), 1)

    def row_step(y, carry):
        total = None
        for item in range(items):
            index = index_ref[pl.ds(item * rows + y, 1), :]
            onehot = (lane_iota == index % lanes).astype(jnp.bfloat16)
            chosen = matmul_exact(parts, onehot, 0).reshape(fields, segments, cols)
            hit = segment_iota == (index // lanes)[None]
            picked = jnp.sum(jnp.where(hit, chosen, 0.0), axis=1)
            term = weight_ref[pl.ds(item * rows + y, 1), :] * picked
            total = term if total is None else total + term
        out_ref[:, pl.ds(y, 1), :] = total[:, None, :]
        return carry

    lax.fori_loop(0, rows, row_step, 0)


def scatter_kernel(back_ref, index_ref, weight_ref, out_ref):
    fields, rows, cols = back_ref.shape
    stacked, lanes = out_ref.shape
    segments = stacked // fields
    items = index_ref.shape[0] // rows
    lane_iota = lax.broadcasted_iota(jnp.int32, (lanes, cols), 0)
    segment_iota = lax.broadcasted_iota(jnp.int32, (fields, segments, cols), 1)

    def row_step(y, total):
        back = back_ref[:, pl.ds(y, 1), :]
        for item in range(items):
            index = index_ref[pl.ds(item * rows + y, 1), :]
            onehot = (lane_iota == index % lanes).astype(jnp.bfloat16)
            weighted = weight_ref[pl.ds(item * rows + y, 1), :][None] * back
            hit = segment_iota == (index // lanes)[None]
            spread = jnp.where(hit, weighted, 0.0).reshape(stacked, cols)
            total = total + matmul_exact(split_parts(spread), onehot, 1)
        return total

    out_ref[...] = lax.fori_loop(0, rows, row_step, jnp.zeros((stacked, lanes), jnp.float32))


def remap_call(kernel, out_shape, *operands, after=()):
    vmem = pltpu.MemorySpace.VMEM
    return pl.pallas_call(
        kernel,
        out_shape=jax.ShapeDtypeStruct(out_shape, jnp.float32),
        in_specs=[pl.BlockSpec(memory_space=vmem)] * len(operands)
        + [pl.BlockSpec(memory_space=pl.ANY)] * len(after),
        out_specs=pl.BlockSpec(memory_space=vmem),
    )(*operands, *after)


def sum_over(values, axis):
    count = lax.axis_size(axis)
    if count & (count - 1):
        return lax.psum(values, axis)
    step = 1
    while step < count:
        pairs = [(i, i ^ step) for i in range(count)]
        values = values + lax.ppermute(values, axis, pairs)
        step *= 2
    return values


def lat_edges(marks, width):
    lat_count = lax.axis_size("lat")
    where_lat = lax.axis_index("lat")
    rows = lax.broadcasted_iota(jnp.int32, marks.shape, 0)
    keep_top = jnp.logical_or(where_lat > 0, rows >= width)
    keep_bottom = jnp.logical_or(where_lat < lat_count - 1, rows < marks.shape[0] - width)
    return jnp.where(jnp.logical_and(keep_top, keep_bottom), marks, 0.0)


def single_rim(values):
    return with_halo(values, (("lat", 2), ("lon", 3)), 1)


def shards(
    adjoint_state,
    mixing_base,
    atm_flux,
    send_count,
    send_segment,
    cover_index,
    cover_weight,
    land_mask,
):
    lat_count = lax.axis_size("lat")
    owned = atm_flux.shape[1]
    counts = send_count[0]
    capacity = send_segment.shape[1] // lat_count
    starts = jnp.cumsum(counts) - counts
    column = jnp.arange(capacity, dtype=jnp.int32)
    places = jnp.minimum(starts[:, None] + column[None, :], send_segment.shape[1] - 1)
    chosen = send_segment[0][places]
    live_slot = column[None, :] < counts[:, None]
    outgoing = atm_flux[:, chosen, :]
    received = lax.all_to_all(outgoing, "lat", split_axis=1, concat_axis=1, tiled=True)
    items, rows, cols = cover_index.shape
    fields = received.shape[0]
    flat_recv = received.reshape(-1, received.shape[-1])
    index_rows = cover_index.reshape(items * rows, cols)
    weight_rows = cover_weight.reshape(items * rows, cols)
    land = land_mask.astype(jnp.float32)
    *pieces, mask = extended_planes(adjoint_state, land_mask, HALO)
    forcing = remap_call(
        gather_kernel, (fields, rows, cols), flat_recv, index_rows, weight_rows
    )
    surface = WIND_GAIN * (forcing[2] * forcing[2] + forcing[3] * forcing[3]) + jax.nn.softplus(
        forcing[1] - forcing[0]
    )
    state_adjoint, flux_back = tridiagonal(pieces, mask, adjoint_state.shape, mixing_base, surface, land)
    buffer = remap_call(scatter_kernel, flat_recv.shape, flux_back, index_rows, weight_rows)
    returned = lax.all_to_all(
        buffer.reshape(received.shape), "lat", split_axis=1, concat_axis=1, tiled=True
    )
    owned_ids = lax.broadcasted_iota(jnp.int32, (owned,) + chosen.shape, 0)
    picks = jnp.logical_and(owned_ids == chosen[None], live_slot[None]).astype(jnp.float32)
    owner_sum = jnp.einsum(
        "sdc,fdck->fsk", picks, returned, precision=lax.Precision.HIGHEST
    )
    flux_adjoint = sum_over(owner_sum, "lon")
    return (state_adjoint, flux_adjoint)


def solution(mesh):
    in_specs = (
        P(None, None, "lat", "lon"),
        P(None, "lat", "lon"),
        P(None, "lat", None),
        P("lat", "lon"),
        P("lat", "lon"),
        P(None, "lat", "lon"),
        P(None, "lat", "lon"),
        P("lat", "lon"),
    )
    out_specs = (P(None, None, "lat", "lon"), P(None, "lat", None))
    return jax.shard_map(shards, mesh=mesh, in_specs=in_specs, out_specs=out_specs, check_vma=False)
```

```python
import math

import jax
import jax.numpy as jnp
import numpy as np
from jax import lax
from jax.experimental import pallas as pl
from jax.experimental.pallas import tpu as pltpu
from jax.sharding import PartitionSpec as P

SMOOTHING = 0.02
WIND_GAIN = 1.0
DEPTH_SCALE = 12.0
FIELD_MIX = (1.0, 1.0, 2.0, 2.0)


HALO = 4


def from_neighbours(block, axis, dim, width):
    count = lax.axis_size(axis)
    to_prev = [(i, (i - 1) % count) for i in range(count)]
    to_next = [(i, (i + 1) % count) for i in range(count)]
    size = block.shape[dim]
    from_next = lax.ppermute(lax.slice_in_dim(block, 0, width, axis=dim), axis, to_prev)
    from_prev = lax.ppermute(lax.slice_in_dim(block, size - width, size, axis=dim), axis, to_next)
    return from_next, from_prev


def extended_planes(values, land_mask, width):
    fields, levels, rows, cols = values.shape
    planes = values.reshape(fields * levels, rows, cols)
    coast = land_mask.astype(jnp.float32)[None]
    stack = jnp.concatenate([planes, coast], axis=0)
    south, north = from_neighbours(stack, "lat", 1, width)
    east, west = from_neighbours(stack, "lon", 2, width)
    sides = jnp.concatenate([east, west], axis=2)
    corner_south, corner_north = from_neighbours(sides, "lat", 1, width)
    wide = -(-(2 * width) // 128) * 128
    edges = jnp.concatenate([sides, corner_south, corner_north], axis=1)
    gap = jnp.zeros(edges.shape[:2] + (wide - 2 * width,), jnp.float32)
    edge_tile = jnp.concatenate([edges[:, :, :width], gap, edges[:, :, width:]], axis=2)
    halo_rows = jnp.concatenate([south, north], axis=1)
    coast_plane = jnp.concatenate(
        [jnp.concatenate([stack[-1], halo_rows[-1]], axis=0), edge_tile[-1]], axis=1
    )
    lat_count = lax.axis_size("lat")
    where_lat = lax.axis_index("lat")
    row = lax.broadcasted_iota(jnp.int32, coast_plane.shape, 0)
    outside = jnp.logical_or(
        jnp.logical_and(where_lat == 0, row >= rows + width),
        jnp.logical_and(where_lat == lat_count - 1, jnp.logical_and(row >= rows, row < rows + width)),
    )
    mask = jnp.where(outside, 0.0, coast_plane)
    return planes, halo_rows, edge_tile, mask


def with_halo(block, sides, width):
    for axis, dim in sides:
        count = lax.axis_size(axis)
        forward = [(i, i + 1) for i in range(count - 1)]
        forward.append((count - 1, 0))
        backward = [(target, source) for source, target in forward]
        low = lax.ppermute(
            lax.slice_in_dim(block, block.shape[dim] - width, None, axis=dim), axis, forward
        )
        high = lax.ppermute(lax.slice_in_dim(block, 0, width, axis=dim), axis, backward)
        block = jnp.concatenate([low, block, high], axis=dim)
    return block


def laplace(values, marks):
    centre = values[..., 1:-1, 1:-1]
    north = marks[:-2, 1:-1] * (values[..., :-2, 1:-1] - centre)
    south = marks[2:, 1:-1] * (values[..., 2:, 1:-1] - centre)
    west = marks[1:-1, :-2] * (values[..., 1:-1, :-2] - centre)
    east = marks[1:-1, 2:] * (values[..., 1:-1, 2:] - centre)
    return marks[1:-1, 1:-1] * (north + south + west + east)


def tridiagonal_kernel(
    decay_ref, inner_ref, rows_ref, edge_ref, mask_ref, base_ref, surf_ref, land_ref,
    out_ref, back_ref, ratio_ref, marks_ref,
):
    fields, levels = out_ref.shape[0], out_ref.shape[1]
    rows, cols = out_ref.shape[2], out_ref.shape[3]
    tall, wide = mask_ref.shape
    marks = mask_ref[...]
    marks_ref[0] = marks * pltpu.roll(marks, 1, 0)
    marks_ref[1] = marks * pltpu.roll(marks, tall - 1, 0)
    marks_ref[2] = marks * pltpu.roll(marks, 1, 1)
    marks_ref[3] = marks * pltpu.roll(marks, wide - 1, 1)
    marks_ref[4] = (marks_ref[0] + marks_ref[1]) + (marks_ref[2] + marks_ref[3])

    def laplace_ext(values, inner=False):
        shifted = [
            pltpu.roll(values, 1, 0),
            pltpu.roll(values, tall - 1, 0),
            pltpu.roll(values, 1, 1),
            pltpu.roll(values, wide - 1, 1),
        ]
        if inner:
            shifted = [part[:rows, :cols] for part in shifted]
            values = values[:rows, :cols]
            weight = [marks_ref[i, :rows, :cols] for i in range(5)]
        else:
            weight = [marks_ref[i] for i in range(5)]
        vertical = weight[0] * shifted[0] + weight[1] * shifted[1]
        across = weight[2] * shifted[2] + weight[3] * shifted[3]
        return (vertical + across) - weight[4] * values

    def smoothed(f, level):
        plane = f * levels + level
        values = jnp.concatenate([inner_ref[plane], rows_ref[plane]], axis=0)
        values = jnp.concatenate([values, edge_ref[plane]], axis=1)
        inner = laplace_ext(values)
        values = values - SMOOTHING * laplace_ext(inner)
        inner = laplace_ext(values)
        return values[:rows, :cols] - SMOOTHING * laplace_ext(inner, inner=True)

    gains = sorted(set(FIELD_MIX))
    groups = [[f for f in range(fields) if FIELD_MIX[f] == g] for g in gains]
    surf = surf_ref[...]
    zero = jnp.zeros_like(surf)

    def step(level, below_mix, above_mix, ratios, parts, sources):
        new_ratios, new_parts = [], list(parts)
        for gi, gain in enumerate(gains):
            below = gain * below_mix
            above = gain * above_mix
            pivot = ((1.0 + below) + above) - below * ratios[gi]
            scale = 1.0 / pivot
            if level is not None:
                ratio = above * scale
                ratio_ref[gi, level] = ratio
                new_ratios.append(ratio)
            for f in groups[gi]:
                value = (sources[f] + below * parts[f]) * scale
                out_ref[f, level if level is not None else levels - 1] = value
                new_parts[f] = value
        return tuple(new_ratios), tuple(new_parts)

    def forward(level, carry):
        below_mix, ratios, parts, sources = carry
        upcoming = tuple(smoothed(f, level + 1) for f in range(fields))
        mix = base_ref[level] + surf * decay_ref[level]
        ratios, parts = step(level, below_mix, mix, ratios, parts, sources)
        return (mix, ratios, parts, upcoming)

    first = tuple(smoothed(f, 0) for f in range(fields))
    carry = (zero, tuple(zero for _ in gains), tuple(zero for _ in range(fields)), first)
    last_mix, ratios, parts, sources = lax.fori_loop(0, levels - 1, forward, carry)
    step(None, last_mix, zero, ratios, parts, sources)

    def backward(i, later):
        level = levels - 2 - i
        result = []
        for gi in range(len(gains)):
            ratio = ratio_ref[gi, level]
            for f in groups[gi]:
                value = out_ref[f, level] + ratio * later[f]
                out_ref[f, level] = value
                result.append((f, value))
        result.sort(key=lambda item: item[0])
        return tuple(v for _, v in result)

    final = tuple(out_ref[f, levels - 1] for f in range(fields))
    lax.fori_loop(0, levels - 1, backward, final)
    land = land_ref[...]
    for f in range(fields):
        back_ref[f] = land * out_ref[f, 0]


def tridiagonal(pieces, mask, shape, mixing_base, surface, land):
    fields, levels = shape[0], shape[1]
    decay_table = np.array(
        [math.exp(-level / DEPTH_SCALE) for level in range(levels)], dtype=np.float32
    )
    vmem = pltpu.MemorySpace.VMEM
    return pl.pallas_call(
        tridiagonal_kernel,
        out_shape=(
            jax.ShapeDtypeStruct(shape, jnp.float32),
            jax.ShapeDtypeStruct((fields,) + shape[2:], jnp.float32),
        ),
        in_specs=[pl.BlockSpec(memory_space=pltpu.MemorySpace.SMEM)]
        + [pl.BlockSpec(memory_space=vmem)] * (len(pieces) + 4),
        out_specs=(pl.BlockSpec(memory_space=vmem), pl.BlockSpec(memory_space=vmem)),
        scratch_shapes=[
            pltpu.VMEM((len(set(FIELD_MIX)), levels) + shape[2:], jnp.float32),
            pltpu.VMEM((5,) + mask.shape, jnp.float32),
        ],
    )(jnp.asarray(decay_table), *pieces, mask, mixing_base, surface, land)


def split_parts(values):
    high = values.astype(jnp.bfloat16)
    low = (values - high.astype(jnp.float32)).astype(jnp.bfloat16)
    return high, low


def matmul_exact(parts, other, contract):
    numbers = (((1,), (contract,)), ((), ()))
    total = None
    for part in parts:
        product = lax.dot_general(part, other, numbers, preferred_element_type=jnp.float32)
        total = product if total is None else total + product
    return total


def gather_kernel(recv_ref, index_ref, weight_ref, *after_and_out):
    out_ref = after_and_out[-1]
    stacked, lanes = recv_ref.shape
    fields, rows, cols = out_ref.shape
    segments = stacked // fields
    items = index_ref.shape[0] // rows
    parts = split_parts(recv_ref[...])
    lane_iota = lax.broadcasted_iota(jnp.int32, (lanes, cols), 0)
    segment_iota = lax.broadcasted_iota(jnp.int32, (fields, segments, cols), 1)

    def row_step(y, carry):
        total = None
        for item in range(items):
            index = index_ref[pl.ds(item * rows + y, 1), :]
            onehot = (lane_iota == index % lanes).astype(jnp.bfloat16)
            chosen = matmul_exact(parts, onehot, 0).reshape(fields, segments, cols)
            hit = segment_iota == (index // lanes)[None]
            picked = jnp.sum(jnp.where(hit, chosen, 0.0), axis=1)
            term = weight_ref[pl.ds(item * rows + y, 1), :] * picked
            total = term if total is None else total + term
        out_ref[:, pl.ds(y, 1), :] = total[:, None, :]
        return carry

    lax.fori_loop(0, rows, row_step, 0, unroll=True)


def scatter_kernel(back_ref, index_ref, weight_ref, out_ref):
    fields, rows, cols = back_ref.shape
    stacked, lanes = out_ref.shape
    segments = stacked // fields
    items = index_ref.shape[0] // rows
    lane_iota = lax.broadcasted_iota(jnp.int32, (lanes, cols), 0)
    segment_iota = lax.broadcasted_iota(jnp.int32, (fields, segments, cols), 1)

    def row_step(y, total):
        back = back_ref[:, pl.ds(y, 1), :]
        for item in range(items):
            index = index_ref[pl.ds(item * rows + y, 1), :]
            onehot = (lane_iota == index % lanes).astype(jnp.bfloat16)
            weighted = weight_ref[pl.ds(item * rows + y, 1), :][None] * back
            hit = segment_iota == (index // lanes)[None]
            spread = jnp.where(hit, weighted, 0.0).reshape(stacked, cols)
            total = total + matmul_exact(split_parts(spread), onehot, 1)
        return total

    out_ref[...] = lax.fori_loop(
        0, rows, row_step, jnp.zeros((stacked, lanes), jnp.float32), unroll=True
    )


def remap_call(kernel, out_shape, *operands, after=()):
    vmem = pltpu.MemorySpace.VMEM
    return pl.pallas_call(
        kernel,
        out_shape=jax.ShapeDtypeStruct(out_shape, jnp.float32),
        in_specs=[pl.BlockSpec(memory_space=vmem)] * len(operands)
        + [pl.BlockSpec(memory_space=pl.ANY)] * len(after),
        out_specs=pl.BlockSpec(memory_space=vmem),
    )(*operands, *after)


def sum_over(values, axis):
    count = lax.axis_size(axis)
    if count & (count - 1):
        return lax.psum(values, axis)
    step = 1
    while step < count:
        pairs = [(i, i ^ step) for i in range(count)]
        values = values + lax.ppermute(values, axis, pairs)
        step *= 2
    return values


def lat_edges(marks, width):
    lat_count = lax.axis_size("lat")
    where_lat = lax.axis_index("lat")
    rows = lax.broadcasted_iota(jnp.int32, marks.shape, 0)
    keep_top = jnp.logical_or(where_lat > 0, rows >= width)
    keep_bottom = jnp.logical_or(where_lat < lat_count - 1, rows < marks.shape[0] - width)
    return jnp.where(jnp.logical_and(keep_top, keep_bottom), marks, 0.0)


def single_rim(values):
    return with_halo(values, (("lat", 2), ("lon", 3)), 1)


def shards(
    adjoint_state,
    mixing_base,
    atm_flux,
    send_count,
    send_segment,
    cover_index,
    cover_weight,
    land_mask,
):
    lat_count = lax.axis_size("lat")
    owned = atm_flux.shape[1]
    counts = send_count[0]
    capacity = send_segment.shape[1] // lat_count
    starts = jnp.cumsum(counts) - counts
    column = jnp.arange(capacity, dtype=jnp.int32)
    places = jnp.minimum(starts[:, None] + column[None, :], send_segment.shape[1] - 1)
    chosen = send_segment[0][places]
    live_slot = column[None, :] < counts[:, None]
    outgoing = atm_flux[:, chosen, :]
    received = lax.all_to_all(outgoing, "lat", split_axis=1, concat_axis=1, tiled=True)
    items, rows, cols = cover_index.shape
    fields = received.shape[0]
    flat_recv = received.reshape(-1, received.shape[-1])
    index_rows = cover_index.reshape(items * rows, cols)
    weight_rows = cover_weight.reshape(items * rows, cols)
    land = land_mask.astype(jnp.float32)
    *pieces, mask = extended_planes(adjoint_state, land_mask, HALO)
    forcing = remap_call(
        gather_kernel, (fields, rows, cols), flat_recv, index_rows, weight_rows, after=tuple(pieces[1:])
    )
    surface = WIND_GAIN * (forcing[2] * forcing[2] + forcing[3] * forcing[3]) + jax.nn.softplus(
        forcing[1] - forcing[0]
    )
    state_adjoint, flux_back = tridiagonal(pieces, mask, adjoint_state.shape, mixing_base, surface, land)
    buffer = remap_call(scatter_kernel, flat_recv.shape, flux_back, index_rows, weight_rows)
    returned = lax.all_to_all(
        buffer.reshape(received.shape), "lat", split_axis=1, concat_axis=1, tiled=True
    )
    owned_ids = lax.broadcasted_iota(jnp.int32, (owned,) + chosen.shape, 0)
    picks = jnp.logical_and(owned_ids == chosen[None], live_slot[None]).astype(jnp.float32)
    owner_sum = jnp.einsum(
        "sdc,fdck->fsk", picks, returned, precision=lax.Precision.HIGHEST
    )
    flux_adjoint = sum_over(owner_sum, "lon")
    return (state_adjoint, flux_adjoint)


def solution(mesh):
    in_specs = (
        P(None, None, "lat", "lon"),
        P(None, "lat", "lon"),
        P(None, "lat", None),
        P("lat", "lon"),
        P("lat", "lon"),
        P(None, "lat", "lon"),
        P(None, "lat", "lon"),
        P("lat", "lon"),
    )
    out_specs = (P(None, None, "lat", "lon"), P(None, "lat", None))
    return jax.shard_map(shards, mesh=mesh, in_specs=in_specs, out_specs=out_specs, check_vma=False)
```

```python
import math

import jax
import jax.numpy as jnp
import numpy as np
from jax import lax
from jax.experimental import pallas as pl
from jax.experimental.pallas import tpu as pltpu
from jax.sharding import PartitionSpec as P

SMOOTHING = 0.02
WIND_GAIN = 1.0
DEPTH_SCALE = 12.0
FIELD_MIX = (1.0, 1.0, 2.0, 2.0)


HALO = 4


def from_neighbours(block, axis, dim, width):
    count = lax.axis_size(axis)
    to_prev = [(i, (i - 1) % count) for i in range(count)]
    to_next = [(i, (i + 1) % count) for i in range(count)]
    size = block.shape[dim]
    from_next = lax.ppermute(lax.slice_in_dim(block, 0, width, axis=dim), axis, to_prev)
    from_prev = lax.ppermute(lax.slice_in_dim(block, size - width, size, axis=dim), axis, to_next)
    return from_next, from_prev


def extended_planes(values, land_mask, width):
    fields, levels, rows, cols = values.shape
    planes = values.reshape(fields * levels, rows, cols)
    coast = land_mask.astype(jnp.float32)[None]
    stack = jnp.concatenate([planes, coast], axis=0)
    south, north = from_neighbours(stack, "lat", 1, width)
    east, west = from_neighbours(stack, "lon", 2, width)
    sides = jnp.concatenate([east, west], axis=2)
    corner_south, corner_north = from_neighbours(sides, "lat", 1, width)
    wide = -(-(2 * width) // 128) * 128
    edges = jnp.concatenate([sides, corner_south, corner_north], axis=1)
    gap = jnp.zeros(edges.shape[:2] + (wide - 2 * width,), jnp.float32)
    edge_tile = jnp.concatenate([edges[:, :, :width], gap, edges[:, :, width:]], axis=2)
    halo_rows = jnp.concatenate([south, north], axis=1)
    coast_plane = jnp.concatenate(
        [jnp.concatenate([stack[-1], halo_rows[-1]], axis=0), edge_tile[-1]], axis=1
    )
    lat_count = lax.axis_size("lat")
    where_lat = lax.axis_index("lat")
    row = lax.broadcasted_iota(jnp.int32, coast_plane.shape, 0)
    outside = jnp.logical_or(
        jnp.logical_and(where_lat == 0, row >= rows + width),
        jnp.logical_and(where_lat == lat_count - 1, jnp.logical_and(row >= rows, row < rows + width)),
    )
    mask = jnp.where(outside, 0.0, coast_plane)
    return planes, halo_rows, edge_tile, mask


def with_halo(block, sides, width):
    for axis, dim in sides:
        count = lax.axis_size(axis)
        forward = [(i, i + 1) for i in range(count - 1)]
        forward.append((count - 1, 0))
        backward = [(target, source) for source, target in forward]
        low = lax.ppermute(
            lax.slice_in_dim(block, block.shape[dim] - width, None, axis=dim), axis, forward
        )
        high = lax.ppermute(lax.slice_in_dim(block, 0, width, axis=dim), axis, backward)
        block = jnp.concatenate([low, block, high], axis=dim)
    return block


def laplace(values, marks):
    centre = values[..., 1:-1, 1:-1]
    north = marks[:-2, 1:-1] * (values[..., :-2, 1:-1] - centre)
    south = marks[2:, 1:-1] * (values[..., 2:, 1:-1] - centre)
    west = marks[1:-1, :-2] * (values[..., 1:-1, :-2] - centre)
    east = marks[1:-1, 2:] * (values[..., 1:-1, 2:] - centre)
    return marks[1:-1, 1:-1] * (north + south + west + east)


def tridiagonal_kernel(
    decay_ref, inner_ref, rows_ref, edge_ref, mask_ref, base_ref, surf_ref, land_ref,
    out_ref, back_ref, ratio_ref, marks_ref,
):
    fields, levels = out_ref.shape[0], out_ref.shape[1]
    rows, cols = out_ref.shape[2], out_ref.shape[3]
    tall, wide = mask_ref.shape
    marks = mask_ref[...]
    marks_ref[0] = marks * pltpu.roll(marks, 1, 0)
    marks_ref[1] = marks * pltpu.roll(marks, tall - 1, 0)
    marks_ref[2] = marks * pltpu.roll(marks, 1, 1)
    marks_ref[3] = marks * pltpu.roll(marks, wide - 1, 1)
    marks_ref[4] = (marks_ref[0] + marks_ref[1]) + (marks_ref[2] + marks_ref[3])

    def laplace_ext(values, inner=False):
        shifted = [
            pltpu.roll(values, 1, 0),
            pltpu.roll(values, tall - 1, 0),
            pltpu.roll(values, 1, 1),
            pltpu.roll(values, wide - 1, 1),
        ]
        if inner:
            shifted = [part[:rows, :cols] for part in shifted]
            values = values[:rows, :cols]
            weight = [marks_ref[i, :rows, :cols] for i in range(5)]
        else:
            weight = [marks_ref[i] for i in range(5)]
        vertical = weight[0] * shifted[0] + weight[1] * shifted[1]
        across = weight[2] * shifted[2] + weight[3] * shifted[3]
        return (vertical + across) - weight[4] * values

    def smoothed(f, level):
        plane = f * levels + level
        values = jnp.concatenate([inner_ref[plane], rows_ref[plane]], axis=0)
        values = jnp.concatenate([values, edge_ref[plane]], axis=1)
        inner = laplace_ext(values)
        values = values - SMOOTHING * laplace_ext(inner)
        inner = laplace_ext(values)
        return values[:rows, :cols] - SMOOTHING * laplace_ext(inner, inner=True)

    gains = sorted(set(FIELD_MIX))
    groups = [[f for f in range(fields) if FIELD_MIX[f] == g] for g in gains]
    surf = surf_ref[...]
    zero = jnp.zeros_like(surf)

    def step(level, below_mix, above_mix, ratios, parts, sources):
        new_ratios, new_parts = [], list(parts)
        for gi, gain in enumerate(gains):
            below = gain * below_mix
            above = gain * above_mix
            pivot = ((1.0 + below) + above) - below * ratios[gi]
            scale = 1.0 / pivot
            if level is not None:
                ratio = above * scale
                ratio_ref[gi, level] = ratio
                new_ratios.append(ratio)
            for f in groups[gi]:
                value = (sources[f] + below * parts[f]) * scale
                out_ref[f, level if level is not None else levels - 1] = value
                new_parts[f] = value
        return tuple(new_ratios), tuple(new_parts)

    def forward(level, carry):
        below_mix, ratios, parts, sources = carry
        upcoming = tuple(smoothed(f, level + 1) for f in range(fields))
        mix = base_ref[level] + surf * decay_ref[level]
        ratios, parts = step(level, below_mix, mix, ratios, parts, sources)
        return (mix, ratios, parts, upcoming)

    first = tuple(smoothed(f, 0) for f in range(fields))
    carry = (zero, tuple(zero for _ in gains), tuple(zero for _ in range(fields)), first)
    last_mix, ratios, parts, sources = lax.fori_loop(0, levels - 1, forward, carry)
    step(None, last_mix, zero, ratios, parts, sources)

    def backward(i, later):
        level = levels - 2 - i
        result = []
        for gi in range(len(gains)):
            ratio = ratio_ref[gi, level]
            for f in groups[gi]:
                value = out_ref[f, level] + ratio * later[f]
                out_ref[f, level] = value
                result.append((f, value))
        result.sort(key=lambda item: item[0])
        return tuple(v for _, v in result)

    final = tuple(out_ref[f, levels - 1] for f in range(fields))
    lax.fori_loop(0, levels - 1, backward, final, unroll=2)
    land = land_ref[...]
    for f in range(fields):
        back_ref[f] = land * out_ref[f, 0]


def tridiagonal(pieces, mask, shape, mixing_base, surface, land):
    fields, levels = shape[0], shape[1]
    decay_table = np.array(
        [math.exp(-level / DEPTH_SCALE) for level in range(levels)], dtype=np.float32
    )
    vmem = pltpu.MemorySpace.VMEM
    return pl.pallas_call(
        tridiagonal_kernel,
        out_shape=(
            jax.ShapeDtypeStruct(shape, jnp.float32),
            jax.ShapeDtypeStruct((fields,) + shape[2:], jnp.float32),
        ),
        in_specs=[pl.BlockSpec(memory_space=pltpu.MemorySpace.SMEM)]
        + [pl.BlockSpec(memory_space=vmem)] * (len(pieces) + 4),
        out_specs=(pl.BlockSpec(memory_space=vmem), pl.BlockSpec(memory_space=vmem)),
        scratch_shapes=[
            pltpu.VMEM((len(set(FIELD_MIX)), levels) + shape[2:], jnp.float32),
            pltpu.VMEM((5,) + mask.shape, jnp.float32),
        ],
    )(jnp.asarray(decay_table), *pieces, mask, mixing_base, surface, land)


def split_parts(values):
    high = values.astype(jnp.bfloat16)
    low = (values - high.astype(jnp.float32)).astype(jnp.bfloat16)
    return high, low


def matmul_exact(parts, other, contract):
    numbers = (((1,), (contract,)), ((), ()))
    total = None
    for part in parts:
        product = lax.dot_general(part, other, numbers, preferred_element_type=jnp.float32)
        total = product if total is None else total + product
    return total


def gather_kernel(recv_ref, index_ref, weight_ref, *after_and_out):
    out_ref = after_and_out[-1]
    stacked, lanes = recv_ref.shape
    fields, rows, cols = out_ref.shape
    segments = stacked // fields
    items = index_ref.shape[0] // rows
    parts = split_parts(recv_ref[...])
    lane_iota = lax.broadcasted_iota(jnp.int32, (lanes, cols), 0)
    segment_iota = lax.broadcasted_iota(jnp.int32, (fields, segments, cols), 1)

    def row_step(y, carry):
        total = None
        for item in range(items):
            index = index_ref[pl.ds(item * rows + y, 1), :]
            onehot = (lane_iota == index % lanes).astype(jnp.bfloat16)
            chosen = matmul_exact(parts, onehot, 0).reshape(fields, segments, cols)
            hit = segment_iota == (index // lanes)[None]
            picked = jnp.sum(jnp.where(hit, chosen, 0.0), axis=1)
            term = weight_ref[pl.ds(item * rows + y, 1), :] * picked
            total = term if total is None else total + term
        out_ref[:, pl.ds(y, 1), :] = total[:, None, :]
        return carry

    lax.fori_loop(0, rows, row_step, 0, unroll=True)


def scatter_kernel(back_ref, index_ref, weight_ref, out_ref):
    fields, rows, cols = back_ref.shape
    stacked, lanes = out_ref.shape
    segments = stacked // fields
    items = index_ref.shape[0] // rows
    lane_iota = lax.broadcasted_iota(jnp.int32, (lanes, cols), 0)
    segment_iota = lax.broadcasted_iota(jnp.int32, (fields, segments, cols), 1)

    def row_step(y, total):
        back = back_ref[:, pl.ds(y, 1), :]
        for item in range(items):
            index = index_ref[pl.ds(item * rows + y, 1), :]
            onehot = (lane_iota == index % lanes).astype(jnp.bfloat16)
            weighted = weight_ref[pl.ds(item * rows + y, 1), :][None] * back
            hit = segment_iota == (index // lanes)[None]
            spread = jnp.where(hit, weighted, 0.0).reshape(stacked, cols)
            total = total + matmul_exact(split_parts(spread), onehot, 1)
        return total

    out_ref[...] = lax.fori_loop(
        0, rows, row_step, jnp.zeros((stacked, lanes), jnp.float32), unroll=True
    )


def remap_call(kernel, out_shape, *operands, after=()):
    vmem = pltpu.MemorySpace.VMEM
    return pl.pallas_call(
        kernel,
        out_shape=jax.ShapeDtypeStruct(out_shape, jnp.float32),
        in_specs=[pl.BlockSpec(memory_space=vmem)] * len(operands)
        + [pl.BlockSpec(memory_space=pl.ANY)] * len(after),
        out_specs=pl.BlockSpec(memory_space=vmem),
    )(*operands, *after)


def sum_over(values, axis):
    count = lax.axis_size(axis)
    if count & (count - 1):
        return lax.psum(values, axis)
    step = 1
    while step < count:
        pairs = [(i, i ^ step) for i in range(count)]
        values = values + lax.ppermute(values, axis, pairs)
        step *= 2
    return values


def lat_edges(marks, width):
    lat_count = lax.axis_size("lat")
    where_lat = lax.axis_index("lat")
    rows = lax.broadcasted_iota(jnp.int32, marks.shape, 0)
    keep_top = jnp.logical_or(where_lat > 0, rows >= width)
    keep_bottom = jnp.logical_or(where_lat < lat_count - 1, rows < marks.shape[0] - width)
    return jnp.where(jnp.logical_and(keep_top, keep_bottom), marks, 0.0)


def single_rim(values):
    return with_halo(values, (("lat", 2), ("lon", 3)), 1)


def shards(
    adjoint_state,
    mixing_base,
    atm_flux,
    send_count,
    send_segment,
    cover_index,
    cover_weight,
    land_mask,
):
    lat_count = lax.axis_size("lat")
    owned = atm_flux.shape[1]
    counts = send_count[0]
    capacity = send_segment.shape[1] // lat_count
    starts = jnp.cumsum(counts) - counts
    column = jnp.arange(capacity, dtype=jnp.int32)
    places = jnp.minimum(starts[:, None] + column[None, :], send_segment.shape[1] - 1)
    chosen = send_segment[0][places]
    live_slot = column[None, :] < counts[:, None]
    outgoing = atm_flux[:, chosen, :]
    received = lax.all_to_all(outgoing, "lat", split_axis=1, concat_axis=1, tiled=True)
    items, rows, cols = cover_index.shape
    fields = received.shape[0]
    flat_recv = received.reshape(-1, received.shape[-1])
    index_rows = cover_index.reshape(items * rows, cols)
    weight_rows = cover_weight.reshape(items * rows, cols)
    land = land_mask.astype(jnp.float32)
    *pieces, mask = extended_planes(adjoint_state, land_mask, HALO)
    forcing = remap_call(
        gather_kernel, (fields, rows, cols), flat_recv, index_rows, weight_rows, after=tuple(pieces[1:])
    )
    surface = WIND_GAIN * (forcing[2] * forcing[2] + forcing[3] * forcing[3]) + jax.nn.softplus(
        forcing[1] - forcing[0]
    )
    state_adjoint, flux_back = tridiagonal(pieces, mask, adjoint_state.shape, mixing_base, surface, land)
    buffer = remap_call(scatter_kernel, flat_recv.shape, flux_back, index_rows, weight_rows)
    returned = lax.all_to_all(
        buffer.reshape(received.shape), "lat", split_axis=1, concat_axis=1, tiled=True
    )
    owned_ids = lax.broadcasted_iota(jnp.int32, (owned,) + chosen.shape, 0)
    picks = jnp.logical_and(owned_ids == chosen[None], live_slot[None]).astype(jnp.float32)
    owner_sum = jnp.einsum(
        "sdc,fdck->fsk", picks, returned, precision=lax.Precision.HIGHEST
    )
    flux_adjoint = sum_over(owner_sum, "lon")
    return (state_adjoint, flux_adjoint)


def solution(mesh):
    in_specs = (
        P(None, None, "lat", "lon"),
        P(None, "lat", "lon"),
        P(None, "lat", None),
        P("lat", "lon"),
        P("lat", "lon"),
        P(None, "lat", "lon"),
        P(None, "lat", "lon"),
        P("lat", "lon"),
    )
    out_specs = (P(None, None, "lat", "lon"), P(None, "lat", None))
    return jax.shard_map(shards, mesh=mesh, in_specs=in_specs, out_specs=out_specs, check_vma=False)
```

```python
import math

import jax
import jax.numpy as jnp
import numpy as np
from jax import lax
from jax.experimental import pallas as pl
from jax.experimental.pallas import tpu as pltpu
from jax.sharding import PartitionSpec as P

SMOOTHING = 0.02
WIND_GAIN = 1.0
DEPTH_SCALE = 12.0
FIELD_MIX = (1.0, 1.0, 2.0, 2.0)


HALO = 4


def from_neighbours(block, axis, dim, width):
    count = lax.axis_size(axis)
    to_prev = [(i, (i - 1) % count) for i in range(count)]
    to_next = [(i, (i + 1) % count) for i in range(count)]
    size = block.shape[dim]
    from_next = lax.ppermute(lax.slice_in_dim(block, 0, width, axis=dim), axis, to_prev)
    from_prev = lax.ppermute(lax.slice_in_dim(block, size - width, size, axis=dim), axis, to_next)
    return from_next, from_prev


def extended_planes(values, land_mask, width):
    fields, levels, rows, cols = values.shape
    planes = values.reshape(fields * levels, rows, cols)
    coast = land_mask.astype(jnp.float32)[None]
    stack = jnp.concatenate([planes, coast], axis=0)
    south, north = from_neighbours(stack, "lat", 1, width)
    tile = 128
    east_tile, west_tile = from_neighbours(stack, "lon", 2, tile)
    lane = lax.broadcasted_iota(jnp.int32, east_tile.shape, 2)
    sides = jnp.where(lane < width, east_tile, west_tile)
    corner_south, corner_north = from_neighbours(sides, "lat", 1, width)
    edge_tile = jnp.concatenate([sides, corner_south, corner_north], axis=1)
    halo_rows = jnp.concatenate([south, north], axis=1)
    coast_plane = jnp.concatenate(
        [jnp.concatenate([stack[-1], halo_rows[-1]], axis=0), edge_tile[-1]], axis=1
    )
    lat_count = lax.axis_size("lat")
    where_lat = lax.axis_index("lat")
    row = lax.broadcasted_iota(jnp.int32, coast_plane.shape, 0)
    outside = jnp.logical_or(
        jnp.logical_and(where_lat == 0, row >= rows + width),
        jnp.logical_and(where_lat == lat_count - 1, jnp.logical_and(row >= rows, row < rows + width)),
    )
    mask = jnp.where(outside, 0.0, coast_plane)
    return planes, halo_rows, edge_tile, mask


def with_halo(block, sides, width):
    for axis, dim in sides:
        count = lax.axis_size(axis)
        forward = [(i, i + 1) for i in range(count - 1)]
        forward.append((count - 1, 0))
        backward = [(target, source) for source, target in forward]
        low = lax.ppermute(
            lax.slice_in_dim(block, block.shape[dim] - width, None, axis=dim), axis, forward
        )
        high = lax.ppermute(lax.slice_in_dim(block, 0, width, axis=dim), axis, backward)
        block = jnp.concatenate([low, block, high], axis=dim)
    return block


def laplace(values, marks):
    centre = values[..., 1:-1, 1:-1]
    north = marks[:-2, 1:-1] * (values[..., :-2, 1:-1] - centre)
    south = marks[2:, 1:-1] * (values[..., 2:, 1:-1] - centre)
    west = marks[1:-1, :-2] * (values[..., 1:-1, :-2] - centre)
    east = marks[1:-1, 2:] * (values[..., 1:-1, 2:] - centre)
    return marks[1:-1, 1:-1] * (north + south + west + east)


def tridiagonal_kernel(
    decay_ref, inner_ref, rows_ref, edge_ref, mask_ref, base_ref, surf_ref, land_ref,
    out_ref, back_ref, ratio_ref, marks_ref,
):
    fields, levels = out_ref.shape[0], out_ref.shape[1]
    rows, cols = out_ref.shape[2], out_ref.shape[3]
    tall, wide = mask_ref.shape
    marks = mask_ref[...]
    marks_ref[0] = marks * pltpu.roll(marks, 1, 0)
    marks_ref[1] = marks * pltpu.roll(marks, tall - 1, 0)
    marks_ref[2] = marks * pltpu.roll(marks, 1, 1)
    marks_ref[3] = marks * pltpu.roll(marks, wide - 1, 1)
    marks_ref[4] = (marks_ref[0] + marks_ref[1]) + (marks_ref[2] + marks_ref[3])

    def laplace_ext(values, inner=False):
        shifted = [
            pltpu.roll(values, 1, 0),
            pltpu.roll(values, tall - 1, 0),
            pltpu.roll(values, 1, 1),
            pltpu.roll(values, wide - 1, 1),
        ]
        if inner:
            shifted = [part[:rows, :cols] for part in shifted]
            values = values[:rows, :cols]
            weight = [marks_ref[i, :rows, :cols] for i in range(5)]
        else:
            weight = [marks_ref[i] for i in range(5)]
        vertical = weight[0] * shifted[0] + weight[1] * shifted[1]
        across = weight[2] * shifted[2] + weight[3] * shifted[3]
        return (vertical + across) - weight[4] * values

    def smoothed(f, level):
        plane = f * levels + level
        values = jnp.concatenate([inner_ref[plane], rows_ref[plane]], axis=0)
        values = jnp.concatenate([values, edge_ref[plane]], axis=1)
        inner = laplace_ext(values)
        values = values - SMOOTHING * laplace_ext(inner)
        inner = laplace_ext(values)
        return values[:rows, :cols] - SMOOTHING * laplace_ext(inner, inner=True)

    gains = sorted(set(FIELD_MIX))
    groups = [[f for f in range(fields) if FIELD_MIX[f] == g] for g in gains]
    surf = surf_ref[...]
    zero = jnp.zeros_like(surf)

    def step(level, below_mix, above_mix, ratios, parts, sources):
        new_ratios, new_parts = [], list(parts)
        for gi, gain in enumerate(gains):
            below = gain * below_mix
            above = gain * above_mix
            pivot = ((1.0 + below) + above) - below * ratios[gi]
            scale = 1.0 / pivot
            if level is not None:
                ratio = above * scale
                ratio_ref[gi, level] = ratio
                new_ratios.append(ratio)
            for f in groups[gi]:
                value = (sources[f] + below * parts[f]) * scale
                out_ref[f, level if level is not None else levels - 1] = value
                new_parts[f] = value
        return tuple(new_ratios), tuple(new_parts)

    def forward(level, carry):
        below_mix, ratios, parts, sources = carry
        upcoming = tuple(smoothed(f, level + 1) for f in range(fields))
        mix = base_ref[level] + surf * decay_ref[level]
        ratios, parts = step(level, below_mix, mix, ratios, parts, sources)
        return (mix, ratios, parts, upcoming)

    first = tuple(smoothed(f, 0) for f in range(fields))
    carry = (zero, tuple(zero for _ in gains), tuple(zero for _ in range(fields)), first)
    last_mix, ratios, parts, sources = lax.fori_loop(0, levels - 1, forward, carry)
    step(None, last_mix, zero, ratios, parts, sources)

    def backward(i, later):
        level = levels - 2 - i
        result = []
        for gi in range(len(gains)):
            ratio = ratio_ref[gi, level]
            for f in groups[gi]:
                value = out_ref[f, level] + ratio * later[f]
                out_ref[f, level] = value
                result.append((f, value))
        result.sort(key=lambda item: item[0])
        return tuple(v for _, v in result)

    final = tuple(out_ref[f, levels - 1] for f in range(fields))
    lax.fori_loop(0, levels - 1, backward, final, unroll=2)
    land = land_ref[...]
    for f in range(fields):
        back_ref[f] = land * out_ref[f, 0]


def tridiagonal(pieces, mask, shape, mixing_base, surface, land):
    fields, levels = shape[0], shape[1]
    decay_table = np.array(
        [math.exp(-level / DEPTH_SCALE) for level in range(levels)], dtype=np.float32
    )
    vmem = pltpu.MemorySpace.VMEM
    return pl.pallas_call(
        tridiagonal_kernel,
        out_shape=(
            jax.ShapeDtypeStruct(shape, jnp.float32),
            jax.ShapeDtypeStruct((fields,) + shape[2:], jnp.float32),
        ),
        in_specs=[pl.BlockSpec(memory_space=pltpu.MemorySpace.SMEM)]
        + [pl.BlockSpec(memory_space=vmem)] * (len(pieces) + 4),
        out_specs=(pl.BlockSpec(memory_space=vmem), pl.BlockSpec(memory_space=vmem)),
        scratch_shapes=[
            pltpu.VMEM((len(set(FIELD_MIX)), levels) + shape[2:], jnp.float32),
            pltpu.VMEM((5,) + mask.shape, jnp.float32),
        ],
    )(jnp.asarray(decay_table), *pieces, mask, mixing_base, surface, land)


def split_parts(values):
    high = values.astype(jnp.bfloat16)
    low = (values - high.astype(jnp.float32)).astype(jnp.bfloat16)
    return high, low


def matmul_exact(parts, other, contract):
    numbers = (((1,), (contract,)), ((), ()))
    total = None
    for part in parts:
        product = lax.dot_general(part, other, numbers, preferred_element_type=jnp.float32)
        total = product if total is None else total + product
    return total


def gather_kernel(recv_ref, index_ref, weight_ref, *after_and_out):
    out_ref = after_and_out[-1]
    stacked, lanes = recv_ref.shape
    fields, rows, cols = out_ref.shape
    segments = stacked // fields
    items = index_ref.shape[0] // rows
    parts = split_parts(recv_ref[...])
    lane_iota = lax.broadcasted_iota(jnp.int32, (lanes, cols), 0)
    segment_iota = lax.broadcasted_iota(jnp.int32, (fields, segments, cols), 1)

    def row_step(y, carry):
        total = None
        for item in range(items):
            index = index_ref[pl.ds(item * rows + y, 1), :]
            onehot = (lane_iota == index % lanes).astype(jnp.bfloat16)
            chosen = matmul_exact(parts, onehot, 0).reshape(fields, segments, cols)
            hit = segment_iota == (index // lanes)[None]
            picked = jnp.sum(jnp.where(hit, chosen, 0.0), axis=1)
            term = weight_ref[pl.ds(item * rows + y, 1), :] * picked
            total = term if total is None else total + term
        out_ref[:, pl.ds(y, 1), :] = total[:, None, :]
        return carry

    lax.fori_loop(0, rows, row_step, 0, unroll=True)


def scatter_kernel(back_ref, index_ref, weight_ref, out_ref):
    fields, rows, cols = back_ref.shape
    stacked, lanes = out_ref.shape
    segments = stacked // fields
    items = index_ref.shape[0] // rows
    lane_iota = lax.broadcasted_iota(jnp.int32, (lanes, cols), 0)
    segment_iota = lax.broadcasted_iota(jnp.int32, (fields, segments, cols), 1)

    def row_step(y, total):
        back = back_ref[:, pl.ds(y, 1), :]
        for item in range(items):
            index = index_ref[pl.ds(item * rows + y, 1), :]
            onehot = (lane_iota == index % lanes).astype(jnp.bfloat16)
            weighted = weight_ref[pl.ds(item * rows + y, 1), :][None] * back
            hit = segment_iota == (index // lanes)[None]
            spread = jnp.where(hit, weighted, 0.0).reshape(stacked, cols)
            total = total + matmul_exact(split_parts(spread), onehot, 1)
        return total

    out_ref[...] = lax.fori_loop(
        0, rows, row_step, jnp.zeros((stacked, lanes), jnp.float32), unroll=True
    )


def remap_call(kernel, out_shape, *operands, after=()):
    vmem = pltpu.MemorySpace.VMEM
    return pl.pallas_call(
        kernel,
        out_shape=jax.ShapeDtypeStruct(out_shape, jnp.float32),
        in_specs=[pl.BlockSpec(memory_space=vmem)] * len(operands)
        + [pl.BlockSpec(memory_space=pl.ANY)] * len(after),
        out_specs=pl.BlockSpec(memory_space=vmem),
    )(*operands, *after)


def sum_over(values, axis):
    count = lax.axis_size(axis)
    if count & (count - 1):
        return lax.psum(values, axis)
    step = 1
    while step < count:
        pairs = [(i, i ^ step) for i in range(count)]
        values = values + lax.ppermute(values, axis, pairs)
        step *= 2
    return values


def lat_edges(marks, width):
    lat_count = lax.axis_size("lat")
    where_lat = lax.axis_index("lat")
    rows = lax.broadcasted_iota(jnp.int32, marks.shape, 0)
    keep_top = jnp.logical_or(where_lat > 0, rows >= width)
    keep_bottom = jnp.logical_or(where_lat < lat_count - 1, rows < marks.shape[0] - width)
    return jnp.where(jnp.logical_and(keep_top, keep_bottom), marks, 0.0)


def single_rim(values):
    return with_halo(values, (("lat", 2), ("lon", 3)), 1)


def shards(
    adjoint_state,
    mixing_base,
    atm_flux,
    send_count,
    send_segment,
    cover_index,
    cover_weight,
    land_mask,
):
    lat_count = lax.axis_size("lat")
    owned = atm_flux.shape[1]
    counts = send_count[0]
    capacity = send_segment.shape[1] // lat_count
    starts = jnp.cumsum(counts) - counts
    column = jnp.arange(capacity, dtype=jnp.int32)
    places = jnp.minimum(starts[:, None] + column[None, :], send_segment.shape[1] - 1)
    chosen = send_segment[0][places]
    live_slot = column[None, :] < counts[:, None]
    outgoing = atm_flux[:, chosen, :]
    received = lax.all_to_all(outgoing, "lat", split_axis=1, concat_axis=1, tiled=True)
    items, rows, cols = cover_index.shape
    fields = received.shape[0]
    flat_recv = received.reshape(-1, received.shape[-1])
    index_rows = cover_index.reshape(items * rows, cols)
    weight_rows = cover_weight.reshape(items * rows, cols)
    land = land_mask.astype(jnp.float32)
    *pieces, mask = extended_planes(adjoint_state, land_mask, HALO)
    forcing = remap_call(
        gather_kernel, (fields, rows, cols), flat_recv, index_rows, weight_rows, after=tuple(pieces[1:])
    )
    surface = WIND_GAIN * (forcing[2] * forcing[2] + forcing[3] * forcing[3]) + jax.nn.softplus(
        forcing[1] - forcing[0]
    )
    state_adjoint, flux_back = tridiagonal(pieces, mask, adjoint_state.shape, mixing_base, surface, land)
    buffer = remap_call(scatter_kernel, flat_recv.shape, flux_back, index_rows, weight_rows)
    returned = lax.all_to_all(
        buffer.reshape(received.shape), "lat", split_axis=1, concat_axis=1, tiled=True
    )
    owned_ids = lax.broadcasted_iota(jnp.int32, (owned,) + chosen.shape, 0)
    picks = jnp.logical_and(owned_ids == chosen[None], live_slot[None]).astype(jnp.float32)
    owner_sum = jnp.einsum(
        "sdc,fdck->fsk", picks, returned, precision=lax.Precision.HIGHEST
    )
    flux_adjoint = sum_over(owner_sum, "lon")
    return (state_adjoint, flux_adjoint)


def solution(mesh):
    in_specs = (
        P(None, None, "lat", "lon"),
        P(None, "lat", "lon"),
        P(None, "lat", None),
        P("lat", "lon"),
        P("lat", "lon"),
        P(None, "lat", "lon"),
        P(None, "lat", "lon"),
        P("lat", "lon"),
    )
    out_specs = (P(None, None, "lat", "lon"), P(None, "lat", None))
    return jax.shard_map(shards, mesh=mesh, in_specs=in_specs, out_specs=out_specs, check_vma=False)
```

```python
import math

import jax
import jax.numpy as jnp
import numpy as np
from jax import lax
from jax.experimental import pallas as pl
from jax.experimental.pallas import tpu as pltpu
from jax.sharding import PartitionSpec as P

SMOOTHING = 0.02
WIND_GAIN = 1.0
DEPTH_SCALE = 12.0
FIELD_MIX = (1.0, 1.0, 2.0, 2.0)


HALO = 4


def from_neighbours(block, axis, dim, width):
    count = lax.axis_size(axis)
    to_prev = [(i, (i - 1) % count) for i in range(count)]
    to_next = [(i, (i + 1) % count) for i in range(count)]
    size = block.shape[dim]
    from_next = lax.ppermute(lax.slice_in_dim(block, 0, width, axis=dim), axis, to_prev)
    from_prev = lax.ppermute(lax.slice_in_dim(block, size - width, size, axis=dim), axis, to_next)
    return from_next, from_prev


def extended_planes(values, land_mask, width):
    fields, levels, rows, cols = values.shape
    planes = values.reshape(fields * levels, rows, cols)
    coast = land_mask.astype(jnp.float32)[None]
    stack = jnp.concatenate([planes, coast], axis=0)
    south, north = from_neighbours(stack, "lat", 1, width)
    east, west = from_neighbours(stack, "lon", 2, width)
    sides = jnp.concatenate([east, west], axis=2)
    corner_south, corner_north = from_neighbours(sides, "lat", 1, width)
    wide = -(-(2 * width) // 128) * 128
    edges = jnp.concatenate([sides, corner_south, corner_north], axis=1)
    gap = jnp.zeros(edges.shape[:2] + (wide - 2 * width,), jnp.float32)
    edge_tile = jnp.concatenate([edges[:, :, :width], gap, edges[:, :, width:]], axis=2)
    halo_rows = jnp.concatenate([south, north], axis=1)
    coast_plane = jnp.concatenate(
        [jnp.concatenate([stack[-1], halo_rows[-1]], axis=0), edge_tile[-1]], axis=1
    )
    lat_count = lax.axis_size("lat")
    where_lat = lax.axis_index("lat")
    row = lax.broadcasted_iota(jnp.int32, coast_plane.shape, 0)
    outside = jnp.logical_or(
        jnp.logical_and(where_lat == 0, row >= rows + width),
        jnp.logical_and(where_lat == lat_count - 1, jnp.logical_and(row >= rows, row < rows + width)),
    )
    mask = jnp.where(outside, 0.0, coast_plane)
    return planes, halo_rows, edge_tile, mask


def with_halo(block, sides, width):
    for axis, dim in sides:
        count = lax.axis_size(axis)
        forward = [(i, i + 1) for i in range(count - 1)]
        forward.append((count - 1, 0))
        backward = [(target, source) for source, target in forward]
        low = lax.ppermute(
            lax.slice_in_dim(block, block.shape[dim] - width, None, axis=dim), axis, forward
        )
        high = lax.ppermute(lax.slice_in_dim(block, 0, width, axis=dim), axis, backward)
        block = jnp.concatenate([low, block, high], axis=dim)
    return block


def laplace(values, marks):
    centre = values[..., 1:-1, 1:-1]
    north = marks[:-2, 1:-1] * (values[..., :-2, 1:-1] - centre)
    south = marks[2:, 1:-1] * (values[..., 2:, 1:-1] - centre)
    west = marks[1:-1, :-2] * (values[..., 1:-1, :-2] - centre)
    east = marks[1:-1, 2:] * (values[..., 1:-1, 2:] - centre)
    return marks[1:-1, 1:-1] * (north + south + west + east)


def tridiagonal_kernel(
    decay_ref, inner_ref, rows_ref, edge_ref, mask_ref, base_ref, surf_ref, land_ref,
    out_ref, back_ref, ratio_ref, marks_ref,
):
    fields, levels = out_ref.shape[0], out_ref.shape[1]
    rows, cols = out_ref.shape[2], out_ref.shape[3]
    tall, wide = mask_ref.shape
    marks = mask_ref[...]
    marks_ref[0] = marks * pltpu.roll(marks, 1, 0)
    marks_ref[1] = marks * pltpu.roll(marks, tall - 1, 0)
    marks_ref[2] = marks * pltpu.roll(marks, 1, 1)
    marks_ref[3] = marks * pltpu.roll(marks, wide - 1, 1)
    marks_ref[4] = (marks_ref[0] + marks_ref[1]) + (marks_ref[2] + marks_ref[3])

    def laplace_ext(values, inner=False):
        shifted = [
            pltpu.roll(values, 1, 0),
            pltpu.roll(values, tall - 1, 0),
            pltpu.roll(values, 1, 1),
            pltpu.roll(values, wide - 1, 1),
        ]
        if inner:
            shifted = [part[:rows, :cols] for part in shifted]
            values = values[:rows, :cols]
            weight = [marks_ref[i, :rows, :cols] for i in range(5)]
        else:
            weight = [marks_ref[i] for i in range(5)]
        vertical = weight[0] * shifted[0] + weight[1] * shifted[1]
        across = weight[2] * shifted[2] + weight[3] * shifted[3]
        return (vertical + across) - weight[4] * values

    def smoothed(f, level):
        plane = f * levels + level
        values = jnp.concatenate([inner_ref[plane], rows_ref[plane]], axis=0)
        values = jnp.concatenate([values, edge_ref[plane]], axis=1)
        inner = laplace_ext(values)
        values = values - SMOOTHING * laplace_ext(inner)
        inner = laplace_ext(values)
        return values[:rows, :cols] - SMOOTHING * laplace_ext(inner, inner=True)

    gains = sorted(set(FIELD_MIX))
    groups = [[f for f in range(fields) if FIELD_MIX[f] == g] for g in gains]
    surf = surf_ref[...]
    zero = jnp.zeros_like(surf)

    def step(level, below_mix, above_mix, ratios, parts, sources):
        new_ratios, new_parts = [], list(parts)
        for gi, gain in enumerate(gains):
            below = gain * below_mix
            above = gain * above_mix
            pivot = ((1.0 + below) + above) - below * ratios[gi]
            scale = 1.0 / pivot
            if level is not None:
                ratio = above * scale
                ratio_ref[gi, level] = ratio
                new_ratios.append(ratio)
            for f in groups[gi]:
                value = (sources[f] + below * parts[f]) * scale
                out_ref[f, level if level is not None else levels - 1] = value
                new_parts[f] = value
        return tuple(new_ratios), tuple(new_parts)

    def forward(level, carry):
        below_mix, ratios, parts, sources = carry
        upcoming = tuple(smoothed(f, level + 1) for f in range(fields))
        mix = base_ref[level] + surf * decay_ref[level]
        ratios, parts = step(level, below_mix, mix, ratios, parts, sources)
        return (mix, ratios, parts, upcoming)

    first = tuple(smoothed(f, 0) for f in range(fields))
    carry = (zero, tuple(zero for _ in gains), tuple(zero for _ in range(fields)), first)
    last_mix, ratios, parts, sources = lax.fori_loop(0, levels - 1, forward, carry)
    step(None, last_mix, zero, ratios, parts, sources)

    def backward(i, later):
        level = levels - 2 - i
        result = []
        for gi in range(len(gains)):
            ratio = ratio_ref[gi, level]
            for f in groups[gi]:
                value = out_ref[f, level] + ratio * later[f]
                out_ref[f, level] = value
                result.append((f, value))
        result.sort(key=lambda item: item[0])
        return tuple(v for _, v in result)

    final = tuple(out_ref[f, levels - 1] for f in range(fields))
    lax.fori_loop(0, levels - 1, backward, final, unroll=2)
    land = land_ref[...]
    for f in range(fields):
        back_ref[f] = land * out_ref[f, 0]


def tridiagonal(pieces, mask, shape, mixing_base, surface, land):
    fields, levels = shape[0], shape[1]
    decay_table = np.array(
        [math.exp(-level / DEPTH_SCALE) for level in range(levels)], dtype=np.float32
    )
    vmem = pltpu.MemorySpace.VMEM
    return pl.pallas_call(
        tridiagonal_kernel,
        out_shape=(
            jax.ShapeDtypeStruct(shape, jnp.float32),
            jax.ShapeDtypeStruct((fields,) + shape[2:], jnp.float32),
        ),
        in_specs=[pl.BlockSpec(memory_space=pltpu.MemorySpace.SMEM)]
        + [pl.BlockSpec(memory_space=vmem)] * (len(pieces) + 4),
        out_specs=(pl.BlockSpec(memory_space=vmem), pl.BlockSpec(memory_space=vmem)),
        scratch_shapes=[
            pltpu.VMEM((len(set(FIELD_MIX)), levels) + shape[2:], jnp.float32),
            pltpu.VMEM((5,) + mask.shape, jnp.float32),
        ],
    )(jnp.asarray(decay_table), *pieces, mask, mixing_base, surface, land)


def split_parts(values):
    high = values.astype(jnp.bfloat16)
    low = (values - high.astype(jnp.float32)).astype(jnp.bfloat16)
    return high, low


def matmul_exact(parts, other, contract):
    numbers = (((1,), (contract,)), ((), ()))
    total = None
    for part in parts:
        product = lax.dot_general(part, other, numbers, preferred_element_type=jnp.float32)
        total = product if total is None else total + product
    return total


def gather_kernel(recv_ref, index_ref, weight_ref, *after_and_out):
    out_ref = after_and_out[-1]
    stacked, lanes = recv_ref.shape
    fields, rows, cols = out_ref.shape
    segments = stacked // fields
    items = index_ref.shape[0] // rows
    parts = split_parts(recv_ref[...])
    lane_iota = lax.broadcasted_iota(jnp.int32, (lanes, cols), 0)
    segment_iota = lax.broadcasted_iota(jnp.int32, (fields, segments, cols), 1)

    def row_step(y, carry):
        total = None
        for item in range(items):
            index = index_ref[pl.ds(item * rows + y, 1), :]
            onehot = (lane_iota == index % lanes).astype(jnp.bfloat16)
            chosen = matmul_exact(parts, onehot, 0).reshape(fields, segments, cols)
            hit = segment_iota == (index // lanes)[None]
            picked = jnp.sum(jnp.where(hit, chosen, 0.0), axis=1)
            term = weight_ref[pl.ds(item * rows + y, 1), :] * picked
            total = term if total is None else total + term
        out_ref[:, pl.ds(y, 1), :] = total[:, None, :]
        return carry

    lax.fori_loop(0, rows, row_step, 0, unroll=True)


def scatter_kernel(back_ref, index_ref, weight_ref, out_ref):
    fields, rows, cols = back_ref.shape
    stacked, lanes = out_ref.shape
    segments = stacked // fields
    items = index_ref.shape[0] // rows
    lane_iota = lax.broadcasted_iota(jnp.int32, (lanes, cols), 0)
    segment_iota = lax.broadcasted_iota(jnp.int32, (fields, segments, cols), 1)

    def row_step(y, total):
        back = back_ref[:, pl.ds(y, 1), :]
        for item in range(items):
            index = index_ref[pl.ds(item * rows + y, 1), :]
            onehot = (lane_iota == index % lanes).astype(jnp.bfloat16)
            weighted = weight_ref[pl.ds(item * rows + y, 1), :][None] * back
            hit = segment_iota == (index // lanes)[None]
            spread = jnp.where(hit, weighted, 0.0).reshape(stacked, cols)
            total = total + matmul_exact(split_parts(spread), onehot, 1)
        return total

    out_ref[...] = lax.fori_loop(
        0, rows, row_step, jnp.zeros((stacked, lanes), jnp.float32), unroll=True
    )


def remap_call(kernel, out_shape, *operands, after=()):
    vmem = pltpu.MemorySpace.VMEM
    return pl.pallas_call(
        kernel,
        out_shape=jax.ShapeDtypeStruct(out_shape, jnp.float32),
        in_specs=[pl.BlockSpec(memory_space=vmem)] * len(operands)
        + [pl.BlockSpec(memory_space=pl.ANY)] * len(after),
        out_specs=pl.BlockSpec(memory_space=vmem),
    )(*operands, *after)


def sum_over(values, axis):
    count = lax.axis_size(axis)
    where = lax.axis_index(axis)
    copies = [values] + [
        lax.ppermute(values, axis, [(i, (i + shift) % count) for i in range(count)])
        for shift in range(1, count)
    ]
    stacked = jnp.stack(copies)
    ordered = [
        lax.dynamic_index_in_dim(stacked, (where - owner) % count, 0, keepdims=False)
        for owner in range(count)
    ]
    while len(ordered) > 1:
        paired = [ordered[i] + ordered[i + 1] for i in range(0, len(ordered) - 1, 2)]
        ordered = paired + ordered[len(ordered) - len(ordered) % 2:]
    return ordered[0]


def lat_edges(marks, width):
    lat_count = lax.axis_size("lat")
    where_lat = lax.axis_index("lat")
    rows = lax.broadcasted_iota(jnp.int32, marks.shape, 0)
    keep_top = jnp.logical_or(where_lat > 0, rows >= width)
    keep_bottom = jnp.logical_or(where_lat < lat_count - 1, rows < marks.shape[0] - width)
    return jnp.where(jnp.logical_and(keep_top, keep_bottom), marks, 0.0)


def single_rim(values):
    return with_halo(values, (("lat", 2), ("lon", 3)), 1)


def shards(
    adjoint_state,
    mixing_base,
    atm_flux,
    send_count,
    send_segment,
    cover_index,
    cover_weight,
    land_mask,
):
    lat_count = lax.axis_size("lat")
    owned = atm_flux.shape[1]
    counts = send_count[0]
    capacity = send_segment.shape[1] // lat_count
    starts = jnp.cumsum(counts) - counts
    column = jnp.arange(capacity, dtype=jnp.int32)
    places = jnp.minimum(starts[:, None] + column[None, :], send_segment.shape[1] - 1)
    chosen = send_segment[0][places]
    live_slot = column[None, :] < counts[:, None]
    outgoing = atm_flux[:, chosen, :]
    received = lax.all_to_all(outgoing, "lat", split_axis=1, concat_axis=1, tiled=True)
    items, rows, cols = cover_index.shape
    fields = received.shape[0]
    flat_recv = received.reshape(-1, received.shape[-1])
    index_rows = cover_index.reshape(items * rows, cols)
    weight_rows = cover_weight.reshape(items * rows, cols)
    land = land_mask.astype(jnp.float32)
    *pieces, mask = extended_planes(adjoint_state, land_mask, HALO)
    forcing = remap_call(
        gather_kernel, (fields, rows, cols), flat_recv, index_rows, weight_rows, after=tuple(pieces[1:])
    )
    surface = WIND_GAIN * (forcing[2] * forcing[2] + forcing[3] * forcing[3]) + jax.nn.softplus(
        forcing[1] - forcing[0]
    )
    state_adjoint, flux_back = tridiagonal(pieces, mask, adjoint_state.shape, mixing_base, surface, land)
    buffer = remap_call(scatter_kernel, flat_recv.shape, flux_back, index_rows, weight_rows)
    returned = lax.all_to_all(
        buffer.reshape(received.shape), "lat", split_axis=1, concat_axis=1, tiled=True
    )
    owned_ids = lax.broadcasted_iota(jnp.int32, (owned,) + chosen.shape, 0)
    picks = jnp.logical_and(owned_ids == chosen[None], live_slot[None]).astype(jnp.float32)
    owner_sum = jnp.einsum(
        "sdc,fdck->fsk", picks, returned, precision=lax.Precision.HIGHEST
    )
    flux_adjoint = sum_over(owner_sum, "lon")
    return (state_adjoint, flux_adjoint)


def solution(mesh):
    in_specs = (
        P(None, None, "lat", "lon"),
        P(None, "lat", "lon"),
        P(None, "lat", None),
        P("lat", "lon"),
        P("lat", "lon"),
        P(None, "lat", "lon"),
        P(None, "lat", "lon"),
        P("lat", "lon"),
    )
    out_specs = (P(None, None, "lat", "lon"), P(None, "lat", None))
    return jax.shard_map(shards, mesh=mesh, in_specs=in_specs, out_specs=out_specs, check_vma=False)
```

```python
import math

import jax
import jax.numpy as jnp
import numpy as np
from jax import lax
from jax.experimental import pallas as pl
from jax.experimental.pallas import tpu as pltpu
from jax.sharding import PartitionSpec as P

SMOOTHING = 0.02
WIND_GAIN = 1.0
DEPTH_SCALE = 12.0
FIELD_MIX = (1.0, 1.0, 2.0, 2.0)


HALO = 4


def from_neighbours(block, axis, dim, width):
    count = lax.axis_size(axis)
    to_prev = [(i, (i - 1) % count) for i in range(count)]
    to_next = [(i, (i + 1) % count) for i in range(count)]
    size = block.shape[dim]
    from_next = lax.ppermute(lax.slice_in_dim(block, 0, width, axis=dim), axis, to_prev)
    from_prev = lax.ppermute(lax.slice_in_dim(block, size - width, size, axis=dim), axis, to_next)
    return from_next, from_prev


def extended_planes(values, land_mask, width):
    fields, levels, rows, cols = values.shape
    planes = values.reshape(fields * levels, rows, cols)
    coast = land_mask.astype(jnp.float32)[None]
    stack = jnp.concatenate([planes, coast], axis=0)
    east, west = from_neighbours(stack, "lon", 2, width)
    sides = jnp.concatenate([east, west], axis=2)
    wide_rows = jnp.concatenate([stack, sides], axis=2)
    south_wide, north_wide = from_neighbours(wide_rows, "lat", 1, width)
    south, corner_south = south_wide[:, :, :cols], south_wide[:, :, cols:]
    north, corner_north = north_wide[:, :, :cols], north_wide[:, :, cols:]
    wide = -(-(2 * width) // 128) * 128
    edges = jnp.concatenate([sides, corner_south, corner_north], axis=1)
    gap = jnp.zeros(edges.shape[:2] + (wide - 2 * width,), jnp.float32)
    edge_tile = jnp.concatenate([edges[:, :, :width], gap, edges[:, :, width:]], axis=2)
    halo_rows = jnp.concatenate([south, north], axis=1)
    coast_plane = jnp.concatenate(
        [jnp.concatenate([stack[-1], halo_rows[-1]], axis=0), edge_tile[-1]], axis=1
    )
    lat_count = lax.axis_size("lat")
    where_lat = lax.axis_index("lat")
    row = lax.broadcasted_iota(jnp.int32, coast_plane.shape, 0)
    outside = jnp.logical_or(
        jnp.logical_and(where_lat == 0, row >= rows + width),
        jnp.logical_and(where_lat == lat_count - 1, jnp.logical_and(row >= rows, row < rows + width)),
    )
    mask = jnp.where(outside, 0.0, coast_plane)
    return planes, halo_rows, edge_tile, mask


def with_halo(block, sides, width):
    for axis, dim in sides:
        count = lax.axis_size(axis)
        forward = [(i, i + 1) for i in range(count - 1)]
        forward.append((count - 1, 0))
        backward = [(target, source) for source, target in forward]
        low = lax.ppermute(
            lax.slice_in_dim(block, block.shape[dim] - width, None, axis=dim), axis, forward
        )
        high = lax.ppermute(lax.slice_in_dim(block, 0, width, axis=dim), axis, backward)
        block = jnp.concatenate([low, block, high], axis=dim)
    return block


def laplace(values, marks):
    centre = values[..., 1:-1, 1:-1]
    north = marks[:-2, 1:-1] * (values[..., :-2, 1:-1] - centre)
    south = marks[2:, 1:-1] * (values[..., 2:, 1:-1] - centre)
    west = marks[1:-1, :-2] * (values[..., 1:-1, :-2] - centre)
    east = marks[1:-1, 2:] * (values[..., 1:-1, 2:] - centre)
    return marks[1:-1, 1:-1] * (north + south + west + east)


def tridiagonal_kernel(
    decay_ref, inner_ref, rows_ref, edge_ref, mask_ref, base_ref, surf_ref, land_ref,
    out_ref, back_ref, ratio_ref, marks_ref,
):
    fields, levels = out_ref.shape[0], out_ref.shape[1]
    rows, cols = out_ref.shape[2], out_ref.shape[3]
    tall, wide = mask_ref.shape
    marks = mask_ref[...]
    marks_ref[0] = marks * pltpu.roll(marks, 1, 0)
    marks_ref[1] = marks * pltpu.roll(marks, tall - 1, 0)
    marks_ref[2] = marks * pltpu.roll(marks, 1, 1)
    marks_ref[3] = marks * pltpu.roll(marks, wide - 1, 1)
    marks_ref[4] = (marks_ref[0] + marks_ref[1]) + (marks_ref[2] + marks_ref[3])

    def laplace_ext(values, inner=False):
        shifted = [
            pltpu.roll(values, 1, 0),
            pltpu.roll(values, tall - 1, 0),
            pltpu.roll(values, 1, 1),
            pltpu.roll(values, wide - 1, 1),
        ]
        if inner:
            shifted = [part[:rows, :cols] for part in shifted]
            values = values[:rows, :cols]
            weight = [marks_ref[i, :rows, :cols] for i in range(5)]
        else:
            weight = [marks_ref[i] for i in range(5)]
        vertical = weight[0] * shifted[0] + weight[1] * shifted[1]
        across = weight[2] * shifted[2] + weight[3] * shifted[3]
        return (vertical + across) - weight[4] * values

    def smoothed(f, level):
        plane = f * levels + level
        values = jnp.concatenate([inner_ref[plane], rows_ref[plane]], axis=0)
        values = jnp.concatenate([values, edge_ref[plane]], axis=1)
        inner = laplace_ext(values)
        values = values - SMOOTHING * laplace_ext(inner)
        inner = laplace_ext(values)
        return values[:rows, :cols] - SMOOTHING * laplace_ext(inner, inner=True)

    gains = sorted(set(FIELD_MIX))
    groups = [[f for f in range(fields) if FIELD_MIX[f] == g] for g in gains]
    surf = surf_ref[...]
    zero = jnp.zeros_like(surf)

    def step(level, below_mix, above_mix, ratios, parts, sources):
        new_ratios, new_parts = [], list(parts)
        for gi, gain in enumerate(gains):
            below = gain * below_mix
            above = gain * above_mix
            pivot = ((1.0 + below) + above) - below * ratios[gi]
            scale = 1.0 / pivot
            if level is not None:
                ratio = above * scale
                ratio_ref[gi, level] = ratio
                new_ratios.append(ratio)
            for f in groups[gi]:
                value = (sources[f] + below * parts[f]) * scale
                out_ref[f, level if level is not None else levels - 1] = value
                new_parts[f] = value
        return tuple(new_ratios), tuple(new_parts)

    def forward(level, carry):
        below_mix, ratios, parts, sources = carry
        upcoming = tuple(smoothed(f, level + 1) for f in range(fields))
        mix = base_ref[level] + surf * decay_ref[level]
        ratios, parts = step(level, below_mix, mix, ratios, parts, sources)
        return (mix, ratios, parts, upcoming)

    first = tuple(smoothed(f, 0) for f in range(fields))
    carry = (zero, tuple(zero for _ in gains), tuple(zero for _ in range(fields)), first)
    last_mix, ratios, parts, sources = lax.fori_loop(0, levels - 1, forward, carry)
    step(None, last_mix, zero, ratios, parts, sources)

    def backward(i, later):
        level = levels - 2 - i
        result = []
        for gi in range(len(gains)):
            ratio = ratio_ref[gi, level]
            for f in groups[gi]:
                value = out_ref[f, level] + ratio * later[f]
                out_ref[f, level] = value
                result.append((f, value))
        result.sort(key=lambda item: item[0])
        return tuple(v for _, v in result)

    final = tuple(out_ref[f, levels - 1] for f in range(fields))
    lax.fori_loop(0, levels - 1, backward, final, unroll=2)
    land = land_ref[...]
    for f in range(fields):
        back_ref[f] = land * out_ref[f, 0]


def tridiagonal(pieces, mask, shape, mixing_base, surface, land):
    fields, levels = shape[0], shape[1]
    decay_table = np.array(
        [math.exp(-level / DEPTH_SCALE) for level in range(levels)], dtype=np.float32
    )
    vmem = pltpu.MemorySpace.VMEM
    return pl.pallas_call(
        tridiagonal_kernel,
        out_shape=(
            jax.ShapeDtypeStruct(shape, jnp.float32),
            jax.ShapeDtypeStruct((fields,) + shape[2:], jnp.float32),
        ),
        in_specs=[pl.BlockSpec(memory_space=pltpu.MemorySpace.SMEM)]
        + [pl.BlockSpec(memory_space=vmem)] * (len(pieces) + 4),
        out_specs=(pl.BlockSpec(memory_space=vmem), pl.BlockSpec(memory_space=vmem)),
        scratch_shapes=[
            pltpu.VMEM((len(set(FIELD_MIX)), levels) + shape[2:], jnp.float32),
            pltpu.VMEM((5,) + mask.shape, jnp.float32),
        ],
    )(jnp.asarray(decay_table), *pieces, mask, mixing_base, surface, land)


def split_parts(values):
    high = values.astype(jnp.bfloat16)
    low = (values - high.astype(jnp.float32)).astype(jnp.bfloat16)
    return high, low


def matmul_exact(parts, other, contract):
    numbers = (((1,), (contract,)), ((), ()))
    total = None
    for part in parts:
        product = lax.dot_general(part, other, numbers, preferred_element_type=jnp.float32)
        total = product if total is None else total + product
    return total


def gather_kernel(recv_ref, index_ref, weight_ref, *after_and_out):
    out_ref = after_and_out[-1]
    stacked, lanes = recv_ref.shape
    fields, rows, cols = out_ref.shape
    segments = stacked // fields
    items = index_ref.shape[0] // rows
    parts = split_parts(recv_ref[...])
    lane_iota = lax.broadcasted_iota(jnp.int32, (lanes, cols), 0)
    segment_iota = lax.broadcasted_iota(jnp.int32, (fields, segments, cols), 1)

    def row_step(y, carry):
        total = None
        for item in range(items):
            index = index_ref[pl.ds(item * rows + y, 1), :]
            onehot = (lane_iota == index % lanes).astype(jnp.bfloat16)
            chosen = matmul_exact(parts, onehot, 0).reshape(fields, segments, cols)
            hit = segment_iota == (index // lanes)[None]
            picked = jnp.sum(jnp.where(hit, chosen, 0.0), axis=1)
            term = weight_ref[pl.ds(item * rows + y, 1), :] * picked
            total = term if total is None else total + term
        out_ref[:, pl.ds(y, 1), :] = total[:, None, :]
        return carry

    lax.fori_loop(0, rows, row_step, 0, unroll=True)


def scatter_kernel(back_ref, index_ref, weight_ref, out_ref):
    fields, rows, cols = back_ref.shape
    stacked, lanes = out_ref.shape
    segments = stacked // fields
    items = index_ref.shape[0] // rows
    lane_iota = lax.broadcasted_iota(jnp.int32, (lanes, cols), 0)
    segment_iota = lax.broadcasted_iota(jnp.int32, (fields, segments, cols), 1)

    def row_step(y, total):
        back = back_ref[:, pl.ds(y, 1), :]
        for item in range(items):
            index = index_ref[pl.ds(item * rows + y, 1), :]
            onehot = (lane_iota == index % lanes).astype(jnp.bfloat16)
            weighted = weight_ref[pl.ds(item * rows + y, 1), :][None] * back
            hit = segment_iota == (index // lanes)[None]
            spread = jnp.where(hit, weighted, 0.0).reshape(stacked, cols)
            total = total + matmul_exact(split_parts(spread), onehot, 1)
        return total

    out_ref[...] = lax.fori_loop(
        0, rows, row_step, jnp.zeros((stacked, lanes), jnp.float32), unroll=True
    )


def remap_call(kernel, out_shape, *operands, after=()):
    vmem = pltpu.MemorySpace.VMEM
    return pl.pallas_call(
        kernel,
        out_shape=jax.ShapeDtypeStruct(out_shape, jnp.float32),
        in_specs=[pl.BlockSpec(memory_space=vmem)] * len(operands)
        + [pl.BlockSpec(memory_space=pl.ANY)] * len(after),
        out_specs=pl.BlockSpec(memory_space=vmem),
    )(*operands, *after)


def sum_over(values, axis):
    count = lax.axis_size(axis)
    where = lax.axis_index(axis)
    copies = [values] + [
        lax.ppermute(values, axis, [(i, (i + shift) % count) for i in range(count)])
        for shift in range(1, count)
    ]
    stacked = jnp.stack(copies)
    ordered = [
        lax.dynamic_index_in_dim(stacked, (where - owner) % count, 0, keepdims=False)
        for owner in range(count)
    ]
    while len(ordered) > 1:
        paired = [ordered[i] + ordered[i + 1] for i in range(0, len(ordered) - 1, 2)]
        ordered = paired + ordered[len(ordered) - len(ordered) % 2:]
    return ordered[0]


def lat_edges(marks, width):
    lat_count = lax.axis_size("lat")
    where_lat = lax.axis_index("lat")
    rows = lax.broadcasted_iota(jnp.int32, marks.shape, 0)
    keep_top = jnp.logical_or(where_lat > 0, rows >= width)
    keep_bottom = jnp.logical_or(where_lat < lat_count - 1, rows < marks.shape[0] - width)
    return jnp.where(jnp.logical_and(keep_top, keep_bottom), marks, 0.0)


def single_rim(values):
    return with_halo(values, (("lat", 2), ("lon", 3)), 1)


def shards(
    adjoint_state,
    mixing_base,
    atm_flux,
    send_count,
    send_segment,
    cover_index,
    cover_weight,
    land_mask,
):
    lat_count = lax.axis_size("lat")
    owned = atm_flux.shape[1]
    counts = send_count[0]
    capacity = send_segment.shape[1] // lat_count
    starts = jnp.cumsum(counts) - counts
    column = jnp.arange(capacity, dtype=jnp.int32)
    places = jnp.minimum(starts[:, None] + column[None, :], send_segment.shape[1] - 1)
    chosen = send_segment[0][places]
    live_slot = column[None, :] < counts[:, None]
    outgoing = atm_flux[:, chosen, :]
    received = lax.all_to_all(outgoing, "lat", split_axis=1, concat_axis=1, tiled=True)
    items, rows, cols = cover_index.shape
    fields = received.shape[0]
    flat_recv = received.reshape(-1, received.shape[-1])
    index_rows = cover_index.reshape(items * rows, cols)
    weight_rows = cover_weight.reshape(items * rows, cols)
    land = land_mask.astype(jnp.float32)
    *pieces, mask = extended_planes(adjoint_state, land_mask, HALO)
    forcing = remap_call(
        gather_kernel, (fields, rows, cols), flat_recv, index_rows, weight_rows, after=tuple(pieces[1:])
    )
    surface = WIND_GAIN * (forcing[2] * forcing[2] + forcing[3] * forcing[3]) + jax.nn.softplus(
        forcing[1] - forcing[0]
    )
    state_adjoint, flux_back = tridiagonal(pieces, mask, adjoint_state.shape, mixing_base, surface, land)
    buffer = remap_call(scatter_kernel, flat_recv.shape, flux_back, index_rows, weight_rows)
    returned = lax.all_to_all(
        buffer.reshape(received.shape), "lat", split_axis=1, concat_axis=1, tiled=True
    )
    owned_ids = lax.broadcasted_iota(jnp.int32, (owned,) + chosen.shape, 0)
    picks = jnp.logical_and(owned_ids == chosen[None], live_slot[None]).astype(jnp.float32)
    owner_sum = jnp.einsum(
        "sdc,fdck->fsk", picks, returned, precision=lax.Precision.HIGHEST
    )
    flux_adjoint = sum_over(owner_sum, "lon")
    return (state_adjoint, flux_adjoint)


def solution(mesh):
    in_specs = (
        P(None, None, "lat", "lon"),
        P(None, "lat", "lon"),
        P(None, "lat", None),
        P("lat", "lon"),
        P("lat", "lon"),
        P(None, "lat", "lon"),
        P(None, "lat", "lon"),
        P("lat", "lon"),
    )
    out_specs = (P(None, None, "lat", "lon"), P(None, "lat", None))
    return jax.shard_map(shards, mesh=mesh, in_specs=in_specs, out_specs=out_specs, check_vma=False)
```

```python
import math

import jax
import jax.numpy as jnp
import numpy as np
from jax import lax
from jax.experimental import pallas as pl
from jax.experimental.pallas import tpu as pltpu
from jax.sharding import PartitionSpec as P

SMOOTHING = 0.02
WIND_GAIN = 1.0
DEPTH_SCALE = 12.0
FIELD_MIX = (1.0, 1.0, 2.0, 2.0)


HALO = 4
SLOTS = 2


def from_neighbours(block, axis, dim, width):
    count = lax.axis_size(axis)
    to_prev = [(i, (i - 1) % count) for i in range(count)]
    to_next = [(i, (i + 1) % count) for i in range(count)]
    size = block.shape[dim]
    from_next = lax.ppermute(lax.slice_in_dim(block, 0, width, axis=dim), axis, to_prev)
    from_prev = lax.ppermute(lax.slice_in_dim(block, size - width, size, axis=dim), axis, to_next)
    return from_next, from_prev


def extended_planes(values, land_mask, width):
    fields, levels, rows, cols = values.shape
    planes = values.reshape(fields * levels, rows, cols)
    coast = land_mask.astype(jnp.float32)[None]
    stack = jnp.concatenate([planes, coast], axis=0)
    south, north = from_neighbours(stack, "lat", 1, width)
    east, west = from_neighbours(stack, "lon", 2, width)
    sides = jnp.concatenate([east, west], axis=2)
    corner_south, corner_north = from_neighbours(sides, "lat", 1, width)
    wide = -(-(2 * width) // 128) * 128
    edges = jnp.concatenate([sides, corner_south, corner_north], axis=1)
    gap = jnp.zeros(edges.shape[:2] + (wide - 2 * width,), jnp.float32)
    edge_tile = jnp.concatenate([edges[:, :, :width], gap, edges[:, :, width:]], axis=2)
    halo_rows = jnp.concatenate([south, north], axis=1)
    coast_plane = jnp.concatenate(
        [jnp.concatenate([stack[-1], halo_rows[-1]], axis=0), edge_tile[-1]], axis=1
    )
    lat_count = lax.axis_size("lat")
    where_lat = lax.axis_index("lat")
    row = lax.broadcasted_iota(jnp.int32, coast_plane.shape, 0)
    outside = jnp.logical_or(
        jnp.logical_and(where_lat == 0, row >= rows + width),
        jnp.logical_and(where_lat == lat_count - 1, jnp.logical_and(row >= rows, row < rows + width)),
    )
    mask = jnp.where(outside, 0.0, coast_plane)
    return planes, halo_rows, edge_tile, mask


def with_halo(block, sides, width):
    for axis, dim in sides:
        count = lax.axis_size(axis)
        forward = [(i, i + 1) for i in range(count - 1)]
        forward.append((count - 1, 0))
        backward = [(target, source) for source, target in forward]
        low = lax.ppermute(
            lax.slice_in_dim(block, block.shape[dim] - width, None, axis=dim), axis, forward
        )
        high = lax.ppermute(lax.slice_in_dim(block, 0, width, axis=dim), axis, backward)
        block = jnp.concatenate([low, block, high], axis=dim)
    return block


def laplace(values, marks):
    centre = values[..., 1:-1, 1:-1]
    north = marks[:-2, 1:-1] * (values[..., :-2, 1:-1] - centre)
    south = marks[2:, 1:-1] * (values[..., 2:, 1:-1] - centre)
    west = marks[1:-1, :-2] * (values[..., 1:-1, :-2] - centre)
    east = marks[1:-1, 2:] * (values[..., 1:-1, 2:] - centre)
    return marks[1:-1, 1:-1] * (north + south + west + east)


def tridiagonal_kernel(
    decay_ref, inner_ref, rows_ref, edge_ref, mask_ref, base_ref, surf_ref, land_ref,
    out_ref, back_ref, ratio_ref, marks_ref,
):
    fields, levels = out_ref.shape[0], out_ref.shape[1]
    rows, cols = out_ref.shape[2], out_ref.shape[3]
    tall, wide = mask_ref.shape
    marks = mask_ref[...]
    marks_ref[0] = marks * pltpu.roll(marks, 1, 0)
    marks_ref[1] = marks * pltpu.roll(marks, tall - 1, 0)
    marks_ref[2] = marks * pltpu.roll(marks, 1, 1)
    marks_ref[3] = marks * pltpu.roll(marks, wide - 1, 1)
    marks_ref[4] = (marks_ref[0] + marks_ref[1]) + (marks_ref[2] + marks_ref[3])

    def laplace_ext(values, inner=False):
        shifted = [
            pltpu.roll(values, 1, 0),
            pltpu.roll(values, tall - 1, 0),
            pltpu.roll(values, 1, 1),
            pltpu.roll(values, wide - 1, 1),
        ]
        if inner:
            shifted = [part[:rows, :cols] for part in shifted]
            values = values[:rows, :cols]
            weight = [marks_ref[i, :rows, :cols] for i in range(5)]
        else:
            weight = [marks_ref[i] for i in range(5)]
        vertical = weight[0] * shifted[0] + weight[1] * shifted[1]
        across = weight[2] * shifted[2] + weight[3] * shifted[3]
        return (vertical + across) - weight[4] * values

    def smoothed(f, level):
        plane = f * levels + level
        values = jnp.concatenate([inner_ref[plane], rows_ref[plane]], axis=0)
        values = jnp.concatenate([values, edge_ref[plane]], axis=1)
        inner = laplace_ext(values)
        values = values - SMOOTHING * laplace_ext(inner)
        inner = laplace_ext(values)
        return values[:rows, :cols] - SMOOTHING * laplace_ext(inner, inner=True)

    gains = sorted(set(FIELD_MIX))
    groups = [[f for f in range(fields) if FIELD_MIX[f] == g] for g in gains]
    surf = surf_ref[...]
    zero = jnp.zeros_like(surf)

    def step(level, below_mix, above_mix, ratios, parts, sources):
        new_ratios, new_parts = [], list(parts)
        for gi, gain in enumerate(gains):
            below = gain * below_mix
            above = gain * above_mix
            pivot = ((1.0 + below) + above) - below * ratios[gi]
            scale = 1.0 / pivot
            if level is not None:
                ratio = above * scale
                ratio_ref[gi, level] = ratio
                new_ratios.append(ratio)
            for f in groups[gi]:
                value = (sources[f] + below * parts[f]) * scale
                out_ref[f, level if level is not None else levels - 1] = value
                new_parts[f] = value
        return tuple(new_ratios), tuple(new_parts)

    def forward(level, carry):
        below_mix, ratios, parts, sources = carry
        upcoming = tuple(smoothed(f, level + 1) for f in range(fields))
        mix = base_ref[level] + surf * decay_ref[level]
        ratios, parts = step(level, below_mix, mix, ratios, parts, sources)
        return (mix, ratios, parts, upcoming)

    first = tuple(smoothed(f, 0) for f in range(fields))
    carry = (zero, tuple(zero for _ in gains), tuple(zero for _ in range(fields)), first)
    last_mix, ratios, parts, sources = lax.fori_loop(0, levels - 1, forward, carry)
    step(None, last_mix, zero, ratios, parts, sources)

    def backward(i, later):
        level = levels - 2 - i
        result = []
        for gi in range(len(gains)):
            ratio = ratio_ref[gi, level]
            for f in groups[gi]:
                value = out_ref[f, level] + ratio * later[f]
                out_ref[f, level] = value
                result.append((f, value))
        result.sort(key=lambda item: item[0])
        return tuple(v for _, v in result)

    final = tuple(out_ref[f, levels - 1] for f in range(fields))
    lax.fori_loop(0, levels - 1, backward, final, unroll=2)
    land = land_ref[...]
    for f in range(fields):
        back_ref[f] = land * out_ref[f, 0]


def tridiagonal(pieces, mask, shape, mixing_base, surface, land):
    fields, levels = shape[0], shape[1]
    decay_table = np.array(
        [math.exp(-level / DEPTH_SCALE) for level in range(levels)], dtype=np.float32
    )
    vmem = pltpu.MemorySpace.VMEM
    return pl.pallas_call(
        tridiagonal_kernel,
        out_shape=(
            jax.ShapeDtypeStruct(shape, jnp.float32),
            jax.ShapeDtypeStruct((fields,) + shape[2:], jnp.float32),
        ),
        in_specs=[pl.BlockSpec(memory_space=pltpu.MemorySpace.SMEM)]
        + [pl.BlockSpec(memory_space=vmem)] * (len(pieces) + 4),
        out_specs=(pl.BlockSpec(memory_space=vmem), pl.BlockSpec(memory_space=vmem)),
        scratch_shapes=[
            pltpu.VMEM((len(set(FIELD_MIX)), levels) + shape[2:], jnp.float32),
            pltpu.VMEM((5,) + mask.shape, jnp.float32),
        ],
    )(jnp.asarray(decay_table), *pieces, mask, mixing_base, surface, land)


def split_parts(values):
    high = values.astype(jnp.bfloat16)
    low = (values - high.astype(jnp.float32)).astype(jnp.bfloat16)
    return high, low


def matmul_exact(parts, other, contract):
    numbers = (((1,), (contract,)), ((), ()))
    total = None
    for part in parts:
        product = lax.dot_general(part, other, numbers, preferred_element_type=jnp.float32)
        total = product if total is None else total + product
    return total


def gather_kernel(recv_ref, index_ref, weight_ref, *after_and_out):
    out_ref = after_and_out[-1]
    stacked, lanes = recv_ref.shape
    fields, rows, cols = out_ref.shape
    segments = stacked // fields
    items = index_ref.shape[0] // rows
    parts = split_parts(recv_ref[...])
    lane_iota = lax.broadcasted_iota(jnp.int32, (lanes, cols), 0)
    segment_iota = lax.broadcasted_iota(jnp.int32, (fields, segments, cols), 1)

    def row_step(y, carry):
        total = None
        for item in range(items):
            index = index_ref[pl.ds(item * rows + y, 1), :]
            onehot = (lane_iota == index % lanes).astype(jnp.bfloat16)
            chosen = matmul_exact(parts, onehot, 0).reshape(fields, segments, cols)
            hit = segment_iota == (index // lanes)[None]
            picked = jnp.sum(jnp.where(hit, chosen, 0.0), axis=1)
            term = weight_ref[pl.ds(item * rows + y, 1), :] * picked
            total = term if total is None else total + term
        out_ref[:, pl.ds(y, 1), :] = total[:, None, :]
        return carry

    lax.fori_loop(0, rows, row_step, 0, unroll=True)


def scatter_kernel(back_ref, index_ref, weight_ref, out_ref):
    fields, rows, cols = back_ref.shape
    stacked, lanes = out_ref.shape
    segments = stacked // fields
    items = index_ref.shape[0] // rows
    lane_iota = lax.broadcasted_iota(jnp.int32, (lanes, cols), 0)
    segment_iota = lax.broadcasted_iota(jnp.int32, (fields, segments, cols), 1)

    def row_step(y, total):
        back = back_ref[:, pl.ds(y, 1), :]
        for item in range(items):
            index = index_ref[pl.ds(item * rows + y, 1), :]
            onehot = (lane_iota == index % lanes).astype(jnp.bfloat16)
            weighted = weight_ref[pl.ds(item * rows + y, 1), :][None] * back
            hit = segment_iota == (index // lanes)[None]
            spread = jnp.where(hit, weighted, 0.0).reshape(stacked, cols)
            total = total + matmul_exact(split_parts(spread), onehot, 1)
        return total

    total = lax.fori_loop(
        0, rows, row_step, jnp.zeros((stacked, lanes), jnp.float32), unroll=True
    )
    pair = SLOTS
    owners = segments // pair
    for owner in range(owners):
        for f in range(fields):
            start = f * segments + owner * pair
            out_ref[pl.ds((owner * fields + f) * pair, pair), :] = total[start:start + pair, :]


def remap_call(kernel, out_shape, *operands, after=()):
    vmem = pltpu.MemorySpace.VMEM
    return pl.pallas_call(
        kernel,
        out_shape=jax.ShapeDtypeStruct(out_shape, jnp.float32),
        in_specs=[pl.BlockSpec(memory_space=vmem)] * len(operands)
        + [pl.BlockSpec(memory_space=pl.ANY)] * len(after),
        out_specs=pl.BlockSpec(memory_space=vmem),
    )(*operands, *after)


def sum_over(values, axis):
    count = lax.axis_size(axis)
    where = lax.axis_index(axis)
    copies = [values] + [
        lax.ppermute(values, axis, [(i, (i + shift) % count) for i in range(count)])
        for shift in range(1, count)
    ]
    stacked = jnp.stack(copies)
    ordered = [
        lax.dynamic_index_in_dim(stacked, (where - owner) % count, 0, keepdims=False)
        for owner in range(count)
    ]
    while len(ordered) > 1:
        paired = [ordered[i] + ordered[i + 1] for i in range(0, len(ordered) - 1, 2)]
        ordered = paired + ordered[len(ordered) - len(ordered) % 2:]
    return ordered[0]


def lat_edges(marks, width):
    lat_count = lax.axis_size("lat")
    where_lat = lax.axis_index("lat")
    rows = lax.broadcasted_iota(jnp.int32, marks.shape, 0)
    keep_top = jnp.logical_or(where_lat > 0, rows >= width)
    keep_bottom = jnp.logical_or(where_lat < lat_count - 1, rows < marks.shape[0] - width)
    return jnp.where(jnp.logical_and(keep_top, keep_bottom), marks, 0.0)


def single_rim(values):
    return with_halo(values, (("lat", 2), ("lon", 3)), 1)


def shards(
    adjoint_state,
    mixing_base,
    atm_flux,
    send_count,
    send_segment,
    cover_index,
    cover_weight,
    land_mask,
):
    lat_count = lax.axis_size("lat")
    owned = atm_flux.shape[1]
    counts = send_count[0]
    capacity = send_segment.shape[1] // lat_count
    starts = jnp.cumsum(counts) - counts
    column = jnp.arange(capacity, dtype=jnp.int32)
    places = jnp.minimum(starts[:, None] + column[None, :], send_segment.shape[1] - 1)
    chosen = send_segment[0][places]
    live_slot = column[None, :] < counts[:, None]
    outgoing = atm_flux[:, chosen, :]
    received = lax.all_to_all(outgoing, "lat", split_axis=1, concat_axis=1, tiled=True)
    items, rows, cols = cover_index.shape
    fields = received.shape[0]
    flat_recv = received.reshape(-1, received.shape[-1])
    index_rows = cover_index.reshape(items * rows, cols)
    weight_rows = cover_weight.reshape(items * rows, cols)
    land = land_mask.astype(jnp.float32)
    *pieces, mask = extended_planes(adjoint_state, land_mask, HALO)
    forcing = remap_call(
        gather_kernel, (fields, rows, cols), flat_recv, index_rows, weight_rows, after=tuple(pieces[1:])
    )
    surface = WIND_GAIN * (forcing[2] * forcing[2] + forcing[3] * forcing[3]) + jax.nn.softplus(
        forcing[1] - forcing[0]
    )
    state_adjoint, flux_back = tridiagonal(pieces, mask, adjoint_state.shape, mixing_base, surface, land)
    buffer = remap_call(scatter_kernel, flat_recv.shape, flux_back, index_rows, weight_rows)
    slots = received.shape[2]
    returned = lax.all_to_all(
        buffer.reshape(received.shape[1], fields, slots, -1), "lat", split_axis=0, concat_axis=0, tiled=True
    )
    owned_ids = lax.broadcasted_iota(jnp.int32, (owned,) + chosen.shape, 0)
    picks = jnp.logical_and(owned_ids == chosen[None], live_slot[None]).astype(jnp.float32)
    owner_sum = jnp.einsum(
        "sdc,dfck->fsk", picks, returned, precision=lax.Precision.HIGHEST
    )
    flux_adjoint = sum_over(owner_sum, "lon")
    return (state_adjoint, flux_adjoint)


def solution(mesh):
    in_specs = (
        P(None, None, "lat", "lon"),
        P(None, "lat", "lon"),
        P(None, "lat", None),
        P("lat", "lon"),
        P("lat", "lon"),
        P(None, "lat", "lon"),
        P(None, "lat", "lon"),
        P("lat", "lon"),
    )
    out_specs = (P(None, None, "lat", "lon"), P(None, "lat", None))
    return jax.shard_map(shards, mesh=mesh, in_specs=in_specs, out_specs=out_specs, check_vma=False)
```
